32 devices in a mesh: dp: 4 (over x, core), fsdp: 8 (over z, y).
Axes of the slice: x: 2, y: 2, z: 4, core: 2. Of those that a mesh axis runs over, the one named last changes fastest.
Arguments:
- tokens: bfloat16 [8, 1024, 768], P('dp', 'fsdp'), may hold values from -6 to 6
- seg_ids: int32 [8, 1024], P('dp'), may hold values from 0 to 7, never falling along the last dimension, each value on 1 to 768 neighbouring positions
- token_types: int32 [8, 1024], P('dp'), may hold values from 0 to 1
- attn_in: bfloat16 [768, 2304], P(('dp', 'fsdp')), may hold values from -0.21875 to 0.21875
- attn_out: bfloat16 [768, 768], P(('dp', 'fsdp')), may hold values from -0.875 to 0.875
- pos_kernel: bfloat16 [768, 768], P(('dp', 'fsdp')), may hold values from -0.375 to 0.375
- ffn_in: bfloat16 [768, 3072], P(('dp', 'fsdp')), may hold values from -0.21875 to 0.21875
- ffn_out: bfloat16 [3072, 768], P(('dp', 'fsdp')), may hold values from -0.109375 to 0.109375
- head_vectors: bfloat16 [5, 768], P(None, ('dp', 'fsdp')), may hold values from -3 to 3
- norm_gains: bfloat16 [2, 768], P(None, ('dp', 'fsdp')), may hold values from 0.5 to 1.5
- norm_shifts: bfloat16 [2, 768], P(None, ('dp', 'fsdp')), may hold values from -3 to 3
- out_bias: bfloat16 [2, 768], P(None, ('dp', 'fsdp')), may hold values from -3 to 3
- ffn_bias: bfloat16 [3072], P(('dp', 'fsdp')), may hold values from -3 to 3
- cotangent: bfloat16 [8, 1024, 768], P('dp', 'fsdp'), may hold values from -6 to 6
Outputs:
- output: bfloat16 [8, 1024, 768], P('dp', 'fsdp')
- input_grad: float32 [8, 1024, 768], P('dp', 'fsdp')
- grad_attn_in: float32 [768, 2304], P(('dp', 'fsdp'))
- grad_attn_out: float32 [768, 768], P(('dp', 'fsdp'))
- grad_pos_kernel: float32 [768, 768], P(('dp', 'fsdp'))
- grad_ffn_in: float32 [768, 3072], P(('dp', 'fsdp'))
- grad_ffn_out: float32 [3072, 768], P(('dp', 'fsdp'))
- grad_head_vectors: float32 [5, 768], P(None, ('dp', 'fsdp'))
- grad_norm_gains: float32 [2, 768], P(None, ('dp', 'fsdp'))
- grad_norm_shifts: float32 [2, 768], P(None, ('dp', 'fsdp'))
- grad_out_bias: float32 [2, 768], P(None, ('dp', 'fsdp'))
- grad_ffn_bias: float32 [3072], P(('dp', 'fsdp'))
The draws below stay inside these ranges and needn't reach their ends.
Inputs may be any that keep to these rules, and one draw needn't show every extreme that they name: `seg_ids`: in each sequence the document numbers never fall; every document has 1 to 768 positions and one has exactly 768; a position attends only to positions of its own document.
All inputs are finite; a program needn't handle non-finite values.
Results may differ from the reference program's by a relative error of at most 0.017.
Values may be sent and summed in bfloat16 or wider, within the bound.
A program may use at most 192 MiB of HBM per device.

```python
import math
import jax
import jax.numpy as jnp
import numpy as np
from jax import lax

D = 768
H = 12
DH = 64
FF = 3072
SEQ = 1024
DOCS = 8
HD = 768
DOC_MOST = 768
NSEQ = 8


def with_ends(values, stream_key, smallest, top_value):
    longest = values.shape.index(max(values.shape))
    spots = []
    for shift in (0, 1):
        where = [jax.random.randint(jax.random.fold_in(stream_key, axis), (), 0, length) for axis, length in enumerate(values.shape)]
        where[longest] = (where[longest] + shift) % values.shape[longest]
        spots.append(tuple(where))
    return values.at[spots[0]].set(smallest).at[spots[1]].set(top_value)


def shard_levels(stream_key, extent, cuts, low, top_value):
    def one(dim, parts):
        draws = jax.random.uniform(jax.random.fold_in(jax.random.fold_in(stream_key, 6), dim), (parts,), jnp.float32, low / len(cuts), top_value / len(cuts))
        return jnp.repeat(jnp.exp(draws), extent[dim] // parts).reshape((-1,) + (1,) * (len(extent) - dim - 1))

    factor_of = one(*cuts[0])
    for cut in cuts[1:]:
        factor_of = factor_of * one(*cut)
    return factor_of


def split_up(amount, total, most, skew):
    portions = [(1 << 20) // math.isqrt(standing ** skew) + 1 for standing in range(2, amount + 1)]
    spare, holding = total - most - (amount - 1), [1] * (amount - 1)
    while spare > 0:
        free = [i for i in range(amount - 1) if holding[i] < most]
        pool, budget = sum([portions[i] for i in free]), spare
        for i in free:
            more = min(most - holding[i], max(1, budget * portions[i] // pool), spare)
            holding[i] = holding[i] + more
            spare = spare - more
    return np.array([most] + holding)


def ragged(own_key, number_of, total, bound, slope):
    if number_of == 2:
        one = jax.random.randint(own_key, (), max(1, total - bound), min(bound, total - 1) + 1)
        return jnp.stack([one, total - one])
    sizes = jnp.asarray(split_up(number_of, total, bound, slope), jnp.int32)
    couples = (number_of - 1) // 2
    giver, taker = sizes[1:1 + 2 * couples:2], sizes[2:2 + 2 * couples:2]
    margin = jnp.minimum(giver - 1, bound - taker)
    moved = jax.random.randint(jax.random.fold_in(own_key, 1), (couples,), 0, 1 << 20) % (margin + 1)
    sizes = sizes.at[1:1 + 2 * couples:2].set(giver - moved).at[2:2 + 2 * couples:2].set(taker + moved)
    return sizes[jax.random.permutation(jax.random.fold_in(own_key, 2), number_of)]


def bell_draw(stream_key, shape, scale, bound, shards=(), kind=jnp.bfloat16):
    level = shard_levels(stream_key, shape, shards, -0.22, 0.18) if shards else 1.0
    values = jax.random.normal(stream_key, shape, jnp.float32) * scale * level
    return jnp.minimum(jnp.maximum(values, -bound), bound).astype(kind)


def setup_inputs(seed: int = 0) -> dict:
    streams_of = jax.random.split(jax.random.key(seed), 15)
    return {
        "tokens": bell_draw(streams_of[0], (NSEQ, SEQ, D), 1.0, 6.0, ((0, 4), (1, 8))),
        "seg_ids": jax.vmap(lambda own: jnp.searchsorted(jnp.cumsum(ragged(own, DOCS, SEQ, DOC_MOST, 2)), jnp.arange(SEQ), side="right"))(jax.random.split(streams_of[1], NSEQ)).reshape((NSEQ, SEQ)).astype(jnp.int32),
        "token_types": with_ends(jax.random.randint(streams_of[2], (NSEQ, SEQ), 0, 2), jax.random.fold_in(streams_of[2], 1), 0, 1).astype(jnp.int32),
        "attn_in": bell_draw(streams_of[3], (D, 3 * HD), D ** -0.5, 0.21875, ((0, 32),)),
        "attn_out": bell_draw(streams_of[4], (HD, D), (HD // 16) ** -0.5, 0.875, ((0, 32),)),
        "pos_kernel": bell_draw(streams_of[5], (D, HD), (4 * DH) ** -0.5, 0.375, ((0, 32),)),
        "ffn_in": bell_draw(streams_of[6], (D, FF), D ** -0.5, 0.21875, ((0, 32),)),
        "ffn_out": bell_draw(streams_of[7], (FF, D), FF ** -0.5, 0.109375, ((0, 32),)),
        "head_vectors": bell_draw(streams_of[8], (5, HD), 0.5, 3.0, ((1, 32),)),
        "norm_gains": jnp.clip(1.0 + 0.1 * jax.random.normal(streams_of[9], (2, D), jnp.float32), 0.5, 1.5).astype(jnp.bfloat16),
        "norm_shifts": bell_draw(streams_of[10], (2, D), 0.5, 3.0, ((1, 32),)),
        "out_bias": bell_draw(streams_of[11], (2, D), 0.5, 3.0, ((1, 32),)),
        "ffn_bias": bell_draw(streams_of[12], (FF,), 0.5, 3.0, ((0, 32),)),
        "cotangent": bell_draw(streams_of[13], (NSEQ, SEQ, D), 1.0, 6.0, ((0, 4), (1, 8))),
    }


@jax.custom_vjp
def low(v):
    return lax.optimization_barrier(v.astype(jnp.bfloat16)).astype(jnp.float32)

@jax.custom_vjp
def low_back(v):
    return v

def low_keep(v):
    return (low(v), None)

def low_pass(kept, grad):
    return (grad,)

def back_keep(v):
    return (v, None)

def back_low(kept, grad):
    return (low(grad),)
low.defvjp(low_keep, low_pass)
low_back.defvjp(back_keep, back_low)
EPSILON = 1e-06
HIGHEST_PREC = lax.Precision.HIGHEST

def gelu_tanh(values):
    return 0.5 * values * (1.0 + jnp.tanh(0.7978845608028654 * (values + 0.044715 * values * values * values)))

def angle_tables(positions, width):
    half_width = width // 2
    freq_index = jnp.arange(half_width, dtype=jnp.float32)
    inverse = jnp.power(10000.0, -freq_index / half_width)
    angles = positions[:, None] * inverse[None, :]
    return (jnp.sin(angles), jnp.cos(angles))

def layer_norm(values, gain, shift):
    center = values - lax.optimization_barrier(jnp.mean(values, axis=-1, keepdims=True))
    inv_std = lax.rsqrt(lax.optimization_barrier(jnp.mean(center * center, axis=-1, keepdims=True)) + EPSILON)
    return center * inv_std * gain + shift

def seq_forward(xs, attn_in, attn_out, pos_kernel, ffn_in, ffn_out, head_vectors, norm_gains, norm_shifts, out_bias, ffn_bias, seg_row, type_row):
    length = xs.shape[0]
    query = low_back(jnp.dot(xs, attn_in[:, :HD], precision=HIGHEST_PREC))
    keys = low(low_back(jnp.dot(xs, attn_in[:, HD:2 * HD], precision=HIGHEST_PREC))).reshape(length, H, DH)
    values = low(low_back(jnp.dot(xs, attn_in[:, 2 * HD:], precision=HIGHEST_PREC))).reshape(length, H, DH)
    q_content = low(query + head_vectors[0]).reshape(length, H, DH)
    q_pos = low(query + head_vectors[1]).reshape(length, H, DH)
    q_type = (query + head_vectors[2]).reshape(length, H, DH)
    type_table = head_vectors[3:5].reshape(2, H, DH)
    type_terms = jnp.einsum('lhe,the->lht', q_type, type_table, precision=HIGHEST_PREC)
    proj_pos = low_back(jnp.einsum('lhe,che->lhc', q_pos, pos_kernel.reshape(D, H, DH), precision=HIGHEST_PREC))
    positions = jnp.arange(length, dtype=jnp.float32)
    sines, cosines = angle_tables(positions, D)
    half_width = D // 2
    pos_sin = proj_pos[..., :half_width]
    pos_cos = proj_pos[..., half_width:]
    sin_q = sines[:, None, :]
    cos_q = cosines[:, None, :]
    q_rel = low(jnp.concatenate([pos_sin * sin_q + pos_cos * cos_q, pos_cos * sin_q - pos_sin * cos_q], axis=-1))
    k_rel = low(jnp.concatenate([cosines, sines], axis=-1))
    scale_factor = DH ** (-0.5)

    def block(pieces):
        qc_block, qr_block, tt_block, seg_block, type_block = pieces
        content = jnp.einsum('bhe,jhe->bhj', qc_block, keys, precision=HIGHEST_PREC)
        position = jnp.einsum('bhc,jc->bhj', qr_block, k_rel, precision=HIGHEST_PREC)
        same_type = (type_block[:, None] == type_row[None, :])[:, None, :]
        typed = jnp.where(same_type, tt_block[:, :, 1:2], tt_block[:, :, 0:1])
        scores = low_back(scale_factor * (content + position + typed))
        allowed = (seg_block[:, None] == seg_row[None, :])[:, None, :]
        masked = jnp.where(allowed, scores, -1e+30)
        top = lax.optimization_barrier(jnp.max(masked, axis=-1, keepdims=True))
        expo = jnp.where(allowed, jnp.exp(masked - top), 0.0)
        probs = low(expo / lax.optimization_barrier(jnp.sum(expo, axis=-1, keepdims=True)))
        return jnp.einsum('bhj,jhe->bhe', probs, values, precision=HIGHEST_PREC)
    block_rows = min(512, length)
    block_count = length // block_rows

    def split(array):
        return array.reshape((block_count, block_rows) + array.shape[1:])
    attn_blocks = lax.map(jax.checkpoint(block), (split(q_content), split(q_rel), split(type_terms), split(seg_row), split(type_row)))
    attn = low(low_back(attn_blocks.reshape(length, HD)))
    branch = low_back(jnp.dot(attn, attn_out, precision=HIGHEST_PREC) + out_bias[0])
    first = layer_norm(xs + branch, norm_gains[0], norm_shifts[0])
    pre_act = low_back(jnp.dot(low(first), ffn_in, precision=HIGHEST_PREC) + ffn_bias)
    hidden = low(gelu_tanh(pre_act))
    second = low_back(jnp.dot(hidden, ffn_out, precision=HIGHEST_PREC) + out_bias[1])
    return layer_norm(first + second, norm_gains[1], norm_shifts[1])

def reference(tokens, seg_ids, token_types, attn_in, attn_out, pos_kernel, ffn_in, ffn_out, head_vectors, norm_gains, norm_shifts, out_bias, ffn_bias, cotangent):
    params = tuple((p.astype(jnp.float32) for p in (attn_in, attn_out, pos_kernel, ffn_in, ffn_out, head_vectors, norm_gains, norm_shifts, out_bias, ffn_bias)))

    def one_sequence(carry, inputs):
        x_seq, cot_seq, seg_row, type_row = inputs

        def forward(x_value, *weights):
            return seq_forward(x_value, *weights, seg_row, type_row)
        result, pull = jax.vjp(forward, x_seq.astype(jnp.float32), *params)
        grads = pull(cot_seq.astype(jnp.float32))
        carry = tuple((c + g for c, g in zip(carry, grads[1:])))
        return (carry, (result.astype(jnp.bfloat16), grads[0]))
    init = tuple((jnp.zeros(p.shape, jnp.float32) for p in params))
    totals, (results, input_grads) = lax.scan(one_sequence, init, (tokens, cotangent, seg_ids, token_types))
    return (results, input_grads, totals[0], totals[1], totals[2], totals[3], totals[4], totals[5], totals[6], totals[7], totals[8], totals[9])
```

```python
import functools

import jax
import jax.numpy as jnp
import numpy as np
from jax import lax
from jax.experimental import pallas as pl
from jax.experimental.pallas import tpu as pltpu
from jax.sharding import PartitionSpec as P

D = 768
H = 12
DH = 64
FF = 3072
HD = 768


EPSILON = 1e-06
HIGHEST_PREC = lax.Precision.HIGHEST


def gelu_tanh(values):
    return (
        0.5
        * values
        * (1.0 + jnp.tanh(0.7978845608028654 * (values + 0.044715 * values * values * values)))
    )


def angle_tables(positions, width):
    half_width = width // 2
    freq_index = jnp.arange(half_width, dtype=jnp.float32)
    inverse = jnp.power(10000.0, -freq_index / half_width)
    angles = positions[:, None] * inverse[None, :]
    return (jnp.sin(angles), jnp.cos(angles))


def layer_norm(values, gain, shift):
    center = values - jnp.mean(values, axis=-1, keepdims=True)
    inv_std = lax.rsqrt(jnp.mean(center * center, axis=-1, keepdims=True) + EPSILON)
    normed = center * inv_std
    return (normed * gain + shift, normed, inv_std)


def norm_back(grad_out, normed, inv_std, gain):
    grad_norm = grad_out * gain
    return inv_std * (
        grad_norm
        - jnp.mean(grad_norm, axis=-1, keepdims=True)
        - normed * jnp.mean(grad_norm * normed, axis=-1, keepdims=True)
    )


def fetch_forward(shards):
    return (
        lax.all_gather(shards[0], ("dp", "fsdp"), axis=0, tiled=True),
        lax.all_gather(shards[1], ("dp", "fsdp"), axis=0, tiled=True),
        lax.all_gather(shards[2], ("dp", "fsdp"), axis=0, tiled=True),
        lax.all_gather(shards[3], ("dp", "fsdp"), axis=0, tiled=True),
        lax.all_gather(shards[4], ("dp", "fsdp"), axis=0, tiled=True),
        lax.all_gather(shards[5], ("dp", "fsdp"), axis=1, tiled=True),
        lax.all_gather(shards[6], ("dp", "fsdp"), axis=1, tiled=True),
        lax.all_gather(shards[7], ("dp", "fsdp"), axis=1, tiled=True),
        lax.all_gather(shards[8], ("dp", "fsdp"), axis=1, tiled=True),
        lax.all_gather(shards[9], ("dp", "fsdp"), axis=0, tiled=True),
    )


def fetch_backward(shards):
    return (
        lax.all_gather(shards[0], ("dp", "fsdp"), axis=0, tiled=True),
        lax.all_gather(shards[1], ("dp", "fsdp"), axis=0, tiled=True),
        lax.all_gather(shards[2], ("dp", "fsdp"), axis=0, tiled=True),
        lax.all_gather(shards[3], ("dp", "fsdp"), axis=0, tiled=True),
        lax.all_gather(shards[4], ("dp", "fsdp"), axis=0, tiled=True),
        lax.all_gather(shards[5], ("dp", "fsdp"), axis=1, tiled=True),
        lax.all_gather(shards[6], ("dp", "fsdp"), axis=1, tiled=True),
        lax.all_gather(shards[7], ("dp", "fsdp"), axis=1, tiled=True),
        lax.all_gather(shards[8], ("dp", "fsdp"), axis=1, tiled=True),
        lax.all_gather(shards[9], ("dp", "fsdp"), axis=0, tiled=True),
    )


def score_block(q_content, q_rel, type_terms, keys3, k_rel, same_type):
    content = jnp.einsum("rhe,jhe->rhj", q_content, keys3, preferred_element_type=jnp.float32)
    position = jnp.einsum("rhc,jc->rhj", q_rel, k_rel, preferred_element_type=jnp.float32)
    typed = jnp.where(same_type, type_terms[:, :, 1:2], type_terms[:, :, 0:1])
    return DH ** (-0.5) * (content + position + typed)


def relative_queries(q_pos, w_pos, positions):
    proj_pos = jnp.einsum(
        "rhe,che->rhc", q_pos, w_pos.reshape(D, H, DH), preferred_element_type=jnp.float32
    )
    sines, cosines = angle_tables(positions, D)
    sin_q = sines[:, None, :]
    cos_q = cosines[:, None, :]
    half_width = D // 2
    pos_sin = proj_pos[..., :half_width]
    pos_cos = proj_pos[..., half_width:]
    q_rel = jnp.concatenate(
        [pos_sin * sin_q + pos_cos * cos_q, pos_cos * sin_q - pos_sin * cos_q], axis=-1
    ).astype(jnp.bfloat16)
    return (q_rel, sin_q, cos_q)


def forward_micro(weights, x_rows, seg_row, type_row, start, k_rel):
    w_in, w_out, w_pos, w_up, w_down, head_vec, gains, shifts, biases, up_bias = weights
    row_count = x_rows.shape[0]
    head_f = head_vec.astype(jnp.float32)
    gains_f = gains.astype(jnp.float32)
    shifts_f = shifts.astype(jnp.float32)
    biases_f = biases.astype(jnp.float32)
    proj = jnp.dot(x_rows, w_in, preferred_element_type=jnp.float32)
    query = proj[:, :HD]
    key_local = proj[:, HD : 2 * HD].astype(jnp.bfloat16)
    value_local = proj[:, 2 * HD :].astype(jnp.bfloat16)
    keys, values = (
        lax.all_gather(key_local, "fsdp", axis=0, tiled=True),
        lax.all_gather(value_local, "fsdp", axis=0, tiled=True),
    )
    keys3 = keys.reshape(keys.shape[0], H, DH)
    values3 = values.reshape(values.shape[0], H, DH)
    q_content = (query + head_f[0]).astype(jnp.bfloat16).reshape(row_count, H, DH)
    q_pos = (query + head_f[1]).astype(jnp.bfloat16).reshape(row_count, H, DH)
    q_type = (query + head_f[2]).reshape(row_count, H, DH)
    type_table = head_f[3:5].reshape(2, H, DH)
    type_terms = jnp.einsum("rhe,the->rht", q_type, type_table, precision=HIGHEST_PREC)
    positions = (start + jnp.arange(row_count, dtype=jnp.int32)).astype(jnp.float32)
    q_rel, sin_q, cos_q = relative_queries(q_pos, w_pos, positions)
    query_seg = lax.dynamic_slice_in_dim(seg_row, start, row_count)
    query_kind = lax.dynamic_slice_in_dim(type_row, start, row_count)
    allowed = (query_seg[:, None] == seg_row[None, :])[:, None, :]
    same_type = (query_kind[:, None] == type_row[None, :])[:, None, :]
    scores = score_block(q_content, q_rel, type_terms, keys3, k_rel, same_type)
    masked = jnp.where(allowed, scores, -1e30)
    top = jnp.max(masked, axis=-1, keepdims=True)
    expo = jnp.where(allowed, jnp.exp(masked - top), 0.0)
    total = jnp.sum(expo, axis=-1, keepdims=True)
    probs_b = (expo / total).astype(jnp.bfloat16)
    log_total = top + jnp.log(total)
    attn = (
        jnp.einsum("rhj,jhe->rhe", probs_b, values3, preferred_element_type=jnp.float32)
        .astype(jnp.bfloat16)
        .reshape(row_count, HD)
    )
    branch = jnp.dot(attn, w_out, preferred_element_type=jnp.float32) + biases_f[0]
    first, normed_one, inv_one = layer_norm(
        x_rows.astype(jnp.float32) + branch, gains_f[0], shifts_f[0]
    )
    first_b = first.astype(jnp.bfloat16)
    pre_act = jnp.dot(first_b, w_up, preferred_element_type=jnp.float32) + up_bias.astype(
        jnp.float32
    )
    hidden = gelu_tanh(pre_act).astype(jnp.bfloat16)
    second = jnp.dot(hidden, w_down, preferred_element_type=jnp.float32) + biases_f[1]
    result, normed_two, inv_two = layer_norm(first + second, gains_f[1], shifts_f[1])
    kept = (
        x_rows,
        q_content,
        q_pos,
        q_rel,
        q_type,
        type_terms,
        sin_q,
        cos_q,
        keys3,
        values3,
        allowed,
        same_type,
        log_total,
        attn,
        normed_one,
        inv_one,
        first_b,
        pre_act,
        hidden,
        normed_two,
        inv_two,
    )
    return (result.astype(jnp.bfloat16), kept)


def backward_micro(weights, kept, grad_rows, k_rel, totals):
    w_in, w_out, w_pos, w_up, w_down, head_vec, gains, shifts, biases, up_bias = weights
    (
        x_rows,
        q_content,
        q_pos,
        q_rel,
        q_type,
        type_terms,
        sin_q,
        cos_q,
        keys3,
        values3,
        allowed,
        same_type,
        log_total,
        attn,
        normed_one,
        inv_one,
        first_b,
        pre_act,
        hidden,
        normed_two,
        inv_two,
    ) = kept
    g_in, g_out, g_pos, g_up, g_down, g_head, g_gains, g_shifts, g_bias, g_upbias = totals
    row_count = x_rows.shape[0]
    head_f = head_vec.astype(jnp.float32)
    gains_f = gains.astype(jnp.float32)
    grad_two = grad_rows.astype(jnp.float32)
    gain_two = jnp.sum(grad_two * normed_two, axis=0)
    shift_two = jnp.sum(grad_two, axis=0)
    grad_h2 = norm_back(grad_two, normed_two, inv_two, gains_f[1])
    grad_second = grad_h2.astype(jnp.bfloat16)
    bias_two = jnp.sum(grad_second.astype(jnp.float32), axis=0)
    g_down = g_down + jnp.einsum(
        "rf,rd->fd", hidden, grad_second, preferred_element_type=jnp.float32
    )
    grad_hidden = jnp.einsum("rd,fd->rf", grad_second, w_down, preferred_element_type=jnp.float32)
    act_pull = jax.vjp(gelu_tanh, pre_act)[1]
    grad_pre = act_pull(grad_hidden)[0].astype(jnp.bfloat16)
    g_upbias = g_upbias + jnp.sum(grad_pre.astype(jnp.float32), axis=0)
    g_up = g_up + jnp.einsum("rd,rf->df", first_b, grad_pre, preferred_element_type=jnp.float32)
    grad_first = grad_h2 + jnp.einsum(
        "rf,df->rd", grad_pre, w_up, preferred_element_type=jnp.float32
    )
    gain_one = jnp.sum(grad_first * normed_one, axis=0)
    shift_one = jnp.sum(grad_first, axis=0)
    grad_h1 = norm_back(grad_first, normed_one, inv_one, gains_f[0])
    grad_branch = grad_h1.astype(jnp.bfloat16)
    bias_one = jnp.sum(grad_branch.astype(jnp.float32), axis=0)
    g_out = g_out + jnp.einsum("rk,rd->kd", attn, grad_branch, preferred_element_type=jnp.float32)
    grad_attn = (
        jnp.einsum("rd,kd->rk", grad_branch, w_out, preferred_element_type=jnp.float32)
        .astype(jnp.bfloat16)
        .reshape(row_count, H, DH)
    )
    scores = score_block(q_content, q_rel, type_terms, keys3, k_rel, same_type)
    probs = jnp.where(allowed, jnp.exp(scores - log_total), 0.0)
    grad_probs = jnp.einsum("rhe,jhe->rhj", grad_attn, values3, preferred_element_type=jnp.float32)
    delta = jnp.sum(probs * grad_probs, axis=-1, keepdims=True)
    grad_scores = (probs * (grad_probs - delta)).astype(jnp.bfloat16) * DH ** (-0.5)
    grad_content = jnp.einsum(
        "rhj,jhe->rhe", grad_scores, keys3, preferred_element_type=jnp.float32
    )
    grad_rel = jnp.einsum("rhj,jc->rhc", grad_scores, k_rel, preferred_element_type=jnp.float32)
    probs_b = probs.astype(jnp.bfloat16)
    value_part = jnp.einsum("rhj,rhe->jhe", probs_b, grad_attn, preferred_element_type=jnp.float32)
    key_part = jnp.einsum(
        "rhj,rhe->jhe", grad_scores, q_content, preferred_element_type=jnp.float32
    )
    key_full, value_full = (
        lax.psum_scatter(
            key_part.reshape(key_part.shape[0], HD).astype(jnp.bfloat16),
            "fsdp",
            scatter_dimension=0,
            tiled=True,
        ).astype(jnp.float32),
        lax.psum_scatter(
            value_part.reshape(value_part.shape[0], HD).astype(jnp.bfloat16),
            "fsdp",
            scatter_dimension=0,
            tiled=True,
        ).astype(jnp.float32),
    )
    scores_f = grad_scores.astype(jnp.float32)
    same_f = same_type.astype(jnp.float32)
    grad_same = jnp.sum(scores_f * same_f, axis=-1)
    grad_diff = jnp.sum(scores_f * (1.0 - same_f), axis=-1)
    grad_terms = jnp.stack([grad_diff, grad_same], axis=-1)
    type_table = head_f[3:5].reshape(2, H, DH)
    grad_qtype = jnp.einsum("rht,the->rhe", grad_terms, type_table, precision=HIGHEST_PREC)
    grad_table = jnp.einsum("rht,rhe->the", grad_terms, q_type, precision=HIGHEST_PREC)
    half_width = D // 2
    rel_first = grad_rel[..., :half_width]
    rel_second = grad_rel[..., half_width:]
    grad_proj = jnp.concatenate(
        [rel_first * sin_q - rel_second * cos_q, rel_first * cos_q + rel_second * sin_q], axis=-1
    ).astype(jnp.bfloat16)
    grad_qpos = jnp.einsum(
        "rhc,che->rhe", grad_proj, w_pos.reshape(D, H, DH), preferred_element_type=jnp.float32
    )
    g_pos = g_pos + jnp.einsum(
        "rhc,rhe->che", grad_proj, q_pos, preferred_element_type=jnp.float32
    ).reshape(D, HD)
    head_terms = jnp.stack(
        [
            jnp.sum(grad_content.reshape(row_count, HD), axis=0),
            jnp.sum(grad_qpos.reshape(row_count, HD), axis=0),
            jnp.sum(grad_qtype.reshape(row_count, HD), axis=0),
            grad_table[0].reshape(HD),
            grad_table[1].reshape(HD),
        ]
    )
    g_head = g_head + head_terms
    grad_query = (grad_content + grad_qpos + grad_qtype).reshape(row_count, HD).astype(jnp.bfloat16)
    grad_proj_in = jnp.concatenate(
        [grad_query, key_full.astype(jnp.bfloat16), value_full.astype(jnp.bfloat16)], axis=1
    )
    g_in = g_in + jnp.einsum("rd,rk->dk", x_rows, grad_proj_in, preferred_element_type=jnp.float32)
    grad_x = grad_h1 + jnp.einsum(
        "rk,dk->rd", grad_proj_in, w_in, preferred_element_type=jnp.float32
    )
    g_gains = g_gains + jnp.stack([gain_one, gain_two])
    g_shifts = g_shifts + jnp.stack([shift_one, shift_two])
    g_bias = g_bias + jnp.stack([bias_one, bias_two])
    return (grad_x, (g_in, g_out, g_pos, g_up, g_down, g_head, g_gains, g_shifts, g_bias, g_upbias))


def per_device(
    tokens,
    seg_ids,
    token_types,
    attn_in,
    attn_out,
    pos_kernel,
    ffn_in,
    ffn_out,
    head_vectors,
    norm_gains,
    norm_shifts,
    out_bias,
    ffn_bias,
    cotangent,
):
    shards = (
        attn_in,
        attn_out,
        pos_kernel,
        ffn_in,
        ffn_out,
        head_vectors,
        norm_gains,
        norm_shifts,
        out_bias,
        ffn_bias,
    )
    micro_count = tokens.shape[0]
    row_count = tokens.shape[1]
    start = lax.axis_index("fsdp") * row_count
    all_positions = jnp.arange(seg_ids.shape[1], dtype=jnp.float32)
    key_sin, key_cos = angle_tables(all_positions, D)
    k_rel = jnp.concatenate([key_cos, key_sin], axis=-1).astype(jnp.bfloat16)
    totals = (
        jnp.zeros((D, 3 * HD), jnp.float32),
        jnp.zeros((HD, D), jnp.float32),
        jnp.zeros((D, HD), jnp.float32),
        jnp.zeros((D, FF), jnp.float32),
        jnp.zeros((FF, D), jnp.float32),
        jnp.zeros((5, HD), jnp.float32),
        jnp.zeros((2, D), jnp.float32),
        jnp.zeros((2, D), jnp.float32),
        jnp.zeros((2, D), jnp.float32),
        jnp.zeros((FF,), jnp.float32),
    )
    results = []
    input_grads = []
    for micro_step in range(micro_count):
        forward_weights = fetch_forward(shards)
        result, kept = forward_micro(
            forward_weights,
            tokens[micro_step],
            seg_ids[micro_step],
            token_types[micro_step],
            start,
            k_rel,
        )
        backward_weights = fetch_backward(shards)
        grad_x, totals = backward_micro(
            backward_weights, kept, cotangent[micro_step], k_rel, totals
        )
        results.append(result)
        input_grads.append(grad_x)
    final = (
        lax.psum_scatter(totals[0], ("dp", "fsdp"), scatter_dimension=0, tiled=True),
        lax.psum_scatter(totals[1], ("dp", "fsdp"), scatter_dimension=0, tiled=True),
        lax.psum_scatter(totals[2], ("dp", "fsdp"), scatter_dimension=0, tiled=True),
        lax.psum_scatter(totals[3], ("dp", "fsdp"), scatter_dimension=0, tiled=True),
        lax.psum_scatter(totals[4], ("dp", "fsdp"), scatter_dimension=0, tiled=True),
        lax.psum_scatter(totals[5], ("dp", "fsdp"), scatter_dimension=1, tiled=True),
        lax.psum_scatter(totals[6], ("dp", "fsdp"), scatter_dimension=1, tiled=True),
        lax.psum_scatter(totals[7], ("dp", "fsdp"), scatter_dimension=1, tiled=True),
        lax.psum_scatter(totals[8], ("dp", "fsdp"), scatter_dimension=1, tiled=True),
        lax.psum_scatter(totals[9], ("dp", "fsdp"), scatter_dimension=0, tiled=True),
    )
    return (
        jnp.stack(results),
        jnp.stack(input_grads),
        final[0],
        final[1],
        final[2],
        final[3],
        final[4],
        final[5],
        final[6],
        final[7],
        final[8],
        final[9],
    )


MESH_ID = pl.DeviceIdType.MESH
Z_OFFSETS = (0, -1, 1, -2, 2, -3, 3)
ANY_SPEC = pl.BlockSpec(memory_space=pl.ANY)
VMEM_SPEC = pl.BlockSpec(memory_space=pltpu.VMEM)


def place():
    dp = lax.axis_index("dp")
    fs = lax.axis_index("fsdp")
    return (dp // 2, dp % 2, fs // 2, fs % 2)


def device(x, c, z, y):
    return (x * 2 + c, z * 2 + y)


def guarded(cond, action):
    if cond is None:
        action()
    else:
        pl.when(cond)(action)


def greet(peers):
    barrier = pltpu.get_barrier_semaphore()
    for cond, peer in peers:
        guarded(
            cond,
            lambda peer=peer: pl.semaphore_signal(
                barrier, inc=1, device_id=peer, device_id_type=MESH_ID
            ),
        )
    count = 0
    for cond, _ in peers:
        count = count + (1 if cond is None else cond.astype(jnp.int32))
    pl.semaphore_wait(barrier, count)


def remote(src, dst, send, recv, to):
    return pltpu.make_async_remote_copy(
        src_ref=src, dst_ref=dst, send_sem=send, recv_sem=recv, device_id=to, device_id_type=MESH_ID
    )


def half_members(kinds, half):
    if half == 0:
        return range(len(kinds))
    return [a for a, kind in enumerate(kinds) if kind in ("split", half)]


def swap_peers():
    x, c, z, y = place()
    peers = []
    for m in range(2):
        away = jnp.logical_or(z // 2 != c, z % 2 != m)
        peers.append((away, device(x, z // 2, 2 * c + m, y)))
    return peers


def swap_copies(src, dst, send, recv, local):
    x, c, z, y = place()

    def both(m):
        peer = device(x, z // 2, 2 * c + m, y)
        out = remote(src.at[m], dst.at[z % 2], send.at[m], recv.at[z % 2], peer)
        into = remote(src.at[m], dst.at[m], send.at[m], recv.at[m], peer)
        here = pltpu.make_async_copy(src.at[m], dst.at[m], local.at[m])
        away = jnp.logical_or(z // 2 != c, z % 2 != m)
        return (out, into, here, away)

    def start():
        for m in range(2):
            out, _, here, away = both(m)
            pl.when(away)(out.start)
            pl.when(jnp.logical_not(away))(here.start)

    def wait():
        for m in range(2):
            out, into, here, away = both(m)
            pl.when(away)(into.wait_recv)
            pl.when(away)(out.wait_send)
            pl.when(jnp.logical_not(away))(here.wait)

    return (start, wait)


def gather_kernel(kinds, swaps, pairs, *refs):
    n = len(kinds)
    srcs, refs = (refs[:n], refs[n:])
    swap_in, refs = (refs[:swaps], refs[swaps:])
    pair_in, refs = (refs[:pairs], refs[pairs:])
    dsts, refs = (refs[:n], refs[n:])
    swap_out, refs = (refs[:swaps], refs[swaps:])
    pair_out, refs = (refs[:pairs], refs[pairs:])
    send_sem, recv_sem, local_sem, swap_sem, pair_sem = refs
    x, c, z, y = place()
    below, above = (z > 0, z < 3)
    nx, ny, partner = (device(1 - x, c, z, y), device(x, c, z, 1 - y), device(x, 1 - c, z, y))
    up, down = (
        device(x, c, jnp.minimum(z + 1, 3), y),
        device(x, c, jnp.maximum(z - 1, 0), y),
    )
    peers = [(None, nx), (None, ny), (None, partner), (below, down), (above, up)]
    if swaps:
        peers += swap_peers()
    greet(peers)

    def slot(a, core, xx, yy, k, half):
        i = (xx * 2 + core) * 8 + k * 2 + yy
        if kinds[a] == "split":
            if half == 0:
                return dsts[a].at[:, i]
            return dsts[a].at[0:2, i] if half == 1 else dsts[a].at[2:4, i]
        return dsts[a].at[i]

    def copies(kind, k, owner, half, to, core, own=False):
        out = []
        for a in half_members(kinds, half):
            there = slot(a, core, owner[0], owner[1], k, half)
            out.append(
                remote(
                    srcs[a] if own else there,
                    there,
                    send_sem.at[kind, a, k],
                    recv_sem.at[kind, a, k],
                    to,
                )
            )
        return out

    started = []

    def send(cond, kind, k, owner, half, to, own=False):
        def go():
            for copy in copies(kind, k, owner, half, to, c, own):
                copy.start()

        def finish():
            for copy in copies(kind, k, owner, half, to, c, own):
                copy.wait_send()

        guarded(cond, go)
        started.append((cond, finish))

    def recv(cond, kind, k, owner, half, core):
        def go():
            for copy in copies(kind, k, owner, half, partner, core):
                copy.wait_recv()

        guarded(cond, go)

    k_up, k_down, k_x, k_y, k_h1, k_h2, p_own, p_x, p_y, p_opp = range(10)
    me, at_x, at_y, opposite = ((x, y), (1 - x, y), (x, 1 - y), (1 - x, 1 - y))

    def level(off):
        k = z + off
        if off == 0:
            return (k, None)
        return (jnp.clip(k, 0, 3), k >= 0 if off < 0 else k <= 3)

    def both(cond, other):
        return other if cond is None else jnp.logical_and(cond, other)

    def column(off):
        k, ok = level(off)
        own = off == 0
        if off < 0:
            recv(ok, k_up, k, me, 0, c)
        if off > 0:
            recv(ok, k_down, k, me, 0, c)
        if off <= 0:
            send(both(ok, above), k_up, k, me, 0, up, own)
        if off >= 0:
            send(both(ok, below), k_down, k, me, 0, down, own)
        send(ok, k_x, k, me, 0, nx, own)
        send(ok, k_y, k, me, 0, ny, own)
        send(ok, p_own, k, me, 0, partner, own)

    def beside(off):
        k, ok = level(off)
        recv(ok, k_x, k, at_x, 0, c)
        send(ok, k_h1, k, at_x, 1, ny)
        send(ok, p_x, k, at_x, 0, partner)
        recv(ok, k_y, k, at_y, 0, c)
        send(ok, k_h2, k, at_y, 2, nx)
        send(ok, p_y, k, at_y, 0, partner)

    def across(off):
        k, ok = level(off)
        recv(ok, k_h1, k, opposite, 1, c)
        recv(ok, k_h2, k, opposite, 2, c)
        send(ok, p_opp, k, opposite, 0, partner)

    locals_ = []
    for a in range(n):
        copy = pltpu.make_async_copy(srcs[a], slot(a, c, x, y, z, 0), local_sem.at[a])
        copy.start()
        locals_.append(copy)
    for act, off in (
        (column, 0),
        ("pairs", 0),
        (column, -1),
        (column, 1),
        (beside, 0),
        (column, -2),
        (column, 2),
        (beside, -1),
        (beside, 1),
        (across, 0),
        (column, -3),
        (column, 3),
        ("swaps", 0),
        (beside, -2),
        (beside, 2),
        (across, -1),
        (across, 1),
        (beside, -3),
        (beside, 3),
        (across, -2),
        (across, 2),
        (across, -3),
        (across, 3),
    ):
        if act == "swaps":
            moves = [
                swap_copies(
                    swap_in[i], swap_out[i], swap_sem.at[i, 0], swap_sem.at[i, 1], swap_sem.at[i, 2]
                )
                for i in range(swaps)
            ]
            for start, _ in moves:
                start()
        elif act == "pairs":
            for i in range(pairs):
                row = pair_in[i].at[z % 2]

                @pl.when(c == z // 2)
                def _(row=row, i=i):
                    remote(row, pair_out[i], pair_sem.at[i, 0], pair_sem.at[i, 1], partner).start()
                    pltpu.make_async_copy(row, pair_out[i], pair_sem.at[i, 2]).start()
        else:
            act(off)
    for k in range(4):
        for kind, owner in ((p_own, me), (p_x, at_x), (p_y, at_y), (p_opp, opposite)):
            recv(None, kind, k, owner, 0, 1 - c)
    for cond, finish in started:
        guarded(cond, finish)
    for copy in locals_:
        copy.wait()
    for _, wait in moves:
        wait()
    for i in range(pairs):
        row = pair_in[i].at[z % 2]
        over = remote(row, pair_out[i], pair_sem.at[i, 0], pair_sem.at[i, 1], partner)
        here = pltpu.make_async_copy(row, pair_out[i], pair_sem.at[i, 2])

        @pl.when(c == z // 2)
        def _(over=over, here=here):
            over.wait_send()
            here.wait()

        pl.when(c != z // 2)(over.wait_recv)


def gather(kinds, arrays, swaps, pairs, collective_id):
    n, s, p = (len(arrays), len(swaps), len(pairs))
    outs = []
    for kind, array in zip(kinds, arrays):
        shape = array.shape[:1] + (32,) + array.shape[1:] if kind == "split" else (32,) + array.shape
        outs.append(jax.ShapeDtypeStruct(shape, array.dtype))
    outs += [jax.ShapeDtypeStruct(a.shape, a.dtype) for a in swaps]
    outs += [jax.ShapeDtypeStruct(a.shape[1:], a.dtype) for a in pairs]
    dma = pltpu.SemaphoreType.DMA
    return pl.pallas_call(
        functools.partial(gather_kernel, kinds, s, p),
        out_shape=outs,
        in_specs=[VMEM_SPEC] * (n + s + p),
        out_specs=[ANY_SPEC] * (n + s + p),
        scratch_shapes=[
            dma((10, n, 4)),
            dma((10, n, 4)),
            dma((n,)),
            dma((max(s, 1), 3, 2)),
            dma((max(p, 1), 3)),
        ],
        compiler_params=pltpu.CompilerParams(collective_id=collective_id, has_side_effects=True),
        name="gather",
    )(*arrays, *swaps, *pairs)


def scatter_kernel(kinds, swaps, *refs):
    n = len(kinds)
    srcs, refs = (refs[:n], refs[n:])
    swap_in, refs = (refs[:swaps], refs[swaps:])
    outs, refs = (refs[:n], refs[n:])
    swap_out, refs = (refs[:swaps], refs[swaps:])
    acc, refs = (refs[:n], refs[n:])
    mate, refs = (refs[:n], refs[n:])
    from_x, refs = (refs[:n], refs[n:])
    from_y, refs = (refs[:n], refs[n:])
    corner, refs = (refs[:n], refs[n:])
    chain, refs = (refs[:n], refs[n:])
    last, refs = (refs[:n], refs[n:])
    send_sem, recv_sem, local_sem, swap_sem = refs
    x, c, z, y = place()
    nx, ny, partner = (device(1 - x, c, z, y), device(x, c, z, 1 - y), device(x, 1 - c, z, y))
    up, down = (
        device(x, c, jnp.minimum(z + 1, 3), y),
        device(x, c, jnp.maximum(z - 1, 0), y),
    )
    peers = [(None, nx), (None, ny), (None, partner), (z > 0, down), (z < 3, up)]
    if swaps:
        peers += swap_peers()
    greet(peers)
    owners = ((x, y), (1 - x, y), (x, 1 - y), (1 - x, 1 - y))

    def level(step):
        side = z // 2
        near = side * (3 - z) + (1 - side) * z
        late = step // 2
        base = (1 - late) * (3 - step) + late * ((1 - near) * (3 - step) + near * (step - 2))
        return side * (3 - base) + (1 - side) * base

    def shard(a, core, owner, k):
        i = (owner[0] * 2 + core) * 8 + k * 2 + owner[1]
        return srcs[a].at[:, i] if kinds[a] == "split" else srcs[a].at[i]

    def half_of(ref, a, half):
        if half and kinds[a] == "split":
            return ref.at[0:2] if half == 1 else ref.at[2:4]
        return ref

    def load(a, k, q):
        return pltpu.make_async_copy(shard(a, c, owners[q], k), acc[a].at[k, q], local_sem.at[a, k, q])

    def over(a, k, q, core):
        return remote(
            shard(a, core, owners[q], k), mate[a].at[k, q], send_sem.at[q, a, k], recv_sem.at[q, a, k], partner
        )

    def hop(kind, a, k, q, half, target, to):
        return remote(
            half_of(acc[a].at[k, q], a, half),
            half_of(target[a].at[k], a, half),
            send_sem.at[kind, a, k],
            recv_sem.at[kind, a, k],
            to,
        )

    t_h1, t_h2, t_x, t_y, t_z, t_last = range(4, 10)

    def begin(step, _):
        k = level(step)
        for q in (3, 1, 2, 0):
            for a in range(n):
                over(a, k, q, 1 - c).start()
                load(a, k, q).start()
        return 0

    lax.fori_loop(0, 4, begin, 0)
    moves = [
        swap_copies(swap_in[i], swap_out[i], swap_sem.at[i, 0], swap_sem.at[i, 1], swap_sem.at[i, 2])
        for i in range(swaps)
    ]
    for start, _ in moves:
        start()

    def wide(ref):
        return ref[...].astype(jnp.float32)

    def arrived(a, k, q):
        load(a, k, q).wait()
        over(a, k, q, c).wait_recv()

    def first(step):
        k = level(step)
        for a in range(n):
            arrived(a, k, 3)
            here = acc[a].at[k, 3]
            here[...] = (wide(here) + wide(mate[a].at[k, 3])).astype(jnp.bfloat16)
            if a in half_members(kinds, 1):
                hop(t_h1, a, k, 3, 1, corner, ny).start()
            if a in half_members(kinds, 2):
                hop(t_h2, a, k, 3, 2, corner, nx).start()

    def second(step):
        k = level(step)
        for q, half, kind, target, to in (
            (1, 1, t_h1, from_x, nx),
            (2, 2, t_h2, from_y, ny),
        ):
            for a in range(n):
                arrived(a, k, q)
                here = acc[a].at[k, q]
                here[...] = (wide(here) + wide(mate[a].at[k, q])).astype(jnp.bfloat16)
                if a in half_members(kinds, half):
                    hop(kind, a, k, 3, half, corner, to).wait_recv()
                    part = half_of(here, a, half)
                    part[...] = (wide(part) + wide(half_of(corner[a].at[k], a, half))).astype(
                        jnp.bfloat16
                    )
                hop(t_x if q == 1 else t_y, a, k, q, 0, target, to).start()

    def gathered(a, k):
        arrived(a, k, 0)
        hop(t_x, a, k, 1, 0, from_x, nx).wait_recv()
        hop(t_y, a, k, 2, 0, from_y, ny).wait_recv()
        return (
            wide(acc[a].at[k, 0])
            + wide(mate[a].at[k, 0])
            + (wide(from_x[a].at[k]) + wide(from_y[a].at[k]))
        )

    def third(step):
        k = level(step)
        inner = jnp.logical_or(jnp.logical_and(k < z, z < 3), jnp.logical_and(k > z, z > 0))
        for a in range(n):
            here = acc[a].at[k, 0]
            here[...] = gathered(a, k).astype(jnp.bfloat16)

            @pl.when(inner)
            def _(a=a, here=here):
                hop(t_z, a, k, 0, 0, chain, up).wait_recv()
                here[...] = (wide(here) + wide(chain[a].at[k])).astype(jnp.bfloat16)

            def final_hop(to, kind, target, a=a):
                return remote(
                    acc[a].at[k, 0], target, send_sem.at[kind, a, k], recv_sem.at[kind, a, k], to
                )

            pl.when(k > z + 1)(final_hop(up, t_z, chain[a].at[k]).start)
            pl.when(k < z - 1)(final_hop(down, t_z, chain[a].at[k]).start)
            pl.when(k == z + 1)(final_hop(up, t_z, last[a].at[0]).start)
            pl.when(k == z - 1)(final_hop(down, t_last, last[a].at[1]).start)

    def body(step, _):
        pl.when(step < 4)(lambda: first(step))
        pl.when(jnp.logical_and(step >= 1, step < 5))(lambda: second(step - 1))
        pl.when(step >= 2)(lambda: third(step - 2))
        return 0

    lax.fori_loop(0, 5, body, 0)
    second_done = None
    for a in range(n):
        outs[a][...] = gathered(a, z)

        @pl.when(z > 0)
        def _(a=a):
            remote(last[a].at[0], last[a].at[0], send_sem.at[t_z, a, z], recv_sem.at[t_z, a, z], up).wait_recv()
            outs[a][...] += wide(last[a].at[0])

        @pl.when(z < 3)
        def _(a=a):
            remote(
                last[a].at[1], last[a].at[1], send_sem.at[t_last, a, z], recv_sem.at[t_last, a, z], up
            ).wait_recv()
            outs[a][...] += wide(last[a].at[1])

    def finish(step, _):
        k = level(step)
        for a in range(n):
            for q in range(4):
                over(a, k, q, 1 - c).wait_send()
            if a in half_members(kinds, 1):
                hop(t_h1, a, k, 3, 1, corner, ny).wait_send()
            if a in half_members(kinds, 2):
                hop(t_h2, a, k, 3, 2, corner, nx).wait_send()
            hop(t_x, a, k, 1, 0, from_x, nx).wait_send()
            hop(t_y, a, k, 2, 0, from_y, ny).wait_send()

            pl.when(jnp.logical_or(k > z, k < z - 1))(
                hop(t_z, a, k, 0, 0, chain, up).wait_send
            )
            pl.when(k == z - 1)(
                remote(
                    acc[a].at[k, 0], last[a].at[1], send_sem.at[t_last, a, k], recv_sem.at[t_last, a, k], down
                ).wait_send
            )
        return 0

    lax.fori_loop(0, 4, finish, 0)
    for _, wait in moves:
        wait()


def scatter(kinds, arrays, swaps, collective_id):
    n, s = (len(arrays), len(swaps))
    shards = []
    for kind, array in zip(kinds, arrays):
        shards.append(array.shape[:1] + array.shape[2:] if kind == "split" else array.shape[1:])
    dma = pltpu.SemaphoreType.DMA
    scratch = []
    for lead in ((4, 4), (4, 4), (4,), (4,), (4,), (4,), (2,)):
        scratch += [pltpu.VMEM(lead + shape, jnp.bfloat16) for shape in shards]
    return pl.pallas_call(
        functools.partial(scatter_kernel, kinds, s),
        out_shape=[jax.ShapeDtypeStruct(shape, jnp.float32) for shape in shards]
        + [jax.ShapeDtypeStruct(a.shape, a.dtype) for a in swaps],
        in_specs=[ANY_SPEC] * (n + s),
        out_specs=[VMEM_SPEC] * n + [ANY_SPEC] * s,
        scratch_shapes=scratch
        + [dma((10, n, 4)), dma((10, n, 4)), dma((n, 4, 4)), dma((max(s, 1), 3, 2))],
        compiler_params=pltpu.CompilerParams(
            collective_id=collective_id, has_side_effects=True, vmem_limit_bytes=60 * 1024 * 1024
        ),
        name="scatter",
    )(*arrays, *swaps)


def trade_kernel(to_heads, src, dst, send_sem, recv_sem, local_sem):
    x, c, z, y = place()
    others = ((y, 1 - c), (1 - y, c), (1 - y, 1 - c))
    greet([(None, device(x, core, z, yy)) for yy, core in others])

    def ends(yy, core, k, mine_y, mine_c):
        if to_heads:
            rows = (2 * mine_c + k) * 2 + mine_y
            return (src.at[yy * 2 + core, k], dst.at[rows])
        rows = (2 * core + k) * 2 + yy
        return (src.at[rows], dst.at[mine_y * 2 + mine_c, k])

    for k in range(2):
        a, b = ends(y, c, k, y, c)
        pltpu.make_async_copy(a, b, local_sem.at[k]).start()
        for i, (yy, core) in reversed(list(enumerate(others))):
            a, b = ends(yy, core, k, y, c)
            remote(a, b, send_sem.at[i, k], recv_sem.at[i, k], device(x, core, z, yy)).start()
    for k in range(2):
        a, b = ends(y, c, k, y, c)
        pltpu.make_async_copy(a, b, local_sem.at[k]).wait()
        for i, (yy, core) in enumerate(others):
            peer = device(x, core, z, yy)
            a, b = ends(yy, core, k, y, c)
            remote(a, b, send_sem.at[i, k], recv_sem.at[i, k], peer).wait_send()
            a, b = ends(y, c, k, yy, core)
            remote(b, b, send_sem.at[i, k], recv_sem.at[i, k], peer).wait_recv()


def trade(array, to_heads, collective_id):
    dma = pltpu.SemaphoreType.DMA
    width = array.shape[-1]
    shape = (8, 128, width) if to_heads else (4, 2, 128, width)
    return pl.pallas_call(
        functools.partial(trade_kernel, to_heads),
        out_shape=jax.ShapeDtypeStruct(shape, array.dtype),
        in_specs=[VMEM_SPEC],
        out_specs=VMEM_SPEC,
        scratch_shapes=[dma((3, 2)), dma((3, 2)), dma((2,))],
        compiler_params=pltpu.CompilerParams(collective_id=collective_id, has_side_effects=True),
        name="trade",
    )(array)


ROWS = 256
MASKED = -1e30
NT = (((1,), (1,)), ((), ()))
TN = (((0,), (0,)), ((), ()))


def mm(a, b, dims=(((1,), (0,)), ((), ()))):
    return lax.dot_general(a, b, dims, preferred_element_type=jnp.float32)


def angle_constants():
    half = D // 2
    inverse = 10000.0 ** (-np.arange(half, dtype=np.float64) / half)
    inverse = inverse.astype(np.float32).astype(np.float64)
    coarse = inverse[:, None] * (1023.0 - 128.0 * np.arange(16)[None, :])
    fine = inverse[:, None] * np.arange(128.0)[None, :]
    coarse_table = np.concatenate([np.sin(coarse), np.cos(coarse)], axis=0).astype(np.float32)
    fine_table = np.concatenate([np.sin(fine), np.cos(fine)], axis=0).astype(np.float32)
    return (coarse_table, fine_table)


def position_kernel(coarse_ref, fine_ref, w_ref, table_ref, keys_ref):
    half = D // 2
    fine_sin = fine_ref[:half, :]
    fine_cos = fine_ref[half:, :]
    weight = w_ref[...]
    for a in range(16):
        big_sin = coarse_ref[:half, a : a + 1]
        big_cos = coarse_ref[half:, a : a + 1]
        sines = big_sin * fine_cos - big_cos * fine_sin
        cosines = big_cos * fine_cos + big_sin * fine_sin
        piece = jnp.concatenate([sines, cosines], axis=0).astype(jnp.bfloat16)
        table_ref[:, a * 128 : (a + 1) * 128] = piece
        keys_ref[:, a * 128 : (a + 1) * 128] = mm(weight, piece, TN).astype(jnp.bfloat16)


def position_tables(w_pos):
    coarse, fine = angle_constants()
    return pl.pallas_call(
        position_kernel,
        out_shape=(
            jax.ShapeDtypeStruct((D, 2048), jnp.bfloat16),
            jax.ShapeDtypeStruct((192, 2048), jnp.bfloat16),
        ),
        name="positions",
    )(jnp.asarray(coarse), jnp.asarray(fine), w_pos)


def query_parts(q, vec, h, kind):
    q = q.astype(jnp.float32)
    lanes = slice(h * 64, h * 64 + 64)
    content = (q + vec[0:1, lanes]).astype(jnp.bfloat16).astype(jnp.float32) * DH ** (-0.5)
    position = (q + vec[1:2, lanes]).astype(jnp.bfloat16) * jnp.bfloat16(DH ** (-0.5))
    typed = q + vec[2:3, lanes]
    other = jnp.sum(typed * vec[3:4, lanes], axis=1, keepdims=True) * DH ** (-0.5)
    same = jnp.sum(typed * vec[4:5, lanes], axis=1, keepdims=True) * DH ** (-0.5)
    to_zero = jnp.where(kind > 0.5, other, same)
    to_one = jnp.where(kind > 0.5, same, other)
    return (content, position, typed, to_zero, to_one)


def wide_query(content, to_zero, to_one, side):
    rows = content.shape[0]
    lane = lax.broadcasted_iota(jnp.int32, (rows, 64), 1)

    def split(value):
        high = value.astype(jnp.bfloat16).astype(jnp.float32)
        return (high, value - high)

    zero_high, zero_low = split(to_zero)
    one_high, one_low = split(to_one)
    extra = jnp.where(
        lane == 0,
        zero_high,
        jnp.where(
            lane == 1, one_high, jnp.where(lane == 2, zero_low, jnp.where(lane == 3, one_low, side))
        ),
    )
    return jnp.concatenate([content, extra], axis=1).astype(jnp.bfloat16)


def attend_kernel(qkv_ref, side_ref, key_side_ref, vec_ref, keys_ref, attn_ref, probs_ref, wide_key):
    step = pl.program_id(0)
    rows = ROWS
    start = pl.multiple_of(step * rows, rows)
    vec = vec_ref[...]

    @pl.when(step == 0)
    def _():
        for h in range(3):
            key = qkv_ref[:, 192 + h * 64 : 256 + h * 64]
            wide_key[h] = jnp.concatenate([key, key_side_ref[...]], axis=1)

    block = qkv_ref[pl.ds(start, rows), 0:192]
    side = side_ref[pl.ds(start, rows), :].astype(jnp.float32)
    kind = side[:, 0:1]
    width = 1024 + rows
    from_n = pl.multiple_of(1024 - rows - start, 128)
    outs = []
    for h in range(3):
        content, position, _, to_zero, to_one = query_parts(
            block[:, h * 64 : h * 64 + 64], vec, h, kind
        )
        query = wide_query(content, to_zero, to_one, side)
        scores = mm(query, wide_key[h], NT)
        slab = mm(position, keys_ref[h * 64 : h * 64 + 64, pl.ds(from_n, width)])
        slab = pltpu.roll(slab, width - (rows - 1), 1, stride=1, stride_axis=0)
        scores = scores + slab[:, :1024]
        top = jnp.max(scores, axis=1, keepdims=True)
        expo = jnp.exp(scores - top)
        total = jnp.sum(expo, axis=1, keepdims=True)
        probs = (expo * (1.0 / total)).astype(jnp.bfloat16)
        probs_ref[h] = probs
        outs.append(mm(probs, qkv_ref[:, 384 + h * 64 : 448 + h * 64]))
    attn_ref[...] = jnp.concatenate(outs, axis=1).astype(jnp.bfloat16)


def attend(qkv, side, key_side, vec, keys):
    rows = ROWS
    whole = lambda shape: pl.BlockSpec(shape, lambda i: (0,) * len(shape))
    return pl.pallas_call(
        attend_kernel,
        grid=(1024 // rows,),
        out_shape=(
            jax.ShapeDtypeStruct((1024, 192), jnp.bfloat16),
            jax.ShapeDtypeStruct((3, 1024, 1024), jnp.bfloat16),
        ),
        in_specs=[
            whole((1024, 576)),
            whole((1024, 64)),
            whole((1024, 64)),
            whole((8, 192)),
            whole((192, 2048)),
        ],
        out_specs=(
            pl.BlockSpec((rows, 192), lambda i: (i, 0)),
            pl.BlockSpec((3, rows, 1024), lambda i: (0, i, 0)),
        ),
        scratch_shapes=[pltpu.VMEM((3, 1024, 128), jnp.bfloat16)],
        compiler_params=pltpu.CompilerParams(vmem_limit_bytes=48 * 1024 * 1024),
        name="attend",
    )(qkv, side, key_side, vec, keys)


def attend_back_kernel(
    qkv_ref,
    side_ref,
    key_side_ref,
    vec_ref,
    keys_ref,
    probs_ref,
    attn_ref,
    grad_ref,
    out_ref,
    grad_keys_ref,
    grad_vec_ref,
    wide_key,
    grad_key,
    grad_value,
    grad_table,
):
    step = pl.program_id(0)
    rows = ROWS
    start = pl.multiple_of(step * rows, rows)
    vec = vec_ref[...]

    @pl.when(step == 0)
    def _():
        for h in range(3):
            key = qkv_ref[:, 192 + h * 64 : 256 + h * 64]
            wide_key[h] = jnp.concatenate([key, key_side_ref[...]], axis=1)
        grad_key[...] = jnp.zeros_like(grad_key)
        grad_value[...] = jnp.zeros_like(grad_value)
        grad_table[...] = jnp.zeros_like(grad_table)
        grad_vec_ref[...] = jnp.zeros_like(grad_vec_ref)

    block = qkv_ref[pl.ds(start, rows), 0:192]
    side = side_ref[pl.ds(start, rows), :].astype(jnp.float32)
    kind = side[:, 0:1]
    width = 1024 + rows
    from_n = pl.multiple_of(1024 - rows - start, 128)
    scale = DH ** (-0.5)
    grads = grad_ref[...]
    outs = attn_ref[...].astype(jnp.float32)
    grad_queries = []
    row = lax.broadcasted_iota(jnp.int32, (rows, rows), 0)
    column = lax.broadcasted_iota(jnp.int32, (rows, rows), 1)
    reverse = jnp.where(row + column == rows - 1, 1.0, 0.0).astype(jnp.bfloat16)
    for h in range(3):
        lanes = slice(h * 64, h * 64 + 64)
        content, position, typed, _, _ = query_parts(block[:, lanes], vec, h, kind)
        probs = probs_ref[h]
        grad = grads[:, lanes]
        delta = jnp.sum(outs[:, lanes] * grad.astype(jnp.float32), axis=1, keepdims=True)
        grad_probs = mm(grad, qkv_ref[:, 384 + h * 64 : 448 + h * 64], NT)
        grad_value[h] += mm(probs, grad, TN)
        grad_scores = probs.astype(jnp.float32) * (grad_probs - delta)
        low = grad_scores.astype(jnp.bfloat16)
        grad_key[h] += mm(low, content.astype(jnp.bfloat16), TN)
        grad_wide = mm(low, wide_key[h])
        turned = mm(reverse, low)
        padded = jnp.concatenate([turned, jnp.zeros((rows, rows), jnp.float32)], axis=1)
        skew = pltpu.roll(padded, 0, 1, stride=1, stride_axis=0).astype(jnp.bfloat16)
        slab = keys_ref[lanes, pl.ds(from_n, width)]
        turned = mm(skew, slab, NT) * scale
        high = turned.astype(jnp.bfloat16)
        rest = (turned - high.astype(jnp.float32)).astype(jnp.bfloat16)
        grad_position = mm(reverse, high) + mm(reverse, rest)
        position = mm(reverse, position).astype(jnp.bfloat16)
        grad_table[lanes, pl.ds(from_n, width)] += mm(position, skew, TN)
        grad_content = grad_wide[:, :64] * scale
        to_zero = grad_wide[:, 64:65] * scale
        to_one = grad_wide[:, 65:66] * scale
        same = jnp.where(kind > 0.5, to_one, to_zero)
        other = jnp.where(kind > 0.5, to_zero, to_one)
        grad_typed = other * vec[3:4, lanes] + same * vec[4:5, lanes]
        total = lambda value: jnp.sum(value, axis=0, keepdims=True)
        grad_vec_ref[:, lanes] += jnp.concatenate(
            [
                total(grad_content),
                total(grad_position),
                total(grad_typed),
                total(other * typed),
                total(same * typed),
                jnp.zeros((3, 64), jnp.float32),
            ],
            axis=0,
        )
        grad_queries.append(grad_content + grad_position + grad_typed)
    out_ref[pl.ds(start, rows), 0:192] = jnp.concatenate(grad_queries, axis=1).astype(jnp.bfloat16)

    @pl.when(step == 1024 // rows - 1)
    def _():
        out_ref[:, 192:384] = jnp.concatenate([grad_key[h] for h in range(3)], axis=1).astype(
            jnp.bfloat16
        )
        out_ref[:, 384:576] = jnp.concatenate([grad_value[h] for h in range(3)], axis=1).astype(
            jnp.bfloat16
        )
        grad_keys_ref[...] = grad_table[...].astype(jnp.bfloat16)


def attend_back(qkv, side, key_side, vec, keys, probs, attn, grad):
    rows = ROWS
    whole = lambda shape: pl.BlockSpec(shape, lambda i: (0,) * len(shape))
    return pl.pallas_call(
        attend_back_kernel,
        grid=(1024 // rows,),
        out_shape=(
            jax.ShapeDtypeStruct((1024, 576), jnp.bfloat16),
            jax.ShapeDtypeStruct((192, 2048), jnp.bfloat16),
            jax.ShapeDtypeStruct((8, 192), jnp.float32),
        ),
        in_specs=[
            whole((1024, 576)),
            whole((1024, 64)),
            whole((1024, 64)),
            whole((8, 192)),
            whole((192, 2048)),
            pl.BlockSpec((3, rows, 1024), lambda i: (0, i, 0)),
            pl.BlockSpec((rows, 192), lambda i: (i, 0)),
            pl.BlockSpec((rows, 192), lambda i: (i, 0)),
        ],
        out_specs=(whole((1024, 576)), whole((192, 2048)), whole((8, 192))),
        scratch_shapes=[
            pltpu.VMEM((3, 1024, 128), jnp.bfloat16),
            pltpu.VMEM((3, 1024, 64), jnp.float32),
            pltpu.VMEM((3, 1024, 64), jnp.float32),
            pltpu.VMEM((192, 2048), jnp.float32),
        ],
        compiler_params=pltpu.CompilerParams(vmem_limit_bytes=56 * 1024 * 1024),
        name="attend_back",
    )(qkv, side, key_side, vec, keys, probs, attn, grad)


def document_sides(seg_row, type_row):
    length = seg_row.shape[0]
    own = (seg_row[:, None] == jnp.arange(8, dtype=jnp.int32)[None, :]).astype(jnp.float32)
    kind = type_row.astype(jnp.float32)[:, None]
    pad = jnp.zeros((length, 52), jnp.float32)
    side = jnp.concatenate([kind, kind, kind, kind, own, pad], axis=1).astype(jnp.bfloat16)
    key_side = jnp.concatenate(
        [1.0 - kind, kind, 1.0 - kind, kind, (1.0 - own) * MASKED, pad], axis=1
    ).astype(jnp.bfloat16)
    return (side, key_side)


KINDS = ("split", 1, 1, 2, 1, 2)


def sequence_device(
    tokens,
    seg_ids,
    token_types,
    attn_in,
    attn_out,
    pos_kernel,
    ffn_in,
    ffn_out,
    head_vectors,
    norm_gains,
    norm_shifts,
    out_bias,
    ffn_bias,
    cotangent,
):
    x, c, z, y = place()
    group = y * 2 + c
    low = jnp.bfloat16
    w_in_shard = attn_in.reshape(24, 3, 4, 192).transpose(2, 0, 1, 3).reshape(4, 24, 576)
    small = jnp.concatenate(
        [
            head_vectors,
            norm_gains,
            norm_shifts,
            out_bias,
            ffn_bias.reshape(4, 24),
            jnp.zeros((1, 24), low),
        ],
        axis=0,
    )
    small = jnp.pad(small, ((0, 0), (0, 104)))
    labels = jnp.stack([seg_ids, token_types], axis=1)
    w_in, w_pos, vectors, w_out, w_up, w_down, rows, cot, label = gather(
        KINDS,
        [w_in_shard, pos_kernel, small, attn_out, ffn_in, ffn_out],
        [tokens, cotangent],
        [labels],
        0,
    )
    w_in = w_in.reshape(4, D, 576)
    w_pos = w_pos.reshape(D, HD)
    w_out = w_out.reshape(HD, D)
    w_up = w_up.reshape(D, FF)
    w_down = w_down.reshape(FF, D)
    rows = rows.reshape(256, D)
    cot = cot.reshape(256, D)
    vectors_f = vectors[:, :, :24].astype(jnp.float32)
    up_bias = vectors_f[:, 11:15, :].reshape(FF)
    vectors_f = vectors_f.transpose(1, 0, 2).reshape(16, D)
    gains_f, shifts_f, biases_f = (vectors_f[5:7], vectors_f[7:9], vectors_f[9:11])
    w_pos_own = lax.dynamic_slice_in_dim(w_pos, group * 192, 192, axis=1)
    vec = jnp.pad(
        lax.dynamic_slice_in_dim(vectors_f[:5], group * 192, 192, axis=1), ((0, 3), (0, 0))
    )
    side, key_side = document_sides(label[0], label[1])

    proj = jnp.einsum("id,tdk->tik", rows, w_in, preferred_element_type=jnp.float32).astype(low)
    qkv = trade(proj.reshape(4, 2, 128, 576), True, 1).reshape(1024, 576)
    table, keys = position_tables(w_pos_own)
    attn_heads, probs = attend(qkv, side, key_side, vec, keys)
    attn = trade(attn_heads.reshape(8, 128, 192), False, 2)
    attn = attn.reshape(4, 256, 192).transpose(1, 0, 2).reshape(256, HD)
    rows_f = rows.astype(jnp.float32)
    branch = jnp.dot(attn, w_out, preferred_element_type=jnp.float32) + biases_f[0]
    first, normed_one, inv_one = layer_norm(rows_f + branch, gains_f[0], shifts_f[0])
    first_b = first.astype(low)
    pre_act = jnp.dot(first_b, w_up, preferred_element_type=jnp.float32) + up_bias
    hidden = gelu_tanh(pre_act).astype(low)
    second = jnp.dot(hidden, w_down, preferred_element_type=jnp.float32) + biases_f[1]
    result, normed_two, inv_two = layer_norm(first + second, gains_f[1], shifts_f[1])
    result = result.astype(low)

    grad_two = cot.astype(jnp.float32)
    gain_two = jnp.sum(grad_two * normed_two, axis=0)
    shift_two = jnp.sum(grad_two, axis=0)
    grad_h2 = norm_back(grad_two, normed_two, inv_two, gains_f[1])
    grad_second = grad_h2.astype(low)
    bias_two = jnp.sum(grad_second.astype(jnp.float32), axis=0)
    g_down = jnp.einsum("rf,rd->fd", hidden, grad_second, preferred_element_type=jnp.float32)
    grad_hidden = jnp.einsum("rd,fd->rf", grad_second, w_down, preferred_element_type=jnp.float32)
    grad_pre = jax.vjp(gelu_tanh, pre_act)[1](grad_hidden)[0].astype(low)
    g_upbias = jnp.sum(grad_pre.astype(jnp.float32), axis=0)
    g_up = jnp.einsum("rd,rf->df", first_b, grad_pre, preferred_element_type=jnp.float32)
    grad_first = grad_h2 + jnp.einsum(
        "rf,df->rd", grad_pre, w_up, preferred_element_type=jnp.float32
    )
    gain_one = jnp.sum(grad_first * normed_one, axis=0)
    shift_one = jnp.sum(grad_first, axis=0)
    grad_h1 = norm_back(grad_first, normed_one, inv_one, gains_f[0])
    grad_branch = grad_h1.astype(low)
    bias_one = jnp.sum(grad_branch.astype(jnp.float32), axis=0)
    g_out = jnp.einsum("rk,rd->kd", attn, grad_branch, preferred_element_type=jnp.float32)
    grad_attn = jnp.einsum(
        "rd,tkd->trk", grad_branch, w_out.reshape(4, 192, D), preferred_element_type=jnp.float32
    ).astype(low)

    grad_heads = trade(grad_attn.reshape(4, 2, 128, 192), True, 3).reshape(1024, 192)
    grad_qkv, grad_keys, grad_vec = attend_back(
        qkv, side, key_side, vec, keys, probs, attn_heads, grad_heads
    )
    grad_proj = trade(grad_qkv.reshape(8, 128, 576), False, 4).reshape(4, 256, 576)
    g_in = jnp.einsum("id,tik->tdk", rows, grad_proj, preferred_element_type=jnp.float32)
    grad_x = grad_h1 + jnp.einsum(
        "tik,tdk->id", grad_proj, w_in, preferred_element_type=jnp.float32
    )
    g_pos = jnp.einsum("cn,kn->ck", table, grad_keys, preferred_element_type=jnp.float32)
    own = (jnp.arange(4) == group).astype(jnp.float32)[None, :, None]
    g_pos = (g_pos[:, None, :] * own).reshape(D, HD).astype(low)
    g_head = (grad_vec[:5, None, :] * own).reshape(5, HD)
    g_small = jnp.concatenate(
        [
            g_head,
            jnp.stack([gain_one, gain_two, shift_one, shift_two, bias_one, bias_two]),
        ],
        axis=0,
    )
    g_small = jnp.concatenate(
        [
            g_small.reshape(11, 32, 24).transpose(1, 0, 2),
            g_upbias.reshape(32, 4, 24),
            jnp.zeros((32, 1, 24), jnp.float32),
        ],
        axis=1,
    )
    g_small = jnp.pad(g_small, ((0, 0), (0, 0), (0, 104))).astype(low)
    f_in, f_pos, f_small, f_out, f_up, f_down, out_rows, grad_rows = scatter(
        KINDS,
        [
            g_in.astype(low).reshape(4, 32, 24, 576),
            g_pos.reshape(32, 24, HD),
            g_small,
            g_out.astype(low).reshape(32, 24, D),
            g_up.astype(low).reshape(32, 24, FF),
            g_down.astype(low).reshape(32, 96, D),
        ],
        [result.reshape(2, 128, D), grad_x.astype(low).reshape(2, 128, D)],
        5,
    )
    f_in = f_in.reshape(4, 24, 3, 192).transpose(1, 2, 0, 3).reshape(24, 3 * HD)
    f_small = f_small[:, :24]
    return (
        out_rows,
        grad_rows.astype(jnp.float32),
        f_in,
        f_out,
        f_pos,
        f_up,
        f_down,
        f_small[0:5],
        f_small[5:7],
        f_small[7:9],
        f_small[9:11],
        f_small[11:15].reshape(96),
    )


def solution(mesh):
    placed = (
        P("dp", "fsdp", None),
        P("dp", None),
        P("dp", None),
        P(("dp", "fsdp"), None),
        P(("dp", "fsdp"), None),
        P(("dp", "fsdp"), None),
        P(("dp", "fsdp"), None),
        P(("dp", "fsdp"), None),
        P(None, ("dp", "fsdp")),
        P(None, ("dp", "fsdp")),
        P(None, ("dp", "fsdp")),
        P(None, ("dp", "fsdp")),
        P(("dp", "fsdp")),
        P("dp", "fsdp", None),
    )
    two_by_four = tuple(mesh.shape[name] for name in ("dp", "fsdp")) == (4, 8)
    return jax.shard_map(
        sequence_device if two_by_four else per_device,
        mesh=mesh,
        in_specs=placed,
        out_specs=(
            P("dp", "fsdp", None),
            P("dp", "fsdp", None),
            P(("dp", "fsdp"), None),
            P(("dp", "fsdp"), None),
            P(("dp", "fsdp"), None),
            P(("dp", "fsdp"), None),
            P(("dp", "fsdp"), None),
            P(None, ("dp", "fsdp")),
            P(None, ("dp", "fsdp")),
            P(None, ("dp", "fsdp")),
            P(None, ("dp", "fsdp")),
            P(("dp", "fsdp")),
        ),
        check_vma=False,
    )
```

```python
import functools

import jax
import jax.numpy as jnp
import numpy as np
from jax import lax
from jax.experimental import pallas as pl
from jax.experimental.pallas import tpu as pltpu
from jax.sharding import PartitionSpec as P

D = 768
H = 12
DH = 64
FF = 3072
HD = 768


EPSILON = 1e-06
HIGHEST_PREC = lax.Precision.HIGHEST


def gelu_tanh(values):
    return (
        0.5
        * values
        * (1.0 + jnp.tanh(0.7978845608028654 * (values + 0.044715 * values * values * values)))
    )


def angle_tables(positions, width):
    half_width = width // 2
    freq_index = jnp.arange(half_width, dtype=jnp.float32)
    inverse = jnp.power(10000.0, -freq_index / half_width)
    angles = positions[:, None] * inverse[None, :]
    return (jnp.sin(angles), jnp.cos(angles))


def layer_norm(values, gain, shift):
    center = values - jnp.mean(values, axis=-1, keepdims=True)
    inv_std = lax.rsqrt(jnp.mean(center * center, axis=-1, keepdims=True) + EPSILON)
    normed = center * inv_std
    return (normed * gain + shift, normed, inv_std)


def norm_back(grad_out, normed, inv_std, gain):
    grad_norm = grad_out * gain
    return inv_std * (
        grad_norm
        - jnp.mean(grad_norm, axis=-1, keepdims=True)
        - normed * jnp.mean(grad_norm * normed, axis=-1, keepdims=True)
    )


def fetch_forward(shards):
    return (
        lax.all_gather(shards[0], ("dp", "fsdp"), axis=0, tiled=True),
        lax.all_gather(shards[1], ("dp", "fsdp"), axis=0, tiled=True),
        lax.all_gather(shards[2], ("dp", "fsdp"), axis=0, tiled=True),
        lax.all_gather(shards[3], ("dp", "fsdp"), axis=0, tiled=True),
        lax.all_gather(shards[4], ("dp", "fsdp"), axis=0, tiled=True),
        lax.all_gather(shards[5], ("dp", "fsdp"), axis=1, tiled=True),
        lax.all_gather(shards[6], ("dp", "fsdp"), axis=1, tiled=True),
        lax.all_gather(shards[7], ("dp", "fsdp"), axis=1, tiled=True),
        lax.all_gather(shards[8], ("dp", "fsdp"), axis=1, tiled=True),
        lax.all_gather(shards[9], ("dp", "fsdp"), axis=0, tiled=True),
    )


def fetch_backward(shards):
    return (
        lax.all_gather(shards[0], ("dp", "fsdp"), axis=0, tiled=True),
        lax.all_gather(shards[1], ("dp", "fsdp"), axis=0, tiled=True),
        lax.all_gather(shards[2], ("dp", "fsdp"), axis=0, tiled=True),
        lax.all_gather(shards[3], ("dp", "fsdp"), axis=0, tiled=True),
        lax.all_gather(shards[4], ("dp", "fsdp"), axis=0, tiled=True),
        lax.all_gather(shards[5], ("dp", "fsdp"), axis=1, tiled=True),
        lax.all_gather(shards[6], ("dp", "fsdp"), axis=1, tiled=True),
        lax.all_gather(shards[7], ("dp", "fsdp"), axis=1, tiled=True),
        lax.all_gather(shards[8], ("dp", "fsdp"), axis=1, tiled=True),
        lax.all_gather(shards[9], ("dp", "fsdp"), axis=0, tiled=True),
    )


def score_block(q_content, q_rel, type_terms, keys3, k_rel, same_type):
    content = jnp.einsum("rhe,jhe->rhj", q_content, keys3, preferred_element_type=jnp.float32)
    position = jnp.einsum("rhc,jc->rhj", q_rel, k_rel, preferred_element_type=jnp.float32)
    typed = jnp.where(same_type, type_terms[:, :, 1:2], type_terms[:, :, 0:1])
    return DH ** (-0.5) * (content + position + typed)


def relative_queries(q_pos, w_pos, positions):
    proj_pos = jnp.einsum(
        "rhe,che->rhc", q_pos, w_pos.reshape(D, H, DH), preferred_element_type=jnp.float32
    )
    sines, cosines = angle_tables(positions, D)
    sin_q = sines[:, None, :]
    cos_q = cosines[:, None, :]
    half_width = D // 2
    pos_sin = proj_pos[..., :half_width]
    pos_cos = proj_pos[..., half_width:]
    q_rel = jnp.concatenate(
        [pos_sin * sin_q + pos_cos * cos_q, pos_cos * sin_q - pos_sin * cos_q], axis=-1
    ).astype(jnp.bfloat16)
    return (q_rel, sin_q, cos_q)


def forward_micro(weights, x_rows, seg_row, type_row, start, k_rel):
    w_in, w_out, w_pos, w_up, w_down, head_vec, gains, shifts, biases, up_bias = weights
    row_count = x_rows.shape[0]
    head_f = head_vec.astype(jnp.float32)
    gains_f = gains.astype(jnp.float32)
    shifts_f = shifts.astype(jnp.float32)
    biases_f = biases.astype(jnp.float32)
    proj = jnp.dot(x_rows, w_in, preferred_element_type=jnp.float32)
    query = proj[:, :HD]
    key_local = proj[:, HD : 2 * HD].astype(jnp.bfloat16)
    value_local = proj[:, 2 * HD :].astype(jnp.bfloat16)
    keys, values = (
        lax.all_gather(key_local, "fsdp", axis=0, tiled=True),
        lax.all_gather(value_local, "fsdp", axis=0, tiled=True),
    )
    keys3 = keys.reshape(keys.shape[0], H, DH)
    values3 = values.reshape(values.shape[0], H, DH)
    q_content = (query + head_f[0]).astype(jnp.bfloat16).reshape(row_count, H, DH)
    q_pos = (query + head_f[1]).astype(jnp.bfloat16).reshape(row_count, H, DH)
    q_type = (query + head_f[2]).reshape(row_count, H, DH)
    type_table = head_f[3:5].reshape(2, H, DH)
    type_terms = jnp.einsum("rhe,the->rht", q_type, type_table, precision=HIGHEST_PREC)
    positions = (start + jnp.arange(row_count, dtype=jnp.int32)).astype(jnp.float32)
    q_rel, sin_q, cos_q = relative_queries(q_pos, w_pos, positions)
    query_seg = lax.dynamic_slice_in_dim(seg_row, start, row_count)
    query_kind = lax.dynamic_slice_in_dim(type_row, start, row_count)
    allowed = (query_seg[:, None] == seg_row[None, :])[:, None, :]
    same_type = (query_kind[:, None] == type_row[None, :])[:, None, :]
    scores = score_block(q_content, q_rel, type_terms, keys3, k_rel, same_type)
    masked = jnp.where(allowed, scores, -1e30)
    top = jnp.max(masked, axis=-1, keepdims=True)
    expo = jnp.where(allowed, jnp.exp(masked - top), 0.0)
    total = jnp.sum(expo, axis=-1, keepdims=True)
    probs_b = (expo / total).astype(jnp.bfloat16)
    log_total = top + jnp.log(total)
    attn = (
        jnp.einsum("rhj,jhe->rhe", probs_b, values3, preferred_element_type=jnp.float32)
        .astype(jnp.bfloat16)
        .reshape(row_count, HD)
    )
    branch = jnp.dot(attn, w_out, preferred_element_type=jnp.float32) + biases_f[0]
    first, normed_one, inv_one = layer_norm(
        x_rows.astype(jnp.float32) + branch, gains_f[0], shifts_f[0]
    )
    first_b = first.astype(jnp.bfloat16)
    pre_act = jnp.dot(first_b, w_up, preferred_element_type=jnp.float32) + up_bias.astype(
        jnp.float32
    )
    hidden = gelu_tanh(pre_act).astype(jnp.bfloat16)
    second = jnp.dot(hidden, w_down, preferred_element_type=jnp.float32) + biases_f[1]
    result, normed_two, inv_two = layer_norm(first + second, gains_f[1], shifts_f[1])
    kept = (
        x_rows,
        q_content,
        q_pos,
        q_rel,
        q_type,
        type_terms,
        sin_q,
        cos_q,
        keys3,
        values3,
        allowed,
        same_type,
        log_total,
        attn,
        normed_one,
        inv_one,
        first_b,
        pre_act,
        hidden,
        normed_two,
        inv_two,
    )
    return (result.astype(jnp.bfloat16), kept)


def backward_micro(weights, kept, grad_rows, k_rel, totals):
    w_in, w_out, w_pos, w_up, w_down, head_vec, gains, shifts, biases, up_bias = weights
    (
        x_rows,
        q_content,
        q_pos,
        q_rel,
        q_type,
        type_terms,
        sin_q,
        cos_q,
        keys3,
        values3,
        allowed,
        same_type,
        log_total,
        attn,
        normed_one,
        inv_one,
        first_b,
        pre_act,
        hidden,
        normed_two,
        inv_two,
    ) = kept
    g_in, g_out, g_pos, g_up, g_down, g_head, g_gains, g_shifts, g_bias, g_upbias = totals
    row_count = x_rows.shape[0]
    head_f = head_vec.astype(jnp.float32)
    gains_f = gains.astype(jnp.float32)
    grad_two = grad_rows.astype(jnp.float32)
    gain_two = jnp.sum(grad_two * normed_two, axis=0)
    shift_two = jnp.sum(grad_two, axis=0)
    grad_h2 = norm_back(grad_two, normed_two, inv_two, gains_f[1])
    grad_second = grad_h2.astype(jnp.bfloat16)
    bias_two = jnp.sum(grad_second.astype(jnp.float32), axis=0)
    g_down = g_down + jnp.einsum(
        "rf,rd->fd", hidden, grad_second, preferred_element_type=jnp.float32
    )
    grad_hidden = jnp.einsum("rd,fd->rf", grad_second, w_down, preferred_element_type=jnp.float32)
    act_pull = jax.vjp(gelu_tanh, pre_act)[1]
    grad_pre = act_pull(grad_hidden)[0].astype(jnp.bfloat16)
    g_upbias = g_upbias + jnp.sum(grad_pre.astype(jnp.float32), axis=0)
    g_up = g_up + jnp.einsum("rd,rf->df", first_b, grad_pre, preferred_element_type=jnp.float32)
    grad_first = grad_h2 + jnp.einsum(
        "rf,df->rd", grad_pre, w_up, preferred_element_type=jnp.float32
    )
    gain_one = jnp.sum(grad_first * normed_one, axis=0)
    shift_one = jnp.sum(grad_first, axis=0)
    grad_h1 = norm_back(grad_first, normed_one, inv_one, gains_f[0])
    grad_branch = grad_h1.astype(jnp.bfloat16)
    bias_one = jnp.sum(grad_branch.astype(jnp.float32), axis=0)
    g_out = g_out + jnp.einsum("rk,rd->kd", attn, grad_branch, preferred_element_type=jnp.float32)
    grad_attn = (
        jnp.einsum("rd,kd->rk", grad_branch, w_out, preferred_element_type=jnp.float32)
        .astype(jnp.bfloat16)
        .reshape(row_count, H, DH)
    )
    scores = score_block(q_content, q_rel, type_terms, keys3, k_rel, same_type)
    probs = jnp.where(allowed, jnp.exp(scores - log_total), 0.0)
    grad_probs = jnp.einsum("rhe,jhe->rhj", grad_attn, values3, preferred_element_type=jnp.float32)
    delta = jnp.sum(probs * grad_probs, axis=-1, keepdims=True)
    grad_scores = (probs * (grad_probs - delta)).astype(jnp.bfloat16) * DH ** (-0.5)
    grad_content = jnp.einsum(
        "rhj,jhe->rhe", grad_scores, keys3, preferred_element_type=jnp.float32
    )
    grad_rel = jnp.einsum("rhj,jc->rhc", grad_scores, k_rel, preferred_element_type=jnp.float32)
    probs_b = probs.astype(jnp.bfloat16)
    value_part = jnp.einsum("rhj,rhe->jhe", probs_b, grad_attn, preferred_element_type=jnp.float32)
    key_part = jnp.einsum(
        "rhj,rhe->jhe", grad_scores, q_content, preferred_element_type=jnp.float32
    )
    key_full, value_full = (
        lax.psum_scatter(
            key_part.reshape(key_part.shape[0], HD).astype(jnp.bfloat16),
            "fsdp",
            scatter_dimension=0,
            tiled=True,
        ).astype(jnp.float32),
        lax.psum_scatter(
            value_part.reshape(value_part.shape[0], HD).astype(jnp.bfloat16),
            "fsdp",
            scatter_dimension=0,
            tiled=True,
        ).astype(jnp.float32),
    )
    scores_f = grad_scores.astype(jnp.float32)
    same_f = same_type.astype(jnp.float32)
    grad_same = jnp.sum(scores_f * same_f, axis=-1)
    grad_diff = jnp.sum(scores_f * (1.0 - same_f), axis=-1)
    grad_terms = jnp.stack([grad_diff, grad_same], axis=-1)
    type_table = head_f[3:5].reshape(2, H, DH)
    grad_qtype = jnp.einsum("rht,the->rhe", grad_terms, type_table, precision=HIGHEST_PREC)
    grad_table = jnp.einsum("rht,rhe->the", grad_terms, q_type, precision=HIGHEST_PREC)
    half_width = D // 2
    rel_first = grad_rel[..., :half_width]
    rel_second = grad_rel[..., half_width:]
    grad_proj = jnp.concatenate(
        [rel_first * sin_q - rel_second * cos_q, rel_first * cos_q + rel_second * sin_q], axis=-1
    ).astype(jnp.bfloat16)
    grad_qpos = jnp.einsum(
        "rhc,che->rhe", grad_proj, w_pos.reshape(D, H, DH), preferred_element_type=jnp.float32
    )
    g_pos = g_pos + jnp.einsum(
        "rhc,rhe->che", grad_proj, q_pos, preferred_element_type=jnp.float32
    ).reshape(D, HD)
    head_terms = jnp.stack(
        [
            jnp.sum(grad_content.reshape(row_count, HD), axis=0),
            jnp.sum(grad_qpos.reshape(row_count, HD), axis=0),
            jnp.sum(grad_qtype.reshape(row_count, HD), axis=0),
            grad_table[0].reshape(HD),
            grad_table[1].reshape(HD),
        ]
    )
    g_head = g_head + head_terms
    grad_query = (grad_content + grad_qpos + grad_qtype).reshape(row_count, HD).astype(jnp.bfloat16)
    grad_proj_in = jnp.concatenate(
        [grad_query, key_full.astype(jnp.bfloat16), value_full.astype(jnp.bfloat16)], axis=1
    )
    g_in = g_in + jnp.einsum("rd,rk->dk", x_rows, grad_proj_in, preferred_element_type=jnp.float32)
    grad_x = grad_h1 + jnp.einsum(
        "rk,dk->rd", grad_proj_in, w_in, preferred_element_type=jnp.float32
    )
    g_gains = g_gains + jnp.stack([gain_one, gain_two])
    g_shifts = g_shifts + jnp.stack([shift_one, shift_two])
    g_bias = g_bias + jnp.stack([bias_one, bias_two])
    return (grad_x, (g_in, g_out, g_pos, g_up, g_down, g_head, g_gains, g_shifts, g_bias, g_upbias))


def per_device(
    tokens,
    seg_ids,
    token_types,
    attn_in,
    attn_out,
    pos_kernel,
    ffn_in,
    ffn_out,
    head_vectors,
    norm_gains,
    norm_shifts,
    out_bias,
    ffn_bias,
    cotangent,
):
    shards = (
        attn_in,
        attn_out,
        pos_kernel,
        ffn_in,
        ffn_out,
        head_vectors,
        norm_gains,
        norm_shifts,
        out_bias,
        ffn_bias,
    )
    micro_count = tokens.shape[0]
    row_count = tokens.shape[1]
    start = lax.axis_index("fsdp") * row_count
    all_positions = jnp.arange(seg_ids.shape[1], dtype=jnp.float32)
    key_sin, key_cos = angle_tables(all_positions, D)
    k_rel = jnp.concatenate([key_cos, key_sin], axis=-1).astype(jnp.bfloat16)
    totals = (
        jnp.zeros((D, 3 * HD), jnp.float32),
        jnp.zeros((HD, D), jnp.float32),
        jnp.zeros((D, HD), jnp.float32),
        jnp.zeros((D, FF), jnp.float32),
        jnp.zeros((FF, D), jnp.float32),
        jnp.zeros((5, HD), jnp.float32),
        jnp.zeros((2, D), jnp.float32),
        jnp.zeros((2, D), jnp.float32),
        jnp.zeros((2, D), jnp.float32),
        jnp.zeros((FF,), jnp.float32),
    )
    results = []
    input_grads = []
    for micro_step in range(micro_count):
        forward_weights = fetch_forward(shards)
        result, kept = forward_micro(
            forward_weights,
            tokens[micro_step],
            seg_ids[micro_step],
            token_types[micro_step],
            start,
            k_rel,
        )
        backward_weights = fetch_backward(shards)
        grad_x, totals = backward_micro(
            backward_weights, kept, cotangent[micro_step], k_rel, totals
        )
        results.append(result)
        input_grads.append(grad_x)
    final = (
        lax.psum_scatter(totals[0], ("dp", "fsdp"), scatter_dimension=0, tiled=True),
        lax.psum_scatter(totals[1], ("dp", "fsdp"), scatter_dimension=0, tiled=True),
        lax.psum_scatter(totals[2], ("dp", "fsdp"), scatter_dimension=0, tiled=True),
        lax.psum_scatter(totals[3], ("dp", "fsdp"), scatter_dimension=0, tiled=True),
        lax.psum_scatter(totals[4], ("dp", "fsdp"), scatter_dimension=0, tiled=True),
        lax.psum_scatter(totals[5], ("dp", "fsdp"), scatter_dimension=1, tiled=True),
        lax.psum_scatter(totals[6], ("dp", "fsdp"), scatter_dimension=1, tiled=True),
        lax.psum_scatter(totals[7], ("dp", "fsdp"), scatter_dimension=1, tiled=True),
        lax.psum_scatter(totals[8], ("dp", "fsdp"), scatter_dimension=1, tiled=True),
        lax.psum_scatter(totals[9], ("dp", "fsdp"), scatter_dimension=0, tiled=True),
    )
    return (
        jnp.stack(results),
        jnp.stack(input_grads),
        final[0],
        final[1],
        final[2],
        final[3],
        final[4],
        final[5],
        final[6],
        final[7],
        final[8],
        final[9],
    )


MESH_ID = pl.DeviceIdType.MESH
Z_OFFSETS = (0, -1, 1, -2, 2, -3, 3)
ANY_SPEC = pl.BlockSpec(memory_space=pl.ANY)
VMEM_SPEC = pl.BlockSpec(memory_space=pltpu.VMEM)


def place():
    dp = lax.axis_index("dp")
    fs = lax.axis_index("fsdp")
    return (dp // 2, dp % 2, fs // 2, fs % 2)


def device(x, c, z, y):
    return (x * 2 + c, z * 2 + y)


def guarded(cond, action):
    if cond is None:
        action()
    else:
        pl.when(cond)(action)


def greet(peers):
    barrier = pltpu.get_barrier_semaphore()
    for cond, peer in peers:
        guarded(
            cond,
            lambda peer=peer: pl.semaphore_signal(
                barrier, inc=1, device_id=peer, device_id_type=MESH_ID
            ),
        )
    count = 0
    for cond, _ in peers:
        count = count + (1 if cond is None else cond.astype(jnp.int32))
    pl.semaphore_wait(barrier, count)


def remote(src, dst, send, recv, to):
    return pltpu.make_async_remote_copy(
        src_ref=src, dst_ref=dst, send_sem=send, recv_sem=recv, device_id=to, device_id_type=MESH_ID
    )


def half_members(kinds, half):
    if half == 0:
        return range(len(kinds))
    return [a for a, kind in enumerate(kinds) if kind in ("split", half)]


def swap_peers():
    x, c, z, y = place()
    peers = []
    for m in range(2):
        away = jnp.logical_or(z // 2 != c, z % 2 != m)
        peers.append((away, device(x, z // 2, 2 * c + m, y)))
    return peers


def swap_copies(src, dst, send, recv, local):
    x, c, z, y = place()

    def both(m):
        peer = device(x, z // 2, 2 * c + m, y)
        out = remote(src.at[m], dst.at[z % 2], send.at[m], recv.at[z % 2], peer)
        into = remote(src.at[m], dst.at[m], send.at[m], recv.at[m], peer)
        here = pltpu.make_async_copy(src.at[m], dst.at[m], local.at[m])
        away = jnp.logical_or(z // 2 != c, z % 2 != m)
        return (out, into, here, away)

    def start():
        for m in range(2):
            out, _, here, away = both(m)
            pl.when(away)(out.start)
            pl.when(jnp.logical_not(away))(here.start)

    def wait():
        for m in range(2):
            out, into, here, away = both(m)
            pl.when(away)(into.wait_recv)
            pl.when(away)(out.wait_send)
            pl.when(jnp.logical_not(away))(here.wait)

    return (start, wait)


ROWS = 256
MASKED = -1e30
NT = (((1,), (1,)), ((), ()))
TN = (((0,), (0,)), ((), ()))


def mm(a, b, dims=(((1,), (0,)), ((), ()))):
    return lax.dot_general(a, b, dims, preferred_element_type=jnp.float32)


def angle_constants():
    half = D // 2
    inverse = 10000.0 ** (-np.arange(half, dtype=np.float64) / half)
    inverse = inverse.astype(np.float32).astype(np.float64)
    coarse = inverse[:, None] * (1023.0 - 128.0 * np.arange(16)[None, :])
    fine = inverse[:, None] * np.arange(128.0)[None, :]
    coarse_table = np.concatenate([np.sin(coarse), np.cos(coarse)], axis=0).astype(np.float32)
    fine_table = np.concatenate([np.sin(fine), np.cos(fine)], axis=0).astype(np.float32)
    return (coarse_table, fine_table)


def query_parts(q, vec, h, kind):
    q = q.astype(jnp.float32)
    lanes = slice(h * 64, h * 64 + 64)
    content = (q + vec[0:1, lanes]).astype(jnp.bfloat16).astype(jnp.float32) * DH ** (-0.5)
    position = (q + vec[1:2, lanes]).astype(jnp.bfloat16) * jnp.bfloat16(DH ** (-0.5))
    typed = q + vec[2:3, lanes]
    other = jnp.sum(typed * vec[3:4, lanes], axis=1, keepdims=True) * DH ** (-0.5)
    same = jnp.sum(typed * vec[4:5, lanes], axis=1, keepdims=True) * DH ** (-0.5)
    to_zero = jnp.where(kind > 0.5, other, same)
    to_one = jnp.where(kind > 0.5, same, other)
    return (content, position, typed, to_zero, to_one)


def wide_query(content, to_zero, to_one, side):
    rows = content.shape[0]
    lane = lax.broadcasted_iota(jnp.int32, (rows, 64), 1)

    def split(value):
        high = value.astype(jnp.bfloat16).astype(jnp.float32)
        return (high, value - high)

    zero_high, zero_low = split(to_zero)
    one_high, one_low = split(to_one)
    extra = jnp.where(
        lane == 0,
        zero_high,
        jnp.where(
            lane == 1, one_high, jnp.where(lane == 2, zero_low, jnp.where(lane == 3, one_low, side))
        ),
    )
    return jnp.concatenate([content, extra], axis=1).astype(jnp.bfloat16)


def level_of(z, off):
    k = z + off
    if off == 0:
        return (k, None)
    return (jnp.clip(k, 0, 3), k >= 0 if off < 0 else k <= 3)


def both(cond, other):
    return other if cond is None else jnp.logical_and(cond, other)


GATHER_ORDER = (
    ("column", 0),
    ("column", -1),
    ("column", 1),
    ("beside", 0),
    ("column", -2),
    ("column", 2),
    ("beside", -1),
    ("beside", 1),
    ("across", 0),
    ("column", -3),
    ("column", 3),
    ("beside", -2),
    ("beside", 2),
    ("across", -1),
    ("across", 1),
    ("beside", -3),
    ("beside", 3),
    ("across", -2),
    ("across", 2),
    ("across", -3),
    ("across", 3),
)


def gather_plan(kinds, srcs, dsts, send_sem, recv_sem, local_sem):
    n = len(kinds)
    x, c, z, y = place()
    below, above = (z > 0, z < 3)
    nx, ny, partner = (device(1 - x, c, z, y), device(x, c, z, 1 - y), device(x, 1 - c, z, y))
    up, down = (
        device(x, c, jnp.minimum(z + 1, 3), y),
        device(x, c, jnp.maximum(z - 1, 0), y),
    )

    def slot(a, core, xx, yy, k):
        return dsts[a].at[(xx * 2 + core) * 8 + k * 2 + yy]

    def copies(kind, k, owner, half, to, core, own=False):
        out = []
        for a in range(n):
            if half and kinds[a] != half:
                continue
            there = slot(a, core, owner[0], owner[1], k)
            out.append(
                remote(
                    srcs[a] if own else there,
                    there,
                    send_sem.at[kind, a, k],
                    recv_sem.at[kind, a, k],
                    to,
                )
            )
        return out

    started = []

    def send(cond, kind, k, owner, half, to, own=False):
        def go():
            for copy in copies(kind, k, owner, half, to, c, own):
                copy.start()

        def finish():
            for copy in copies(kind, k, owner, half, to, c, own):
                copy.wait_send()

        guarded(cond, go)
        started.append((cond, finish))

    def recv(cond, kind, k, owner, half, core):
        def go():
            for copy in copies(kind, k, owner, half, partner, core):
                copy.wait_recv()

        guarded(cond, go)

    k_up, k_down, k_x, k_y, k_h1, k_h2, p_own, p_x, p_y, p_opp = range(10)
    me, at_x, at_y, opposite = ((x, y), (1 - x, y), (x, 1 - y), (1 - x, 1 - y))

    def act(name, off):
        k, ok = level_of(z, off)
        own = off == 0
        if name == "column":
            if own:
                for a in range(n):
                    pltpu.make_async_copy(srcs[a], slot(a, c, x, y, z), local_sem.at[a]).start()
            if off < 0:
                recv(ok, k_up, k, me, 0, c)
            if off > 0:
                recv(ok, k_down, k, me, 0, c)
            if off <= 0:
                send(both(ok, above), k_up, k, me, 0, up, own)
            if off >= 0:
                send(both(ok, below), k_down, k, me, 0, down, own)
            send(ok, k_x, k, me, 0, nx, own)
            send(ok, k_y, k, me, 0, ny, own)
            send(ok, p_own, k, me, 0, partner, own)
        elif name == "beside":
            recv(ok, k_x, k, at_x, 0, c)
            send(ok, k_h1, k, at_x, 1, ny)
            send(ok, p_x, k, at_x, 0, partner)
            recv(ok, k_y, k, at_y, 0, c)
            send(ok, k_h2, k, at_y, 2, nx)
            send(ok, p_y, k, at_y, 0, partner)
        else:
            recv(ok, k_h1, k, opposite, 1, c)
            recv(ok, k_h2, k, opposite, 2, c)
            send(ok, p_opp, k, opposite, 0, partner)

    def arrive():
        for k in range(4):
            for kind, owner in ((p_own, me), (p_x, at_x), (p_y, at_y), (p_opp, opposite)):
                recv(None, kind, k, owner, 0, 1 - c)
        for a in range(n):
            pltpu.make_async_copy(srcs[a], slot(a, c, x, y, z), local_sem.at[a]).wait()

    def leave():
        for cond, finish in started:
            guarded(cond, finish)

    return (act, arrive, leave)


def forward_kernel(
    tokens,
    cot,
    seg,
    kinds_row,
    w_att_shard,
    small_shard,
    out_shard,
    up_shard,
    down_shard,
    coarse,
    fine,
    x_seq,
    cot_own,
    w_att,
    small,
    w_out,
    w_up,
    w_down,
    sides,
    table,
    keys,
    qkv,
    probs,
    attn_heads,
    attn,
    vec,
    seg_other,
    kind_other,
    wide_key,
    block_sem,
    swap_sem,
    label_sem,
    quad_sem,
    att_send,
    att_recv,
    small_send,
    small_recv,
    small_local,
    big_send,
    big_recv,
    big_local,
    trade_send,
    trade_recv,
    trade_local,
):
    x, c, z, y = place()
    group = y * 2 + c
    below, above = (z > 0, z < 3)
    nx, ny, partner = (device(1 - x, c, z, y), device(x, c, z, 1 - y), device(x, 1 - c, z, y))
    cross = device(x, 1 - c, z, 1 - y)
    up, down = (
        device(x, c, jnp.minimum(z + 1, 3), y),
        device(x, c, jnp.maximum(z - 1, 0), y),
    )
    peers = [(None, nx), (None, ny), (None, partner), (None, cross), (below, down), (above, up)]
    greet(peers + swap_peers())

    def block_of(core, k, yy):
        return (2 * core + k) * 2 + yy

    def block_copy(kind, b, to):
        return remote(x_seq.at[b], x_seq.at[b], block_sem.at[kind, b], block_sem.at[3, b], to)

    def first_hop(m):
        peer = device(x, z // 2, 2 * c + m, y)
        away = jnp.logical_or(z // 2 != c, z % 2 != m)
        out = remote(
            tokens.at[m], x_seq.at[z * 2 + y], swap_sem.at[0, m], block_sem.at[3, z * 2 + y], peer
        )
        here = pltpu.make_async_copy(tokens.at[m], x_seq.at[z * 2 + y], swap_sem.at[1, m])
        return (away, out, here)

    for m in range(2):
        away, out, here = first_hop(m)
        pl.when(away)(out.start)
        pl.when(jnp.logical_not(away))(here.start)
    label_out = [
        remote(seg, seg_other, label_sem.at[0], label_sem.at[1], partner),
        remote(kinds_row, kind_other, label_sem.at[2], label_sem.at[3], partner),
    ]
    for copy in label_out:
        copy.start()

    quad = ((y, 1 - c), (1 - y, c), (1 - y, 1 - c))

    def piece(i, yy, core, dst_y, dst_c, to):
        return remote(
            w_att_shard.at[dst_y * 2 + dst_c],
            w_att.at[x, core, z, yy],
            quad_sem.at[0, i],
            quad_sem.at[1, i],
            to,
        )

    own_piece = pltpu.make_async_copy(w_att_shard.at[group], w_att.at[x, c, z, y], quad_sem.at[2, 0])
    own_piece.start()
    for i, (yy, core) in enumerate(quad):
        piece(i, y, c, yy, core, device(x, core, z, yy)).start()

    small_act, small_arrive, small_leave = gather_plan(
        (1,), [small_shard], [small], small_send, small_recv, small_local
    )
    big_act, big_arrive, big_leave = gather_plan(
        (2, 1, 2), [out_shard, up_shard, down_shard], [w_out, w_up, w_down], big_send, big_recv, big_local
    )
    small_act("column", 0)

    def level_copy(kind, xx, k, to):
        part = w_att.at[xx, :, k]
        return remote(part, part, att_send.at[kind, k], att_recv.at[kind, k], to)

    att_started = []

    def att_send_to(cond, kind, k, to):
        copy = level_copy(kind, x, k, to)
        guarded(cond, copy.start)
        att_started.append((cond, copy))

    def att_column(off):
        k, ok = level_of(z, off)
        if off == 0:
            own_piece.wait()
            for i, (yy, core) in enumerate(quad):
                piece(i, yy, core, yy, core, partner).wait_recv()
        if off < 0:
            guarded(ok, level_copy(0, x, k, up).wait_recv)
        if off > 0:
            guarded(ok, level_copy(1, x, k, down).wait_recv)
        if off <= 0:
            att_send_to(both(ok, above), 0, k, up)
        if off >= 0:
            att_send_to(both(ok, below), 1, k, down)
        att_send_to(ok, 2, k, nx)

    att_column(0)

    half = D // 2
    fine_sin = fine[:half, :]
    fine_cos = fine[half:, :]

    def angles(a):
        big_sin = coarse[:half, a : a + 1]
        big_cos = coarse[half:, a : a + 1]
        sines = big_sin * fine_cos - big_cos * fine_sin
        cosines = big_cos * fine_cos + big_sin * fine_sin
        table[:half, a * 128 : (a + 1) * 128] = sines.astype(jnp.bfloat16)
        table[half:, a * 128 : (a + 1) * 128] = cosines.astype(jnp.bfloat16)

    for a in range(8):
        angles(a)

    def got(m):
        b = block_of(c, m, y)
        own = jnp.logical_and(z // 2 == c, z % 2 == m)
        source = block_copy(0, b, partner)
        here = pltpu.make_async_copy(tokens.at[m], x_seq.at[b], swap_sem.at[1, m])
        pl.when(jnp.logical_not(own))(source.wait_recv)
        pl.when(own)(here.wait)
        block_copy(1, b, ny).start()
        block_copy(0, b, partner).start()

    got(0)
    got(1)
    att_column(-1)
    att_column(1)
    small_act("column", -1)
    small_act("column", 1)
    small_act("beside", 0)
    for a in range(8, 12):
        angles(a)
    for m in range(2):
        b = block_of(c, m, 1 - y)
        block_copy(1, b, ny).wait_recv()
        block_copy(2, b, partner).start()
    att_column(-2)
    att_column(2)
    for name, off in GATHER_ORDER[4:9]:
        small_act(name, off)
    att_column(-3)
    att_column(3)
    big_act("column", 0)
    cot_start, cot_wait = swap_copies(
        cot, cot_own, swap_sem.at[2], swap_sem.at[3], swap_sem.at[4]
    )
    cot_start()
    for a in range(12, 16):
        angles(a)
    for name, off in GATHER_ORDER[9:]:
        small_act(name, off)

    for copy in label_out:
        copy.wait()
    mine = (c == z // 2).astype(jnp.int32)
    odd = z % 2

    def row_of(here, there):
        own = here[0:1, :] * (1 - odd) + here[1:2, :] * odd
        other = there[0:1, :] * (1 - odd) + there[1:2, :] * odd
        return own * mine + other * (1 - mine)

    seg_row = row_of(seg[...], seg_other[...])
    kind_row = row_of(kinds_row[...], kind_other[...])
    line = lax.broadcasted_iota(jnp.int32, (128, 1024), 0)
    seg_all = jnp.broadcast_to(seg_row, (128, 1024))
    kind_all = jnp.broadcast_to(kind_row, (128, 1024)).astype(jnp.float32)
    side_t = jnp.where(line < 4, kind_all, jnp.where(seg_all == line - 4, 1.0, 0.0))
    key_t = jnp.where(
        line < 68,
        jnp.where(line % 2 == 0, 1.0 - kind_all, kind_all),
        jnp.where(line < 76, jnp.where(seg_all == line - 68, 0.0, MASKED), 0.0),
    )
    side_t = jnp.where(line < 64, side_t, key_t)
    sides[...] = jnp.transpose(side_t).astype(jnp.bfloat16)

    big_act("column", -1)
    big_act("column", 1)
    big_act("beside", 0)
    small_arrive()
    heads = jnp.concatenate(
        [small[group * 8 + i][:, :24].astype(jnp.float32) for i in range(8)], axis=1
    )
    vec[...] = heads[0:8, :]

    for k in range(4):
        level_copy(2, 1 - x, k, nx).wait_recv()
    weights = w_att[...].astype(jnp.float32).reshape(D, D).astype(jnp.bfloat16)
    keys[...] = mm(weights[:, 512:768], table[...], TN)[64:256, :].astype(jnp.bfloat16)

    for k in range(2):
        for yy in range(2):
            b = (2 * (1 - c) + k) * 2 + yy
            kind = jnp.where(yy == y, 0, 2)
            remote(x_seq.at[b], x_seq.at[b], block_sem.at[0, b], block_sem.at[3, b], partner).wait_recv()

    @pl.loop(0, 4)
    def _(step):
        both_rows = x_seq[pl.ds(step * 2, 2)].reshape(256, D)
        qkv[pl.ds(pl.multiple_of(step * 256, 256), 256), :] = mm(both_rows, weights)[:, :576].astype(
            jnp.bfloat16
        )

    for h in range(3):
        wide_key[h] = jnp.concatenate(
            [qkv[:, 192 + h * 64 : 256 + h * 64], sides[:, 64:128]], axis=1
        )
    big_act("column", -2)
    big_act("column", 2)
    big_act("beside", -1)
    big_act("beside", 1)
    big_act("across", 0)
    later = (
        (("column", -3), ("column", 3), ("beside", -2), ("beside", 2)),
        (("across", -1), ("across", 1)),
        (("beside", -3), ("beside", 3), ("across", -2), ("across", 2)),
        (("across", -3), ("across", 3)),
    )

    def send_rows(zb, start):
        core = zb // 2
        for yy in range(2):
            b = zb * 2 + yy
            src = attn_heads.at[pl.ds(pl.multiple_of(b * 128, 128), 128)]
            dst = attn.at[group, zb % 2]
            away = jnp.logical_or(core != c, yy != y)
            out = remote(
                src, dst, trade_send.at[b], trade_recv.at[group, zb % 2], device(x, core, z, yy)
            )
            here = pltpu.make_async_copy(src, dst, trade_local.at[zb % 2])
            if start:
                pl.when(away)(out.start)
                pl.when(jnp.logical_not(away))(here.start)
            else:
                pl.when(away)(out.wait_send)
                pl.when(jnp.logical_not(away))(here.wait)

    width = 1024 + ROWS

    @pl.loop(0, 4)
    def _(step):
        start = pl.multiple_of(step * ROWS, ROWS)
        block = qkv[pl.ds(start, ROWS), 0:192]
        side = sides[pl.ds(start, ROWS), 0:64].astype(jnp.float32)
        kind = side[:, 0:1]
        from_n = pl.multiple_of(1024 - ROWS - start, 128)
        outs = []
        values = vec[...]
        for h in range(3):
            content, position, _, to_zero, to_one = query_parts(
                block[:, h * 64 : h * 64 + 64], values, h, kind
            )
            query = wide_query(content, to_zero, to_one, side)
            scores = mm(query, wide_key[h], NT)
            slab = mm(position, keys[h * 64 : h * 64 + 64, pl.ds(from_n, width)])
            slab = pltpu.roll(slab, width - (ROWS - 1), 1, stride=1, stride_axis=0)
            scores = scores + slab[:, :1024]
            top = jnp.max(scores, axis=1, keepdims=True)
            expo = jnp.exp(scores - top)
            total = jnp.sum(expo, axis=1, keepdims=True)
            prob = (expo * (1.0 / total)).astype(jnp.bfloat16)
            probs[h, pl.ds(start, ROWS), :] = prob
            outs.append(mm(prob, qkv[:, 384 + h * 64 : 448 + h * 64]))
        attn_heads[pl.ds(start, ROWS), :] = jnp.concatenate(outs, axis=1).astype(jnp.bfloat16)
        send_rows(step, True)

    for acts in later:
        for name, off in acts:
            big_act(name, off)
    big_arrive()
    cot_wait()
    for zb in range(4):
        send_rows(zb, False)
    for yy, core in quad:
        for k in range(2):
            remote(
                attn.at[yy * 2 + core, k],
                attn.at[yy * 2 + core, k],
                trade_send.at[0],
                trade_recv.at[yy * 2 + core, k],
                partner,
            ).wait_recv()
    big_leave()
    small_leave()
    for cond, copy in att_started:
        guarded(cond, copy.wait_send)
    for i, (yy, core) in enumerate(quad):
        piece(i, y, c, yy, core, device(x, core, z, yy)).wait_send()
    for m in range(2):
        away, out, _ = first_hop(m)
        pl.when(away)(out.wait_send)
        block_copy(0, block_of(c, m, y), partner).wait_send()
        block_copy(1, block_of(c, m, y), ny).wait_send()
        block_copy(2, block_of(c, m, 1 - y), partner).wait_send()


def forward_attention(tokens, cot, seg, kinds_row, w_att, small, w_out, w_up, w_down, collective_id):
    low = jnp.bfloat16
    dma = pltpu.SemaphoreType.DMA
    coarse, fine = angle_constants()
    shape = jax.ShapeDtypeStruct
    outs = [
        (shape((8, 128, D), low), VMEM_SPEC),
        (shape((2, 128, D), low), ANY_SPEC),
        (shape((2, 2, 4, 2, 24, D), low), VMEM_SPEC),
        (shape((32, 16, 128), low), VMEM_SPEC),
        (shape((32, 24, D), low), ANY_SPEC),
        (shape((32, 24, FF), low), ANY_SPEC),
        (shape((32, 96, D), low), ANY_SPEC),
        (shape((1024, 128), low), VMEM_SPEC),
        (shape((D, 2048), low), VMEM_SPEC),
        (shape((192, 2048), low), VMEM_SPEC),
        (shape((1024, 576), low), VMEM_SPEC),
        (shape((3, 1024, 1024), low), VMEM_SPEC),
        (shape((1024, 192), low), VMEM_SPEC),
        (shape((4, 2, 128, 192), low), VMEM_SPEC),
        (shape((8, 192), jnp.float32), VMEM_SPEC),
    ]
    return pl.pallas_call(
        forward_kernel,
        out_shape=[o[0] for o in outs],
        in_specs=[VMEM_SPEC] * 11,
        out_specs=[o[1] for o in outs],
        scratch_shapes=[
            pltpu.VMEM((2, 1024), jnp.int32),
            pltpu.VMEM((2, 1024), jnp.int32),
            pltpu.VMEM((3, 1024, 128), low),
            dma((4, 8)),
            dma((5, 2)),
            dma((4,)),
            dma((3, 3)),
            dma((3, 4)),
            dma((3, 4)),
            dma((10, 1, 4)),
            dma((10, 1, 4)),
            dma((1,)),
            dma((10, 3, 4)),
            dma((10, 3, 4)),
            dma((3,)),
            dma((8,)),
            dma((4, 2)),
            dma((2,)),
        ],
        compiler_params=pltpu.CompilerParams(
            collective_id=collective_id, has_side_effects=True, vmem_limit_bytes=56 * 1024 * 1024
        ),
        name="forward_attention",
    )(
        tokens,
        cot,
        seg,
        kinds_row,
        w_att,
        small,
        w_out,
        w_up,
        w_down,
        jnp.asarray(coarse),
        jnp.asarray(fine),
    )


def farthest_first(z, step):
    side = z // 2
    near = side * (3 - z) + (1 - side) * z
    late = step // 2
    base = (1 - late) * (3 - step) + late * ((1 - near) * (3 - step) + near * (step - 2))
    return side * (3 - base) + (1 - side) * base


def wide(ref):
    return ref[...].astype(jnp.float32)


def scatter_plan(kinds, srcs, outs, buffers, send_sem, recv_sem, local_sem):
    n = len(kinds)
    acc, mate, from_x, from_y, corner, chain, last = (
        buffers[i * n : (i + 1) * n] for i in range(7)
    )
    x, c, z, y = place()
    nx, ny, partner = (device(1 - x, c, z, y), device(x, c, z, 1 - y), device(x, 1 - c, z, y))
    up, down = (
        device(x, c, jnp.minimum(z + 1, 3), y),
        device(x, c, jnp.maximum(z - 1, 0), y),
    )
    owners = ((x, y), (1 - x, y), (x, 1 - y), (1 - x, 1 - y))
    low = jnp.bfloat16

    def shard(a, core, owner, k):
        return srcs[a].at[(owner[0] * 2 + core) * 8 + k * 2 + owner[1]]

    def load(a, k, q):
        return pltpu.make_async_copy(shard(a, c, owners[q], k), acc[a].at[k, q], local_sem.at[a, k, q])

    def over(a, k, q, core):
        return remote(
            shard(a, core, owners[q], k),
            mate[a].at[k, q],
            send_sem.at[q, a, k],
            recv_sem.at[q, a, k],
            partner,
        )

    def hop(kind, a, k, q, target, to):
        return remote(acc[a].at[k, q], target, send_sem.at[kind, a, k], recv_sem.at[kind, a, k], to)

    t_half, t_x, t_y, t_z, t_last = range(4, 9)

    def half_to(a):
        return ny if kinds[a] == 1 else nx

    def begin():
        @pl.loop(0, 4)
        def _(step):
            k = farthest_first(z, step)
            for q in (3, 1, 2, 0):
                for a in range(n):
                    over(a, k, q, 1 - c).start()
                    load(a, k, q).start()

    def arrived(a, k, q):
        load(a, k, q).wait()
        over(a, k, q, c).wait_recv()

    def first(step):
        k = farthest_first(z, step)
        for a in range(n):
            arrived(a, k, 3)
            here = acc[a].at[k, 3]
            here[...] = (wide(here) + wide(mate[a].at[k, 3])).astype(low)
            hop(t_half, a, k, 3, corner[a].at[k], half_to(a)).start()

    def second(step):
        k = farthest_first(z, step)
        for q, half, kind, target, to in ((1, 1, t_x, from_x, nx), (2, 2, t_y, from_y, ny)):
            for a in range(n):
                arrived(a, k, q)
                here = acc[a].at[k, q]
                if kinds[a] == half:
                    hop(t_half, a, k, 3, corner[a].at[k], to).wait_recv()
                    here[...] = (
                        wide(here) + wide(mate[a].at[k, q]) + wide(corner[a].at[k])
                    ).astype(low)
                else:
                    here[...] = (wide(here) + wide(mate[a].at[k, q])).astype(low)
                hop(kind, a, k, q, target[a].at[k], to).start()

    def gathered(a, k):
        arrived(a, k, 0)
        hop(t_x, a, k, 1, from_x[a].at[k], nx).wait_recv()
        hop(t_y, a, k, 2, from_y[a].at[k], ny).wait_recv()
        return (
            wide(acc[a].at[k, 0])
            + wide(mate[a].at[k, 0])
            + (wide(from_x[a].at[k]) + wide(from_y[a].at[k]))
        )

    def third(step):
        k = farthest_first(z, step)
        inner = jnp.logical_or(jnp.logical_and(k < z, z < 3), jnp.logical_and(k > z, z > 0))
        for a in range(n):
            here = acc[a].at[k, 0]
            here[...] = gathered(a, k).astype(low)

            @pl.when(inner)
            def _(a=a, here=here):
                hop(t_z, a, k, 0, chain[a].at[k], up).wait_recv()
                here[...] = (wide(here) + wide(chain[a].at[k])).astype(low)

            pl.when(k > z + 1)(hop(t_z, a, k, 0, chain[a].at[k], up).start)
            pl.when(k < z - 1)(hop(t_z, a, k, 0, chain[a].at[k], down).start)
            pl.when(k == z + 1)(hop(t_z, a, k, 0, last[a].at[0], up).start)
            pl.when(k == z - 1)(hop(t_last, a, k, 0, last[a].at[1], down).start)

    def body(step):
        pl.when(step < 4)(lambda: first(step))
        pl.when(jnp.logical_and(step >= 1, step < 5))(lambda: second(step - 1))
        pl.when(step >= 2)(lambda: third(step - 2))

    def end():
        for a in range(n):
            outs[a][...] = gathered(a, z)

            @pl.when(z > 0)
            def _(a=a):
                hop(t_z, a, z, 0, last[a].at[0], up).wait_recv()
                outs[a][...] += wide(last[a].at[0])

            @pl.when(z < 3)
            def _(a=a):
                hop(t_last, a, z, 0, last[a].at[1], down).wait_recv()
                outs[a][...] += wide(last[a].at[1])

    def leave():
        @pl.loop(0, 4)
        def _(step):
            k = farthest_first(z, step)
            for a in range(n):
                for q in range(4):
                    over(a, k, q, 1 - c).wait_send()
                hop(t_half, a, k, 3, corner[a].at[k], half_to(a)).wait_send()
                hop(t_x, a, k, 1, from_x[a].at[k], nx).wait_send()
                hop(t_y, a, k, 2, from_y[a].at[k], ny).wait_send()
                pl.when(jnp.logical_or(k > z, k < z - 1))(
                    hop(t_z, a, k, 0, chain[a].at[k], up).wait_send
                )
                pl.when(k == z - 1)(hop(t_last, a, k, 0, last[a].at[1], down).wait_send)

    return (begin, body, end, leave)


def scatter_buffers(shards):
    out = []
    for lead in ((4, 4), (4, 4), (4,), (4,), (4,), (4,), (2,)):
        out += [pltpu.VMEM(lead + shape, jnp.bfloat16) for shape in shards]
    return out


def scatter_semaphores(n):
    dma = pltpu.SemaphoreType.DMA
    return [dma((9, n, 4)), dma((9, n, 4)), dma((n, 4, 4))]


BIG_SHARDS = ((24, D), (24, FF), (96, D))


def backward_kernel(
    grad_attn,
    grad_h1,
    result,
    g_small,
    g_out,
    g_up,
    g_down,
    qkv,
    sides,
    vec_small,
    table,
    keys,
    probs,
    attn_heads,
    x_seq,
    w_att,
    out_rows,
    out_grad,
    f_att,
    f_small,
    f_out,
    f_up,
    f_down,
    grad_heads,
    grad_qkv,
    wide_key,
    weights,
    grad_key,
    grad_value,
    grad_table,
    grad_vec,
    g_wide,
    g_att,
    att_x,
    att_z,
    att_last,
    att_q,
    dx_part,
    dx_in,
    dx_y,
    dx_out,
    dx_back,
    small_full,
    trade_send,
    trade_recv,
    trade_local,
    swap_sem,
    att_send,
    att_recv,
    quad_sem,
    dx_sem,
    *rest,
):
    small_buffers, rest = (rest[:7], rest[7:])
    small_sems, rest = (rest[:3], rest[3:])
    big_buffers, big_sems = (rest[:21], rest[21:])
    low = jnp.bfloat16
    x, c, z, y = place()
    group = y * 2 + c
    nx, ny, partner = (device(1 - x, c, z, y), device(x, c, z, 1 - y), device(x, 1 - c, z, y))
    cross = device(x, 1 - c, z, 1 - y)
    up, down = (
        device(x, c, jnp.minimum(z + 1, 3), y),
        device(x, c, jnp.maximum(z - 1, 0), y),
    )
    peers = [(None, nx), (None, ny), (None, partner), (None, cross), (z > 0, down), (z < 3, up)]
    greet(peers + swap_peers())
    quad = ((y, 1 - c), (1 - y, c), (1 - y, 1 - c))

    def trade_copy(i, k):
        yy, core = quad[i]
        b = (2 * c + k) * 2 + y
        return remote(
            grad_attn.at[yy * 2 + core, k],
            grad_heads.at[b],
            trade_send.at[i, k],
            trade_recv.at[b],
            device(x, core, z, yy),
        )

    def trade_here(k):
        b = (2 * c + k) * 2 + y
        return pltpu.make_async_copy(grad_attn.at[group, k], grad_heads.at[b], trade_local.at[k])

    for k in range(2):
        for i in (2, 1, 0):
            trade_copy(i, k).start()
        trade_here(k).start()
    big_begin, big_body, big_end, big_leave = scatter_plan(
        (2, 1, 2), [g_out, g_up, g_down], [f_out, f_up, f_down], big_buffers, *big_sems
    )
    small_begin, small_body, small_end, small_leave = scatter_plan(
        (1,), [small_full], [f_small], small_buffers, *small_sems
    )
    big_begin()
    result_start, result_wait = swap_copies(
        result, out_rows, swap_sem.at[0], swap_sem.at[1], swap_sem.at[2]
    )
    result_start()
    vec = vec_small[...]
    for h in range(3):
        key = qkv[:, 192 + h * 64 : 256 + h * 64]
        wide_key[h] = jnp.concatenate([key, sides[:, 64:128]], axis=1)
    weights[...] = wide(w_att).reshape(D, D).astype(low)
    grad_key[...] = jnp.zeros_like(grad_key)
    grad_value[...] = jnp.zeros_like(grad_value)
    grad_table[...] = jnp.zeros_like(grad_table)
    grad_vec[...] = jnp.zeros_like(grad_vec)
    for k in range(2):
        trade_here(k).wait()
        for yy, core in quad:
            b = (2 * core + k) * 2 + yy
            remote(
                grad_heads.at[b], grad_heads.at[b], trade_send.at[0, 0], trade_recv.at[b], partner
            ).wait_recv()

    width = 1024 + ROWS
    scale = DH ** (-0.5)

    @pl.loop(0, 4)
    def _(step):
        big_body(step)
        start = pl.multiple_of(step * ROWS, ROWS)
        block = qkv[pl.ds(start, ROWS), 0:192]
        side = sides[pl.ds(start, ROWS), 0:64].astype(jnp.float32)
        kind = side[:, 0:1]
        from_n = pl.multiple_of(1024 - ROWS - start, 128)
        grads = grad_heads[pl.ds(step * 2, 2)].reshape(ROWS, 192)
        outs = attn_heads[pl.ds(start, ROWS), :].astype(jnp.float32)
        grad_queries = []
        row = lax.broadcasted_iota(jnp.int32, (ROWS, ROWS), 0)
        column = lax.broadcasted_iota(jnp.int32, (ROWS, ROWS), 1)
        reverse = jnp.where(row + column == ROWS - 1, 1.0, 0.0).astype(low)
        for h in range(3):
            lanes = slice(h * 64, h * 64 + 64)
            content, position, typed, _, _ = query_parts(block[:, lanes], vec, h, kind)
            prob = probs[h, pl.ds(start, ROWS), :]
            grad = grads[:, lanes]
            delta = jnp.sum(outs[:, lanes] * grad.astype(jnp.float32), axis=1, keepdims=True)
            grad_probs = mm(grad, qkv[:, 384 + h * 64 : 448 + h * 64], NT)
            grad_value[h] += mm(prob, grad, TN)
            grad_scores = (prob.astype(jnp.float32) * (grad_probs - delta)).astype(low)
            grad_key[h] += mm(grad_scores, content.astype(low), TN)
            grad_wide = mm(grad_scores, wide_key[h])
            turned = mm(reverse, grad_scores)
            padded = jnp.concatenate([turned, jnp.zeros((ROWS, ROWS), jnp.float32)], axis=1)
            skew = pltpu.roll(padded, 0, 1, stride=1, stride_axis=0).astype(low)
            slab = keys[lanes, pl.ds(from_n, width)]
            turned = mm(skew, slab, NT) * scale
            high = turned.astype(low)
            low_part = (turned - high.astype(jnp.float32)).astype(low)
            grad_position = mm(reverse, high) + mm(reverse, low_part)
            position = mm(reverse, position).astype(low)
            grad_table[lanes, pl.ds(from_n, width)] += mm(position, skew, TN)
            grad_content = grad_wide[:, :64] * scale
            to_zero = grad_wide[:, 64:65] * scale
            to_one = grad_wide[:, 65:66] * scale
            same = jnp.where(kind > 0.5, to_one, to_zero)
            other = jnp.where(kind > 0.5, to_zero, to_one)
            grad_typed = other * vec[3:4, lanes] + same * vec[4:5, lanes]
            total = lambda value: jnp.sum(value, axis=0, keepdims=True)
            grad_vec[:, lanes] += jnp.concatenate(
                [
                    total(grad_content),
                    total(grad_position),
                    total(grad_typed),
                    total(other * typed),
                    total(same * typed),
                    jnp.zeros((3, 64), jnp.float32),
                ],
                axis=0,
            )
            grad_queries.append(grad_content + grad_position + grad_typed)
        grad_qkv[pl.ds(start, ROWS), 0:192] = jnp.concatenate(grad_queries, axis=1).astype(low)

    grad_qkv[:, 192:384] = jnp.concatenate([grad_key[h] for h in range(3)], axis=1).astype(low)
    grad_qkv[:, 384:576] = jnp.concatenate([grad_value[h] for h in range(3)], axis=1).astype(low)

    small_full[...] = g_small[...]
    line = lax.broadcasted_iota(jnp.int32, (16, 128), 0)
    for i in range(8):
        part = jnp.concatenate(
            [grad_vec[:, i * 24 : i * 24 + 24], jnp.zeros((8, 104), jnp.float32)], axis=1
        )
        part = jnp.concatenate([part, jnp.zeros((8, 128), jnp.float32)], axis=0)
        here = small_full.at[group * 8 + i]
        here[...] = jnp.where(line < 5, part, wide(here)).astype(low)
    small_begin()

    def dx_rows(core, k):
        start = pl.multiple_of((2 * core + k) * 256, 256)
        value = mm(grad_qkv[pl.ds(start, 256), :], weights[:, :576], NT)
        dx_part[pl.ds((2 * core + k) * 2, 2)] = value.astype(low).reshape(2, 128, D)

    def dx_over(core, k):
        part = dx_part.at[pl.ds((2 * core + k) * 2, 2)]
        return remote(part, dx_in.at[k], dx_sem.at[0, k], dx_sem.at[1, k], partner)

    for k in range(2):
        dx_rows(1 - c, k)
        dx_over(1 - c, k).start()

    g_wide[:, 0:576] = mm(x_seq[...].reshape(1024, D), grad_qkv[...], TN)
    g_wide[:, 576:768] = mm(table[...], grad_table[...].astype(low), NT)
    g_att[...] = g_wide[...].reshape(2, 2, 4, 2, 24, D).astype(low)

    def att_over(k):
        return remote(g_att.at[1 - x, :, k], att_x.at[k], att_send.at[0, k], att_recv.at[0, k], nx)

    for step in range(4):
        att_over(farthest_first(z, step)).start()
    small_body(0)
    for k in range(2):
        dx_rows(c, k)

    def dx_out_copy(k):
        return remote(dx_out.at[k], dx_y.at[k], dx_sem.at[2, k], dx_sem.at[3, k], ny)

    for k in range(2):
        dx_over(c, k).wait_recv()
        b = (2 * c + k) * 2 + 1 - y
        dx_out[k] = (wide(dx_part.at[b]) + wide(dx_in.at[k, 1 - y])).astype(low)
        dx_out_copy(k).start()
    big_body(4)
    small_body(1)

    def att_hop(kind, k, target, to):
        part = g_att.at[x, :, k]
        return remote(part, target, att_send.at[kind, k], att_recv.at[kind, k], to)

    for step in range(3):
        k = farthest_first(z, step)
        att_over(k).wait_recv()
        inner = jnp.logical_or(jnp.logical_and(k < z, z < 3), jnp.logical_and(k > z, z > 0))
        here = g_att.at[x, :, k]
        here[...] = (wide(here) + wide(att_x.at[k])).astype(low)

        @pl.when(inner)
        def _(here=here, k=k):
            att_hop(1, k, att_z.at[k], up).wait_recv()
            here[...] = (wide(here) + wide(att_z.at[k])).astype(low)

        pl.when(k > z + 1)(att_hop(1, k, att_z.at[k], up).start)
        pl.when(k < z - 1)(att_hop(1, k, att_z.at[k], down).start)
        pl.when(k == z + 1)(att_hop(1, k, att_last.at[0], up).start)
        pl.when(k == z - 1)(att_hop(2, k, att_last.at[1], down).start)
        small_body(step + 2)

    back_start, back_wait = swap_copies(
        dx_back.at[0], dx_back.at[1], swap_sem.at[3], swap_sem.at[4], swap_sem.at[5]
    )
    for k in range(2):
        dx_out_copy(k).wait_recv()
        b = (2 * c + k) * 2 + y
        value = wide(dx_part.at[b]) + wide(dx_in.at[k, y]) + wide(dx_y.at[k]) + grad_h1[k]
        dx_back[0, k] = value.astype(low)
    back_start()

    att_over(z).wait_recv()
    g_att[x, :, z] = (wide(g_att.at[x, :, z]) + wide(att_x.at[z])).astype(low)

    @pl.when(z > 0)
    def _():
        att_hop(1, z, att_last.at[0], up).wait_recv()
        g_att[x, :, z] = (wide(g_att.at[x, :, z]) + wide(att_last.at[0])).astype(low)

    @pl.when(z < 3)
    def _():
        att_hop(2, z, att_last.at[1], down).wait_recv()
        g_att[x, :, z] = (wide(g_att.at[x, :, z]) + wide(att_last.at[1])).astype(low)

    def quad_copy(i):
        yy, core = quad[i]
        return remote(
            g_att.at[x, core, z, yy],
            att_q.at[group],
            quad_sem.at[0, i],
            quad_sem.at[1, i],
            device(x, core, z, yy),
        )

    for i in range(3):
        quad_copy(i).start()
    small_end()
    big_end()
    f_att[group] = wide(g_att.at[x, c, z, y])
    for i, (yy, core) in enumerate(quad):
        other = yy * 2 + core
        remote(
            att_q.at[other], att_q.at[other], quad_sem.at[0, i], quad_sem.at[1, i], partner
        ).wait_recv()
        f_att[other] = wide(att_q.at[other])
    back_wait()
    out_grad[...] = wide(dx_back.at[1])
    result_wait()
    for k in range(2):
        for i in range(3):
            trade_copy(i, k).wait_send()
        dx_over(1 - c, k).wait_send()
        dx_out_copy(k).wait_send()
    for i in range(3):
        quad_copy(i).wait_send()
    for step in range(4):
        k = farthest_first(z, step)
        att_over(k).wait_send()
        pl.when(jnp.logical_or(k > z, k < z - 1))(att_hop(1, k, att_z.at[k], up).wait_send)
        pl.when(k == z - 1)(att_hop(2, k, att_last.at[1], down).wait_send)
    big_leave()
    small_leave()


def backward_attention(arrays, collective_id):
    low = jnp.bfloat16
    dma = pltpu.SemaphoreType.DMA
    shape = jax.ShapeDtypeStruct
    vmem = pltpu.VMEM
    in_specs = [VMEM_SPEC] * 4 + [ANY_SPEC] * 3 + [VMEM_SPEC] * 9
    outs = [
        (shape((2, 128, D), low), ANY_SPEC),
        (shape((2, 128, D), jnp.float32), VMEM_SPEC),
        (shape((4, 24, D), jnp.float32), VMEM_SPEC),
        (shape((16, 128), jnp.float32), VMEM_SPEC),
        (shape((24, D), jnp.float32), VMEM_SPEC),
        (shape((24, FF), jnp.float32), VMEM_SPEC),
        (shape((96, D), jnp.float32), VMEM_SPEC),
    ]
    return pl.pallas_call(
        backward_kernel,
        out_shape=[o[0] for o in outs],
        in_specs=in_specs,
        out_specs=[o[1] for o in outs],
        scratch_shapes=[
            vmem((8, 128, 192), low),
            vmem((1024, 576), low),
            vmem((3, 1024, 128), low),
            vmem((D, D), low),
            vmem((3, 1024, 64), jnp.float32),
            vmem((3, 1024, 64), jnp.float32),
            vmem((192, 2048), jnp.float32),
            vmem((8, 192), jnp.float32),
            vmem((D, D), jnp.float32),
            vmem((2, 2, 4, 2, 24, D), low),
            vmem((4, 2, 2, 24, D), low),
            vmem((4, 2, 2, 24, D), low),
            vmem((2, 2, 2, 24, D), low),
            vmem((4, 24, D), low),
            vmem((8, 128, D), low),
            vmem((2, 2, 128, D), low),
            vmem((2, 128, D), low),
            vmem((2, 128, D), low),
            vmem((2, 2, 128, D), low),
            vmem((32, 16, 128), low),
            dma((3, 2)),
            dma((8,)),
            dma((2,)),
            dma((6, 2)),
            dma((3, 4)),
            dma((3, 4)),
            dma((2, 3)),
            dma((4, 2)),
        ]
        + scatter_buffers(((16, 128),))
        + scatter_semaphores(1)
        + scatter_buffers(BIG_SHARDS)
        + scatter_semaphores(3),
        compiler_params=pltpu.CompilerParams(
            collective_id=collective_id, has_side_effects=True, vmem_limit_bytes=63 * 1024 * 1024
        ),
        name="backward_attention",
    )(*arrays)


def sequence_device(
    tokens,
    seg_ids,
    token_types,
    attn_in,
    attn_out,
    pos_kernel,
    ffn_in,
    ffn_out,
    head_vectors,
    norm_gains,
    norm_shifts,
    out_bias,
    ffn_bias,
    cotangent,
):
    x, c, z, y = place()
    low = jnp.bfloat16
    w_att_shard = jnp.concatenate(
        [attn_in.reshape(24, 3, 4, 192), pos_kernel.reshape(24, 1, 4, 192)], axis=1
    )
    w_att_shard = w_att_shard.transpose(2, 0, 1, 3).reshape(4, 24, D)
    small = jnp.concatenate(
        [
            head_vectors,
            norm_gains,
            norm_shifts,
            out_bias,
            ffn_bias.reshape(4, 24),
            jnp.zeros((1, 24), low),
        ],
        axis=0,
    )
    small = jnp.pad(small, ((0, 0), (0, 104)))
    (
        x_seq,
        cot,
        w_att,
        vectors,
        w_out,
        w_up,
        w_down,
        sides,
        table,
        keys,
        qkv,
        probs,
        attn_heads,
        attn,
        vec,
    ) = forward_attention(
        tokens, cotangent, seg_ids, token_types, w_att_shard, small, attn_out, ffn_in, ffn_out, 0
    )
    w_out = w_out.reshape(HD, D)
    w_up = w_up.reshape(D, FF)
    w_down = w_down.reshape(FF, D)
    cot = cot.reshape(256, D)
    rows = lax.dynamic_slice(x_seq.reshape(4, 2, 128, D), (2 * c, y, 0, 0), (2, 1, 128, D))
    rows_f = rows.reshape(256, D).astype(jnp.float32)
    vectors_f = vectors[:, :, :24].astype(jnp.float32)
    up_bias = vectors_f[:, 11:15, :].reshape(FF)
    vectors_f = vectors_f.transpose(1, 0, 2).reshape(16, D)
    gains_f, shifts_f, biases_f = (vectors_f[5:7], vectors_f[7:9], vectors_f[9:11])

    attn = attn.reshape(4, 256, 192).transpose(1, 0, 2).reshape(256, HD)
    branch = jnp.dot(attn, w_out, preferred_element_type=jnp.float32) + biases_f[0]
    first, normed_one, inv_one = layer_norm(rows_f + branch, gains_f[0], shifts_f[0])
    first_b = first.astype(low)
    pre_act = jnp.dot(first_b, w_up, preferred_element_type=jnp.float32) + up_bias
    hidden = gelu_tanh(pre_act).astype(low)
    second = jnp.dot(hidden, w_down, preferred_element_type=jnp.float32) + biases_f[1]
    result, normed_two, inv_two = layer_norm(first + second, gains_f[1], shifts_f[1])
    result = result.astype(low)

    grad_two = cot.astype(jnp.float32)
    gain_two = jnp.sum(grad_two * normed_two, axis=0)
    shift_two = jnp.sum(grad_two, axis=0)
    grad_h2 = norm_back(grad_two, normed_two, inv_two, gains_f[1])
    grad_second = grad_h2.astype(low)
    bias_two = jnp.sum(grad_second.astype(jnp.float32), axis=0)
    g_down = jnp.einsum("rf,rd->fd", hidden, grad_second, preferred_element_type=jnp.float32)
    grad_hidden = jnp.einsum("rd,fd->rf", grad_second, w_down, preferred_element_type=jnp.float32)
    grad_pre = jax.vjp(gelu_tanh, pre_act)[1](grad_hidden)[0].astype(low)
    g_upbias = jnp.sum(grad_pre.astype(jnp.float32), axis=0)
    g_up = jnp.einsum("rd,rf->df", first_b, grad_pre, preferred_element_type=jnp.float32)
    grad_first = grad_h2 + jnp.einsum(
        "rf,df->rd", grad_pre, w_up, preferred_element_type=jnp.float32
    )
    gain_one = jnp.sum(grad_first * normed_one, axis=0)
    shift_one = jnp.sum(grad_first, axis=0)
    grad_h1 = norm_back(grad_first, normed_one, inv_one, gains_f[0])
    grad_branch = grad_h1.astype(low)
    bias_one = jnp.sum(grad_branch.astype(jnp.float32), axis=0)
    g_out = jnp.einsum("rk,rd->kd", attn, grad_branch, preferred_element_type=jnp.float32)
    grad_attn = jnp.einsum(
        "rd,tkd->trk", grad_branch, w_out.reshape(4, 192, D), preferred_element_type=jnp.float32
    ).astype(low)

    g_small = jnp.concatenate(
        [
            jnp.zeros((5, D), jnp.float32),
            jnp.stack([gain_one, gain_two, shift_one, shift_two, bias_one, bias_two]),
        ],
        axis=0,
    )
    g_small = jnp.concatenate(
        [
            g_small.reshape(11, 32, 24).transpose(1, 0, 2),
            g_upbias.reshape(32, 4, 24),
            jnp.zeros((32, 1, 24), jnp.float32),
        ],
        axis=1,
    )
    g_small = jnp.pad(g_small, ((0, 0), (0, 0), (0, 104))).astype(low)
    out_rows, grad_rows, f_att, f_small, f_out, f_up, f_down = backward_attention(
        [
            grad_attn.reshape(4, 2, 128, 192),
            grad_h1.reshape(2, 128, D),
            result.reshape(2, 128, D),
            g_small,
            g_out.astype(low).reshape(32, 24, D),
            g_up.astype(low).reshape(32, 24, FF),
            g_down.astype(low).reshape(32, 96, D),
            qkv,
            sides,
            vec,
            table,
            keys,
            probs,
            attn_heads,
            x_seq,
            w_att,
        ],
        1,
    )
    f_att = f_att.reshape(4, 24, 4, 192).transpose(1, 2, 0, 3)
    f_small = f_small[:, :24]
    return (
        out_rows,
        grad_rows,
        f_att[:, :3].reshape(24, 3 * HD),
        f_out,
        f_att[:, 3].reshape(24, HD),
        f_up,
        f_down,
        f_small[0:5],
        f_small[5:7],
        f_small[7:9],
        f_small[9:11],
        f_small[11:15].reshape(96),
    )


def solution(mesh):
    placed = (
        P("dp", "fsdp", None),
        P("dp", None),
        P("dp", None),
        P(("dp", "fsdp"), None),
        P(("dp", "fsdp"), None),
        P(("dp", "fsdp"), None),
        P(("dp", "fsdp"), None),
        P(("dp", "fsdp"), None),
        P(None, ("dp", "fsdp")),
        P(None, ("dp", "fsdp")),
        P(None, ("dp", "fsdp")),
        P(None, ("dp", "fsdp")),
        P(("dp", "fsdp")),
        P("dp", "fsdp", None),
    )
    two_by_four = tuple(mesh.shape[name] for name in ("dp", "fsdp")) == (4, 8)
    return jax.shard_map(
        sequence_device if two_by_four else per_device,
        mesh=mesh,
        in_specs=placed,
        out_specs=(
            P("dp", "fsdp", None),
            P("dp", "fsdp", None),
            P(("dp", "fsdp"), None),
            P(("dp", "fsdp"), None),
            P(("dp", "fsdp"), None),
            P(("dp", "fsdp"), None),
            P(("dp", "fsdp"), None),
            P(None, ("dp", "fsdp")),
            P(None, ("dp", "fsdp")),
            P(None, ("dp", "fsdp")),
            P(None, ("dp", "fsdp")),
            P(("dp", "fsdp")),
        ),
        check_vma=False,
    )
```

```python
import functools

import jax
import jax.numpy as jnp
import numpy as np
from jax import lax
from jax.experimental import pallas as pl
from jax.experimental.pallas import tpu as pltpu
from jax.sharding import PartitionSpec as P

D = 768
H = 12
DH = 64
FF = 3072
HD = 768


EPSILON = 1e-06
HIGHEST_PREC = lax.Precision.HIGHEST


def gelu_tanh(values):
    return (
        0.5
        * values
        * (1.0 + jnp.tanh(0.7978845608028654 * (values + 0.044715 * values * values * values)))
    )


def angle_tables(positions, width):
    half_width = width // 2
    freq_index = jnp.arange(half_width, dtype=jnp.float32)
    inverse = jnp.power(10000.0, -freq_index / half_width)
    angles = positions[:, None] * inverse[None, :]
    return (jnp.sin(angles), jnp.cos(angles))


def layer_norm(values, gain, shift):
    center = values - jnp.mean(values, axis=-1, keepdims=True)
    inv_std = lax.rsqrt(jnp.mean(center * center, axis=-1, keepdims=True) + EPSILON)
    normed = center * inv_std
    return (normed * gain + shift, normed, inv_std)


def norm_back(grad_out, normed, inv_std, gain):
    grad_norm = grad_out * gain
    return inv_std * (
        grad_norm
        - jnp.mean(grad_norm, axis=-1, keepdims=True)
        - normed * jnp.mean(grad_norm * normed, axis=-1, keepdims=True)
    )


def fetch_forward(shards):
    return (
        lax.all_gather(shards[0], ("dp", "fsdp"), axis=0, tiled=True),
        lax.all_gather(shards[1], ("dp", "fsdp"), axis=0, tiled=True),
        lax.all_gather(shards[2], ("dp", "fsdp"), axis=0, tiled=True),
        lax.all_gather(shards[3], ("dp", "fsdp"), axis=0, tiled=True),
        lax.all_gather(shards[4], ("dp", "fsdp"), axis=0, tiled=True),
        lax.all_gather(shards[5], ("dp", "fsdp"), axis=1, tiled=True),
        lax.all_gather(shards[6], ("dp", "fsdp"), axis=1, tiled=True),
        lax.all_gather(shards[7], ("dp", "fsdp"), axis=1, tiled=True),
        lax.all_gather(shards[8], ("dp", "fsdp"), axis=1, tiled=True),
        lax.all_gather(shards[9], ("dp", "fsdp"), axis=0, tiled=True),
    )


def fetch_backward(shards):
    return (
        lax.all_gather(shards[0], ("dp", "fsdp"), axis=0, tiled=True),
        lax.all_gather(shards[1], ("dp", "fsdp"), axis=0, tiled=True),
        lax.all_gather(shards[2], ("dp", "fsdp"), axis=0, tiled=True),
        lax.all_gather(shards[3], ("dp", "fsdp"), axis=0, tiled=True),
        lax.all_gather(shards[4], ("dp", "fsdp"), axis=0, tiled=True),
        lax.all_gather(shards[5], ("dp", "fsdp"), axis=1, tiled=True),
        lax.all_gather(shards[6], ("dp", "fsdp"), axis=1, tiled=True),
        lax.all_gather(shards[7], ("dp", "fsdp"), axis=1, tiled=True),
        lax.all_gather(shards[8], ("dp", "fsdp"), axis=1, tiled=True),
        lax.all_gather(shards[9], ("dp", "fsdp"), axis=0, tiled=True),
    )


def score_block(q_content, q_rel, type_terms, keys3, k_rel, same_type):
    content = jnp.einsum("rhe,jhe->rhj", q_content, keys3, preferred_element_type=jnp.float32)
    position = jnp.einsum("rhc,jc->rhj", q_rel, k_rel, preferred_element_type=jnp.float32)
    typed = jnp.where(same_type, type_terms[:, :, 1:2], type_terms[:, :, 0:1])
    return DH ** (-0.5) * (content + position + typed)


def relative_queries(q_pos, w_pos, positions):
    proj_pos = jnp.einsum(
        "rhe,che->rhc", q_pos, w_pos.reshape(D, H, DH), preferred_element_type=jnp.float32
    )
    sines, cosines = angle_tables(positions, D)
    sin_q = sines[:, None, :]
    cos_q = cosines[:, None, :]
    half_width = D // 2
    pos_sin = proj_pos[..., :half_width]
    pos_cos = proj_pos[..., half_width:]
    q_rel = jnp.concatenate(
        [pos_sin * sin_q + pos_cos * cos_q, pos_cos * sin_q - pos_sin * cos_q], axis=-1
    ).astype(jnp.bfloat16)
    return (q_rel, sin_q, cos_q)


def forward_micro(weights, x_rows, seg_row, type_row, start, k_rel):
    w_in, w_out, w_pos, w_up, w_down, head_vec, gains, shifts, biases, up_bias = weights
    row_count = x_rows.shape[0]
    head_f = head_vec.astype(jnp.float32)
    gains_f = gains.astype(jnp.float32)
    shifts_f = shifts.astype(jnp.float32)
    biases_f = biases.astype(jnp.float32)
    proj = jnp.dot(x_rows, w_in, preferred_element_type=jnp.float32)
    query = proj[:, :HD]
    key_local = proj[:, HD : 2 * HD].astype(jnp.bfloat16)
    value_local = proj[:, 2 * HD :].astype(jnp.bfloat16)
    keys, values = (
        lax.all_gather(key_local, "fsdp", axis=0, tiled=True),
        lax.all_gather(value_local, "fsdp", axis=0, tiled=True),
    )
    keys3 = keys.reshape(keys.shape[0], H, DH)
    values3 = values.reshape(values.shape[0], H, DH)
    q_content = (query + head_f[0]).astype(jnp.bfloat16).reshape(row_count, H, DH)
    q_pos = (query + head_f[1]).astype(jnp.bfloat16).reshape(row_count, H, DH)
    q_type = (query + head_f[2]).reshape(row_count, H, DH)
    type_table = head_f[3:5].reshape(2, H, DH)
    type_terms = jnp.einsum("rhe,the->rht", q_type, type_table, precision=HIGHEST_PREC)
    positions = (start + jnp.arange(row_count, dtype=jnp.int32)).astype(jnp.float32)
    q_rel, sin_q, cos_q = relative_queries(q_pos, w_pos, positions)
    query_seg = lax.dynamic_slice_in_dim(seg_row, start, row_count)
    query_kind = lax.dynamic_slice_in_dim(type_row, start, row_count)
    allowed = (query_seg[:, None] == seg_row[None, :])[:, None, :]
    same_type = (query_kind[:, None] == type_row[None, :])[:, None, :]
    scores = score_block(q_content, q_rel, type_terms, keys3, k_rel, same_type)
    masked = jnp.where(allowed, scores, -1e30)
    top = jnp.max(masked, axis=-1, keepdims=True)
    expo = jnp.where(allowed, jnp.exp(masked - top), 0.0)
    total = jnp.sum(expo, axis=-1, keepdims=True)
    probs_b = (expo / total).astype(jnp.bfloat16)
    log_total = top + jnp.log(total)
    attn = (
        jnp.einsum("rhj,jhe->rhe", probs_b, values3, preferred_element_type=jnp.float32)
        .astype(jnp.bfloat16)
        .reshape(row_count, HD)
    )
    branch = jnp.dot(attn, w_out, preferred_element_type=jnp.float32) + biases_f[0]
    first, normed_one, inv_one = layer_norm(
        x_rows.astype(jnp.float32) + branch, gains_f[0], shifts_f[0]
    )
    first_b = first.astype(jnp.bfloat16)
    pre_act = jnp.dot(first_b, w_up, preferred_element_type=jnp.float32) + up_bias.astype(
        jnp.float32
    )
    hidden = gelu_tanh(pre_act).astype(jnp.bfloat16)
    second = jnp.dot(hidden, w_down, preferred_element_type=jnp.float32) + biases_f[1]
    result, normed_two, inv_two = layer_norm(first + second, gains_f[1], shifts_f[1])
    kept = (
        x_rows,
        q_content,
        q_pos,
        q_rel,
        q_type,
        type_terms,
        sin_q,
        cos_q,
        keys3,
        values3,
        allowed,
        same_type,
        log_total,
        attn,
        normed_one,
        inv_one,
        first_b,
        pre_act,
        hidden,
        normed_two,
        inv_two,
    )
    return (result.astype(jnp.bfloat16), kept)


def backward_micro(weights, kept, grad_rows, k_rel, totals):
    w_in, w_out, w_pos, w_up, w_down, head_vec, gains, shifts, biases, up_bias = weights
    (
        x_rows,
        q_content,
        q_pos,
        q_rel,
        q_type,
        type_terms,
        sin_q,
        cos_q,
        keys3,
        values3,
        allowed,
        same_type,
        log_total,
        attn,
        normed_one,
        inv_one,
        first_b,
        pre_act,
        hidden,
        normed_two,
        inv_two,
    ) = kept
    g_in, g_out, g_pos, g_up, g_down, g_head, g_gains, g_shifts, g_bias, g_upbias = totals
    row_count = x_rows.shape[0]
    head_f = head_vec.astype(jnp.float32)
    gains_f = gains.astype(jnp.float32)
    grad_two = grad_rows.astype(jnp.float32)
    gain_two = jnp.sum(grad_two * normed_two, axis=0)
    shift_two = jnp.sum(grad_two, axis=0)
    grad_h2 = norm_back(grad_two, normed_two, inv_two, gains_f[1])
    grad_second = grad_h2.astype(jnp.bfloat16)
    bias_two = jnp.sum(grad_second.astype(jnp.float32), axis=0)
    g_down = g_down + jnp.einsum(
        "rf,rd->fd", hidden, grad_second, preferred_element_type=jnp.float32
    )
    grad_hidden = jnp.einsum("rd,fd->rf", grad_second, w_down, preferred_element_type=jnp.float32)
    act_pull = jax.vjp(gelu_tanh, pre_act)[1]
    grad_pre = act_pull(grad_hidden)[0].astype(jnp.bfloat16)
    g_upbias = g_upbias + jnp.sum(grad_pre.astype(jnp.float32), axis=0)
    g_up = g_up + jnp.einsum("rd,rf->df", first_b, grad_pre, preferred_element_type=jnp.float32)
    grad_first = grad_h2 + jnp.einsum(
        "rf,df->rd", grad_pre, w_up, preferred_element_type=jnp.float32
    )
    gain_one = jnp.sum(grad_first * normed_one, axis=0)
    shift_one = jnp.sum(grad_first, axis=0)
    grad_h1 = norm_back(grad_first, normed_one, inv_one, gains_f[0])
    grad_branch = grad_h1.astype(jnp.bfloat16)
    bias_one = jnp.sum(grad_branch.astype(jnp.float32), axis=0)
    g_out = g_out + jnp.einsum("rk,rd->kd", attn, grad_branch, preferred_element_type=jnp.float32)
    grad_attn = (
        jnp.einsum("rd,kd->rk", grad_branch, w_out, preferred_element_type=jnp.float32)
        .astype(jnp.bfloat16)
        .reshape(row_count, H, DH)
    )
    scores = score_block(q_content, q_rel, type_terms, keys3, k_rel, same_type)
    probs = jnp.where(allowed, jnp.exp(scores - log_total), 0.0)
    grad_probs = jnp.einsum("rhe,jhe->rhj", grad_attn, values3, preferred_element_type=jnp.float32)
    delta = jnp.sum(probs * grad_probs, axis=-1, keepdims=True)
    grad_scores = (probs * (grad_probs - delta)).astype(jnp.bfloat16) * DH ** (-0.5)
    grad_content = jnp.einsum(
        "rhj,jhe->rhe", grad_scores, keys3, preferred_element_type=jnp.float32
    )
    grad_rel = jnp.einsum("rhj,jc->rhc", grad_scores, k_rel, preferred_element_type=jnp.float32)
    probs_b = probs.astype(jnp.bfloat16)
    value_part = jnp.einsum("rhj,rhe->jhe", probs_b, grad_attn, preferred_element_type=jnp.float32)
    key_part = jnp.einsum(
        "rhj,rhe->jhe", grad_scores, q_content, preferred_element_type=jnp.float32
    )
    key_full, value_full = (
        lax.psum_scatter(
            key_part.reshape(key_part.shape[0], HD).astype(jnp.bfloat16),
            "fsdp",
            scatter_dimension=0,
            tiled=True,
        ).astype(jnp.float32),
        lax.psum_scatter(
            value_part.reshape(value_part.shape[0], HD).astype(jnp.bfloat16),
            "fsdp",
            scatter_dimension=0,
            tiled=True,
        ).astype(jnp.float32),
    )
    scores_f = grad_scores.astype(jnp.float32)
    same_f = same_type.astype(jnp.float32)
    grad_same = jnp.sum(scores_f * same_f, axis=-1)
    grad_diff = jnp.sum(scores_f * (1.0 - same_f), axis=-1)
    grad_terms = jnp.stack([grad_diff, grad_same], axis=-1)
    type_table = head_f[3:5].reshape(2, H, DH)
    grad_qtype = jnp.einsum("rht,the->rhe", grad_terms, type_table, precision=HIGHEST_PREC)
    grad_table = jnp.einsum("rht,rhe->the", grad_terms, q_type, precision=HIGHEST_PREC)
    half_width = D // 2
    rel_first = grad_rel[..., :half_width]
    rel_second = grad_rel[..., half_width:]
    grad_proj = jnp.concatenate(
        [rel_first * sin_q - rel_second * cos_q, rel_first * cos_q + rel_second * sin_q], axis=-1
    ).astype(jnp.bfloat16)
    grad_qpos = jnp.einsum(
        "rhc,che->rhe", grad_proj, w_pos.reshape(D, H, DH), preferred_element_type=jnp.float32
    )
    g_pos = g_pos + jnp.einsum(
        "rhc,rhe->che", grad_proj, q_pos, preferred_element_type=jnp.float32
    ).reshape(D, HD)
    head_terms = jnp.stack(
        [
            jnp.sum(grad_content.reshape(row_count, HD), axis=0),
            jnp.sum(grad_qpos.reshape(row_count, HD), axis=0),
            jnp.sum(grad_qtype.reshape(row_count, HD), axis=0),
            grad_table[0].reshape(HD),
            grad_table[1].reshape(HD),
        ]
    )
    g_head = g_head + head_terms
    grad_query = (grad_content + grad_qpos + grad_qtype).reshape(row_count, HD).astype(jnp.bfloat16)
    grad_proj_in = jnp.concatenate(
        [grad_query, key_full.astype(jnp.bfloat16), value_full.astype(jnp.bfloat16)], axis=1
    )
    g_in = g_in + jnp.einsum("rd,rk->dk", x_rows, grad_proj_in, preferred_element_type=jnp.float32)
    grad_x = grad_h1 + jnp.einsum(
        "rk,dk->rd", grad_proj_in, w_in, preferred_element_type=jnp.float32
    )
    g_gains = g_gains + jnp.stack([gain_one, gain_two])
    g_shifts = g_shifts + jnp.stack([shift_one, shift_two])
    g_bias = g_bias + jnp.stack([bias_one, bias_two])
    return (grad_x, (g_in, g_out, g_pos, g_up, g_down, g_head, g_gains, g_shifts, g_bias, g_upbias))


def per_device(
    tokens,
    seg_ids,
    token_types,
    attn_in,
    attn_out,
    pos_kernel,
    ffn_in,
    ffn_out,
    head_vectors,
    norm_gains,
    norm_shifts,
    out_bias,
    ffn_bias,
    cotangent,
):
    shards = (
        attn_in,
        attn_out,
        pos_kernel,
        ffn_in,
        ffn_out,
        head_vectors,
        norm_gains,
        norm_shifts,
        out_bias,
        ffn_bias,
    )
    micro_count = tokens.shape[0]
    row_count = tokens.shape[1]
    start = lax.axis_index("fsdp") * row_count
    all_positions = jnp.arange(seg_ids.shape[1], dtype=jnp.float32)
    key_sin, key_cos = angle_tables(all_positions, D)
    k_rel = jnp.concatenate([key_cos, key_sin], axis=-1).astype(jnp.bfloat16)
    totals = (
        jnp.zeros((D, 3 * HD), jnp.float32),
        jnp.zeros((HD, D), jnp.float32),
        jnp.zeros((D, HD), jnp.float32),
        jnp.zeros((D, FF), jnp.float32),
        jnp.zeros((FF, D), jnp.float32),
        jnp.zeros((5, HD), jnp.float32),
        jnp.zeros((2, D), jnp.float32),
        jnp.zeros((2, D), jnp.float32),
        jnp.zeros((2, D), jnp.float32),
        jnp.zeros((FF,), jnp.float32),
    )
    results = []
    input_grads = []
    for micro_step in range(micro_count):
        forward_weights = fetch_forward(shards)
        result, kept = forward_micro(
            forward_weights,
            tokens[micro_step],
            seg_ids[micro_step],
            token_types[micro_step],
            start,
            k_rel,
        )
        backward_weights = fetch_backward(shards)
        grad_x, totals = backward_micro(
            backward_weights, kept, cotangent[micro_step], k_rel, totals
        )
        results.append(result)
        input_grads.append(grad_x)
    final = (
        lax.psum_scatter(totals[0], ("dp", "fsdp"), scatter_dimension=0, tiled=True),
        lax.psum_scatter(totals[1], ("dp", "fsdp"), scatter_dimension=0, tiled=True),
        lax.psum_scatter(totals[2], ("dp", "fsdp"), scatter_dimension=0, tiled=True),
        lax.psum_scatter(totals[3], ("dp", "fsdp"), scatter_dimension=0, tiled=True),
        lax.psum_scatter(totals[4], ("dp", "fsdp"), scatter_dimension=0, tiled=True),
        lax.psum_scatter(totals[5], ("dp", "fsdp"), scatter_dimension=1, tiled=True),
        lax.psum_scatter(totals[6], ("dp", "fsdp"), scatter_dimension=1, tiled=True),
        lax.psum_scatter(totals[7], ("dp", "fsdp"), scatter_dimension=1, tiled=True),
        lax.psum_scatter(totals[8], ("dp", "fsdp"), scatter_dimension=1, tiled=True),
        lax.psum_scatter(totals[9], ("dp", "fsdp"), scatter_dimension=0, tiled=True),
    )
    return (
        jnp.stack(results),
        jnp.stack(input_grads),
        final[0],
        final[1],
        final[2],
        final[3],
        final[4],
        final[5],
        final[6],
        final[7],
        final[8],
        final[9],
    )


MESH_ID = pl.DeviceIdType.MESH
Z_OFFSETS = (0, -1, 1, -2, 2, -3, 3)
ANY_SPEC = pl.BlockSpec(memory_space=pl.ANY)
VMEM_SPEC = pl.BlockSpec(memory_space=pltpu.VMEM)


def place():
    dp = lax.axis_index("dp")
    fs = lax.axis_index("fsdp")
    return (dp // 2, dp % 2, fs // 2, fs % 2)


def device(x, c, z, y):
    return (x * 2 + c, z * 2 + y)


def guarded(cond, action):
    if cond is None:
        action()
    else:
        pl.when(cond)(action)


def greet(peers):
    barrier = pltpu.get_barrier_semaphore()
    for cond, peer in peers:
        guarded(
            cond,
            lambda peer=peer: pl.semaphore_signal(
                barrier, inc=1, device_id=peer, device_id_type=MESH_ID
            ),
        )
    count = 0
    for cond, _ in peers:
        count = count + (1 if cond is None else cond.astype(jnp.int32))
    pl.semaphore_wait(barrier, count)


def remote(src, dst, send, recv, to):
    return pltpu.make_async_remote_copy(
        src_ref=src, dst_ref=dst, send_sem=send, recv_sem=recv, device_id=to, device_id_type=MESH_ID
    )


def half_members(kinds, half):
    if half == 0:
        return range(len(kinds))
    return [a for a, kind in enumerate(kinds) if kind in ("split", half)]


def swap_peers():
    x, c, z, y = place()
    peers = []
    for m in range(2):
        away = jnp.logical_or(z // 2 != c, z % 2 != m)
        peers.append((away, device(x, z // 2, 2 * c + m, y)))
    return peers


def swap_copies(src, dst, send, recv, local):
    x, c, z, y = place()

    def both(m):
        peer = device(x, z // 2, 2 * c + m, y)
        out = remote(src.at[m], dst.at[z % 2], send.at[m], recv.at[z % 2], peer)
        into = remote(src.at[m], dst.at[m], send.at[m], recv.at[m], peer)
        here = pltpu.make_async_copy(src.at[m], dst.at[m], local.at[m])
        away = jnp.logical_or(z // 2 != c, z % 2 != m)
        return (out, into, here, away)

    def start():
        for m in range(2):
            out, _, here, away = both(m)
            pl.when(away)(out.start)
            pl.when(jnp.logical_not(away))(here.start)

    def wait():
        for m in range(2):
            out, into, here, away = both(m)
            pl.when(away)(into.wait_recv)
            pl.when(away)(out.wait_send)
            pl.when(jnp.logical_not(away))(here.wait)

    return (start, wait)


ROWS = 256
MASKED = -1e30
NT = (((1,), (1,)), ((), ()))
TN = (((0,), (0,)), ((), ()))


def mm(a, b, dims=(((1,), (0,)), ((), ()))):
    return lax.dot_general(a, b, dims, preferred_element_type=jnp.float32)


def angle_constants():
    half = D // 2
    inverse = 10000.0 ** (-np.arange(half, dtype=np.float64) / half)
    inverse = inverse.astype(np.float32).astype(np.float64)
    coarse = inverse[:, None] * (1023.0 - 128.0 * np.arange(16)[None, :])
    fine = inverse[:, None] * np.arange(128.0)[None, :]
    coarse_table = np.concatenate([np.sin(coarse), np.cos(coarse)], axis=0).astype(np.float32)
    fine_table = np.concatenate([np.sin(fine), np.cos(fine)], axis=0).astype(np.float32)
    return (coarse_table, fine_table)


def query_parts(q, vec, h, kind):
    q = q.astype(jnp.float32)
    lanes = slice(h * 64, h * 64 + 64)
    content = (q + vec[0:1, lanes]).astype(jnp.bfloat16).astype(jnp.float32) * DH ** (-0.5)
    position = (q + vec[1:2, lanes]).astype(jnp.bfloat16) * jnp.bfloat16(DH ** (-0.5))
    typed = q + vec[2:3, lanes]
    other = jnp.sum(typed * vec[3:4, lanes], axis=1, keepdims=True) * DH ** (-0.5)
    same = jnp.sum(typed * vec[4:5, lanes], axis=1, keepdims=True) * DH ** (-0.5)
    to_zero = jnp.where(kind > 0.5, other, same)
    to_one = jnp.where(kind > 0.5, same, other)
    return (content, position, typed, to_zero, to_one)


def wide_query(content, to_zero, to_one, side):
    rows = content.shape[0]
    lane = lax.broadcasted_iota(jnp.int32, (rows, 64), 1)

    def split(value):
        high = value.astype(jnp.bfloat16).astype(jnp.float32)
        return (high, value - high)

    zero_high, zero_low = split(to_zero)
    one_high, one_low = split(to_one)
    extra = jnp.where(
        lane == 0,
        zero_high,
        jnp.where(
            lane == 1, one_high, jnp.where(lane == 2, zero_low, jnp.where(lane == 3, one_low, side))
        ),
    )
    return jnp.concatenate([content, extra], axis=1).astype(jnp.bfloat16)


def level_of(z, off):
    k = z + off
    if off == 0:
        return (k, None)
    return (jnp.clip(k, 0, 3), k >= 0 if off < 0 else k <= 3)


def both(cond, other):
    return other if cond is None else jnp.logical_and(cond, other)


def wide(ref):
    return ref[...].astype(jnp.float32)


GATHER_ORDER = (
    ("column", 0),
    ("column", -1),
    ("column", 1),
    ("beside", 0),
    ("column", -2),
    ("column", 2),
    ("beside", -1),
    ("beside", 1),
    ("across", 0),
    ("column", -3),
    ("column", 3),
    ("beside", -2),
    ("beside", 2),
    ("across", -1),
    ("across", 1),
    ("beside", -3),
    ("beside", 3),
    ("across", -2),
    ("across", 2),
    ("across", -3),
    ("across", 3),
)


def gather_plan(kinds, srcs, dsts, send_sem, recv_sem, local_sem):
    n = len(kinds)
    x, c, z, y = place()
    below, above = (z > 0, z < 3)
    nx, ny, partner = (device(1 - x, c, z, y), device(x, c, z, 1 - y), device(x, 1 - c, z, y))
    up, down = (
        device(x, c, jnp.minimum(z + 1, 3), y),
        device(x, c, jnp.maximum(z - 1, 0), y),
    )

    def slot(a, core, xx, yy, k):
        return dsts[a].at[(xx * 2 + core) * 8 + k * 2 + yy]

    def copies(kind, k, owner, half, to, core, own=False):
        out = []
        for a in range(n):
            if half and kinds[a] != half:
                continue
            there = slot(a, core, owner[0], owner[1], k)
            out.append(
                remote(
                    srcs[a] if own else there,
                    there,
                    send_sem.at[kind, a, k],
                    recv_sem.at[kind, a, k],
                    to,
                )
            )
        return out

    started = []

    def send(cond, kind, k, owner, half, to, own=False):
        def go():
            for copy in copies(kind, k, owner, half, to, c, own):
                copy.start()

        def finish():
            for copy in copies(kind, k, owner, half, to, c, own):
                copy.wait_send()

        guarded(cond, go)
        started.append((cond, finish))

    def recv(cond, kind, k, owner, half, core):
        def go():
            for copy in copies(kind, k, owner, half, partner, core):
                copy.wait_recv()

        guarded(cond, go)

    k_up, k_down, k_x, k_y, k_h1, k_h2, p_own, p_x, p_y, p_opp = range(10)
    me, at_x, at_y, opposite = ((x, y), (1 - x, y), (x, 1 - y), (1 - x, 1 - y))

    def act(name, off):
        k, ok = level_of(z, off)
        own = off == 0
        if name == "column":
            if own:
                for a in range(n):
                    pltpu.make_async_copy(srcs[a], slot(a, c, x, y, z), local_sem.at[a]).start()
            if off < 0:
                recv(ok, k_up, k, me, 0, c)
            if off > 0:
                recv(ok, k_down, k, me, 0, c)
            if off <= 0:
                send(both(ok, above), k_up, k, me, 0, up, own)
            if off >= 0:
                send(both(ok, below), k_down, k, me, 0, down, own)
            send(ok, k_x, k, me, 0, nx, own)
            send(ok, k_y, k, me, 0, ny, own)
            send(ok, p_own, k, me, 0, partner, own)
        elif name == "beside":
            recv(ok, k_x, k, at_x, 0, c)
            send(ok, k_h1, k, at_x, 1, ny)
            send(ok, p_x, k, at_x, 0, partner)
            recv(ok, k_y, k, at_y, 0, c)
            send(ok, k_h2, k, at_y, 2, nx)
            send(ok, p_y, k, at_y, 0, partner)
        else:
            recv(ok, k_h1, k, opposite, 1, c)
            recv(ok, k_h2, k, opposite, 2, c)
            send(ok, p_opp, k, opposite, 0, partner)

    def arrive():
        for k in range(4):
            for kind, owner in ((p_own, me), (p_x, at_x), (p_y, at_y), (p_opp, opposite)):
                recv(None, kind, k, owner, 0, 1 - c)
        for a in range(n):
            pltpu.make_async_copy(srcs[a], slot(a, c, x, y, z), local_sem.at[a]).wait()

    def leave():
        for cond, finish in started:
            guarded(cond, finish)

    return (act, arrive, leave)


def forward_kernel(
    tokens,
    cot,
    seg,
    kinds_row,
    in_shard,
    pos_shard,
    head_shard,
    gain_shard,
    shift_shard,
    bias_shard,
    ffn_bias_shard,
    out_shard,
    up_shard,
    down_shard,
    coarse,
    fine,
    x_seq,
    cot_own,
    w_att,
    w_out,
    w_up,
    w_down,
    sides,
    table,
    keys,
    qkv,
    probs,
    attn_heads,
    rows,
    attn_rows,
    params,
    up_bias,
    vec,
    w_att_shard,
    small_shard,
    small,
    attn,
    seg_other,
    kind_other,
    wide_key,
    block_sem,
    swap_sem,
    label_sem,
    quad_sem,
    att_send,
    att_recv,
    small_send,
    small_recv,
    small_local,
    big_send,
    big_recv,
    big_local,
    trade_send,
    trade_recv,
    trade_local,
):
    x, c, z, y = place()
    group = y * 2 + c
    below, above = (z > 0, z < 3)
    nx, ny, partner = (device(1 - x, c, z, y), device(x, c, z, 1 - y), device(x, 1 - c, z, y))
    cross = device(x, 1 - c, z, 1 - y)
    up, down = (
        device(x, c, jnp.minimum(z + 1, 3), y),
        device(x, c, jnp.maximum(z - 1, 0), y),
    )
    wide_in = wide(in_shard)
    wide_pos = wide(pos_shard)
    for g in range(4):
        lanes = [wide_in[:, s * HD + g * 192 : s * HD + g * 192 + 192] for s in range(3)]
        lanes.append(wide_pos[:, g * 192 : g * 192 + 192])
        w_att_shard[g] = jnp.concatenate(lanes, axis=1).astype(jnp.bfloat16)
    narrow = [wide(ref) for ref in (head_shard, gain_shard, shift_shard, bias_shard)]
    narrow = jnp.concatenate(narrow + [jnp.zeros((5, 24), jnp.float32)], axis=0)
    narrow = jnp.concatenate([narrow, jnp.zeros((16, 104), jnp.float32)], axis=1)
    long = jnp.concatenate([wide(ffn_bias_shard), jnp.zeros((1, 32), jnp.float32)], axis=1)
    row = lax.broadcasted_iota(jnp.int32, (16, 128), 0)
    small_shard[...] = jnp.where(row == 11, jnp.broadcast_to(long, (16, 128)), narrow).astype(
        jnp.bfloat16
    )
    peers = [(None, nx), (None, ny), (None, partner), (None, cross), (below, down), (above, up)]
    greet(peers + swap_peers())

    def block_of(core, k, yy):
        return (2 * core + k) * 2 + yy

    def block_copy(kind, b, to):
        return remote(x_seq.at[b], x_seq.at[b], block_sem.at[kind, b], block_sem.at[3, b], to)

    def first_hop(m):
        peer = device(x, z // 2, 2 * c + m, y)
        away = jnp.logical_or(z // 2 != c, z % 2 != m)
        out = remote(
            tokens.at[m], x_seq.at[z * 2 + y], swap_sem.at[0, m], block_sem.at[3, z * 2 + y], peer
        )
        here = pltpu.make_async_copy(tokens.at[m], x_seq.at[z * 2 + y], swap_sem.at[1, m])
        return (away, out, here)

    for m in range(2):
        away, out, here = first_hop(m)
        pl.when(away)(out.start)
        pl.when(jnp.logical_not(away))(here.start)
    label_out = [
        remote(seg, seg_other, label_sem.at[0], label_sem.at[1], partner),
        remote(kinds_row, kind_other, label_sem.at[2], label_sem.at[3], partner),
    ]
    for copy in label_out:
        copy.start()

    quad = ((y, 1 - c), (1 - y, c), (1 - y, 1 - c))

    def piece(i, yy, core, dst_y, dst_c, to):
        return remote(
            w_att_shard.at[dst_y * 2 + dst_c],
            w_att.at[x, core, z, yy],
            quad_sem.at[0, i],
            quad_sem.at[1, i],
            to,
        )

    own_piece = pltpu.make_async_copy(w_att_shard.at[group], w_att.at[x, c, z, y], quad_sem.at[2, 0])
    own_piece.start()
    for i, (yy, core) in enumerate(quad):
        piece(i, y, c, yy, core, device(x, core, z, yy)).start()

    small_act, small_arrive, small_leave = gather_plan(
        (1,), [small_shard], [small], small_send, small_recv, small_local
    )
    big_act, big_arrive, big_leave = gather_plan(
        (2, 1, 2), [out_shard, up_shard, down_shard], [w_out, w_up, w_down], big_send, big_recv, big_local
    )
    small_act("column", 0)

    def level_copy(kind, xx, k, to):
        part = w_att.at[xx, :, k]
        return remote(part, part, att_send.at[kind, k], att_recv.at[kind, k], to)

    att_started = []

    def att_send_to(cond, kind, k, to):
        copy = level_copy(kind, x, k, to)
        guarded(cond, copy.start)
        att_started.append((cond, copy))

    def att_column(off):
        k, ok = level_of(z, off)
        if off == 0:
            own_piece.wait()
            for i, (yy, core) in enumerate(quad):
                piece(i, yy, core, yy, core, partner).wait_recv()
        if off < 0:
            guarded(ok, level_copy(0, x, k, up).wait_recv)
        if off > 0:
            guarded(ok, level_copy(1, x, k, down).wait_recv)
        if off <= 0:
            att_send_to(both(ok, above), 0, k, up)
        if off >= 0:
            att_send_to(both(ok, below), 1, k, down)
        att_send_to(ok, 2, k, nx)

    att_column(0)

    half = D // 2
    fine_sin = fine[:half, :]
    fine_cos = fine[half:, :]

    def angles(a):
        big_sin = coarse[:half, a : a + 1]
        big_cos = coarse[half:, a : a + 1]
        sines = big_sin * fine_cos - big_cos * fine_sin
        cosines = big_cos * fine_cos + big_sin * fine_sin
        table[:half, a * 128 : (a + 1) * 128] = sines.astype(jnp.bfloat16)
        table[half:, a * 128 : (a + 1) * 128] = cosines.astype(jnp.bfloat16)

    for a in range(8):
        angles(a)

    def got(m):
        b = block_of(c, m, y)
        own = jnp.logical_and(z // 2 == c, z % 2 == m)
        source = block_copy(0, b, partner)
        here = pltpu.make_async_copy(tokens.at[m], x_seq.at[b], swap_sem.at[1, m])
        pl.when(jnp.logical_not(own))(source.wait_recv)
        pl.when(own)(here.wait)
        block_copy(1, b, ny).start()
        block_copy(0, b, partner).start()

    got(0)
    got(1)
    att_column(-1)
    att_column(1)
    small_act("column", -1)
    small_act("column", 1)
    small_act("beside", 0)
    for a in range(8, 12):
        angles(a)
    for m in range(2):
        b = block_of(c, m, 1 - y)
        block_copy(1, b, ny).wait_recv()
        block_copy(2, b, partner).start()
    att_column(-2)
    att_column(2)
    for name, off in GATHER_ORDER[4:9]:
        small_act(name, off)
    att_column(-3)
    att_column(3)
    big_act("column", 0)
    cot_start, cot_wait = swap_copies(
        cot, cot_own, swap_sem.at[2], swap_sem.at[3], swap_sem.at[4]
    )
    cot_start()
    for a in range(12, 16):
        angles(a)
    for name, off in GATHER_ORDER[9:]:
        small_act(name, off)

    for copy in label_out:
        copy.wait()
    mine = (c == z // 2).astype(jnp.int32)
    odd = z % 2

    def row_of(here, there):
        own = here[0:1, :] * (1 - odd) + here[1:2, :] * odd
        other = there[0:1, :] * (1 - odd) + there[1:2, :] * odd
        return own * mine + other * (1 - mine)

    seg_row = row_of(seg[...], seg_other[...])
    kind_row = row_of(kinds_row[...], kind_other[...])
    line = lax.broadcasted_iota(jnp.int32, (128, 1024), 0)
    seg_all = jnp.broadcast_to(seg_row, (128, 1024))
    kind_all = jnp.broadcast_to(kind_row, (128, 1024)).astype(jnp.float32)
    side_t = jnp.where(line < 4, kind_all, jnp.where(seg_all == line - 4, 1.0, 0.0))
    key_t = jnp.where(
        line < 68,
        jnp.where(line % 2 == 0, 1.0 - kind_all, kind_all),
        jnp.where(line < 76, jnp.where(seg_all == line - 68, 0.0, MASKED), 0.0),
    )
    side_t = jnp.where(line < 64, side_t, key_t)
    sides[...] = jnp.transpose(side_t).astype(jnp.bfloat16)

    big_act("column", -1)
    big_act("column", 1)
    big_act("beside", 0)
    small_arrive()
    heads = jnp.concatenate(
        [small[group * 8 + i][:, :24].astype(jnp.float32) for i in range(8)], axis=1
    )
    vec[...] = heads[0:8, :]
    params[...] = jnp.concatenate([wide(small.at[i])[:, :24] for i in range(32)], axis=1)
    up_bias[...] = jnp.concatenate([wide(small.at[i])[11:12, :96] for i in range(32)], axis=1)

    for k in range(4):
        level_copy(2, 1 - x, k, nx).wait_recv()
    weights = w_att[...].astype(jnp.float32).reshape(D, D).astype(jnp.bfloat16)
    keys[...] = mm(weights[:, 512:768], table[...], TN)[64:256, :].astype(jnp.bfloat16)

    for k in range(2):
        for yy in range(2):
            b = (2 * (1 - c) + k) * 2 + yy
            kind = jnp.where(yy == y, 0, 2)
            remote(x_seq.at[b], x_seq.at[b], block_sem.at[0, b], block_sem.at[3, b], partner).wait_recv()

    @pl.loop(0, 4)
    def _(step):
        both_rows = x_seq[pl.ds(step * 2, 2)].reshape(256, D)
        qkv[pl.ds(pl.multiple_of(step * 256, 256), 256), :] = mm(both_rows, weights)[:, :576].astype(
            jnp.bfloat16
        )

    for h in range(3):
        wide_key[h] = jnp.concatenate(
            [qkv[:, 192 + h * 64 : 256 + h * 64], sides[:, 64:128]], axis=1
        )
    big_act("column", -2)
    big_act("column", 2)
    big_act("beside", -1)
    big_act("beside", 1)
    big_act("across", 0)
    later = (
        (("column", -3), ("column", 3), ("beside", -2), ("beside", 2)),
        (("across", -1), ("across", 1)),
        (("beside", -3), ("beside", 3), ("across", -2), ("across", 2)),
        (("across", -3), ("across", 3)),
    )

    def send_rows(zb, start):
        core = zb // 2
        for yy in range(2):
            b = zb * 2 + yy
            src = attn_heads.at[pl.ds(pl.multiple_of(b * 128, 128), 128)]
            dst = attn.at[group, zb % 2]
            away = jnp.logical_or(core != c, yy != y)
            out = remote(
                src, dst, trade_send.at[b], trade_recv.at[group, zb % 2], device(x, core, z, yy)
            )
            here = pltpu.make_async_copy(src, dst, trade_local.at[zb % 2])
            if start:
                pl.when(away)(out.start)
                pl.when(jnp.logical_not(away))(here.start)
            else:
                pl.when(away)(out.wait_send)
                pl.when(jnp.logical_not(away))(here.wait)

    width = 1024 + ROWS

    @pl.loop(0, 4)
    def _(step):
        start = pl.multiple_of(step * ROWS, ROWS)
        block = qkv[pl.ds(start, ROWS), 0:192]
        side = sides[pl.ds(start, ROWS), 0:64].astype(jnp.float32)
        kind = side[:, 0:1]
        from_n = pl.multiple_of(1024 - ROWS - start, 128)
        outs = []
        values = vec[...]
        for h in range(3):
            content, position, _, to_zero, to_one = query_parts(
                block[:, h * 64 : h * 64 + 64], values, h, kind
            )
            query = wide_query(content, to_zero, to_one, side)
            scores = mm(query, wide_key[h], NT)
            slab = mm(position, keys[h * 64 : h * 64 + 64, pl.ds(from_n, width)])
            slab = pltpu.roll(slab, width - (ROWS - 1), 1, stride=1, stride_axis=0)
            scores = scores + slab[:, :1024]
            top = jnp.max(scores, axis=1, keepdims=True)
            expo = jnp.exp(scores - top)
            total = jnp.sum(expo, axis=1, keepdims=True)
            prob = (expo * (1.0 / total)).astype(jnp.bfloat16)
            probs[h, pl.ds(start, ROWS), :] = prob
            outs.append(mm(prob, qkv[:, 384 + h * 64 : 448 + h * 64]))
        attn_heads[pl.ds(start, ROWS), :] = jnp.concatenate(outs, axis=1).astype(jnp.bfloat16)
        send_rows(step, True)

    for acts in later:
        for name, off in acts:
            big_act(name, off)
    big_arrive()
    cot_wait()
    for zb in range(4):
        send_rows(zb, False)
    for yy, core in quad:
        for k in range(2):
            remote(
                attn.at[yy * 2 + core, k],
                attn.at[yy * 2 + core, k],
                trade_send.at[0],
                trade_recv.at[yy * 2 + core, k],
                partner,
            ).wait_recv()
    for k in range(2):
        rows[k] = x_seq[block_of(c, k, y)]
        attn_rows[k] = jnp.concatenate([attn[g, k] for g in range(4)], axis=1)
    big_leave()
    small_leave()
    for cond, copy in att_started:
        guarded(cond, copy.wait_send)
    for i, (yy, core) in enumerate(quad):
        piece(i, y, c, yy, core, device(x, core, z, yy)).wait_send()
    for m in range(2):
        away, out, _ = first_hop(m)
        pl.when(away)(out.wait_send)
        block_copy(0, block_of(c, m, y), partner).wait_send()
        block_copy(1, block_of(c, m, y), ny).wait_send()
        block_copy(2, block_of(c, m, 1 - y), partner).wait_send()


def forward_attention(arrays, collective_id):
    low = jnp.bfloat16
    dma = pltpu.SemaphoreType.DMA
    coarse, fine = angle_constants()
    shape = jax.ShapeDtypeStruct
    outs = [
        (shape((8, 128, D), low), VMEM_SPEC),
        (shape((2, 128, D), low), ANY_SPEC),
        (shape((2, 2, 4, 2, 24, D), low), VMEM_SPEC),
        (shape((32, 24, D), low), ANY_SPEC),
        (shape((32, 24, FF), low), ANY_SPEC),
        (shape((32, 96, D), low), ANY_SPEC),
        (shape((1024, 128), low), VMEM_SPEC),
        (shape((D, 2048), low), VMEM_SPEC),
        (shape((192, 2048), low), VMEM_SPEC),
        (shape((1024, 576), low), VMEM_SPEC),
        (shape((3, 1024, 1024), low), VMEM_SPEC),
        (shape((1024, 192), low), VMEM_SPEC),
        (shape((2, 128, D), low), VMEM_SPEC),
        (shape((2, 128, D), low), VMEM_SPEC),
        (shape((16, D), jnp.float32), VMEM_SPEC),
        (shape((1, FF), jnp.float32), VMEM_SPEC),
        (shape((8, 192), jnp.float32), VMEM_SPEC),
    ]
    return pl.pallas_call(
        forward_kernel,
        out_shape=[o[0] for o in outs],
        in_specs=[VMEM_SPEC] * 16,
        out_specs=[o[1] for o in outs],
        scratch_shapes=[
            pltpu.VMEM((4, 24, D), low),
            pltpu.VMEM((16, 128), low),
            pltpu.VMEM((32, 16, 128), low),
            pltpu.VMEM((4, 2, 128, 192), low),
            pltpu.VMEM((2, 1024), jnp.int32),
            pltpu.VMEM((2, 1024), jnp.int32),
            pltpu.VMEM((3, 1024, 128), low),
            dma((4, 8)),
            dma((5, 2)),
            dma((4,)),
            dma((3, 3)),
            dma((3, 4)),
            dma((3, 4)),
            dma((10, 1, 4)),
            dma((10, 1, 4)),
            dma((1,)),
            dma((10, 3, 4)),
            dma((10, 3, 4)),
            dma((3,)),
            dma((8,)),
            dma((4, 2)),
            dma((2,)),
        ],
        compiler_params=pltpu.CompilerParams(
            collective_id=collective_id, has_side_effects=True, vmem_limit_bytes=56 * 1024 * 1024
        ),
        name="forward_attention",
    )(*arrays, jnp.asarray(coarse), jnp.asarray(fine))


def farthest_first(z, step):
    side = z // 2
    near = side * (3 - z) + (1 - side) * z
    late = step // 2
    base = (1 - late) * (3 - step) + late * ((1 - near) * (3 - step) + near * (step - 2))
    return side * (3 - base) + (1 - side) * base


def scatter_plan(kinds, srcs, outs, buffers, send_sem, recv_sem, local_sem):
    n = len(kinds)
    acc, mate, from_x, from_y, corner, chain, last = (
        buffers[i * n : (i + 1) * n] for i in range(7)
    )
    x, c, z, y = place()
    nx, ny, partner = (device(1 - x, c, z, y), device(x, c, z, 1 - y), device(x, 1 - c, z, y))
    up, down = (
        device(x, c, jnp.minimum(z + 1, 3), y),
        device(x, c, jnp.maximum(z - 1, 0), y),
    )
    owners = ((x, y), (1 - x, y), (x, 1 - y), (1 - x, 1 - y))
    low = jnp.bfloat16

    def shard(a, core, owner, k):
        return srcs[a].at[(owner[0] * 2 + core) * 8 + k * 2 + owner[1]]

    def load(a, k, q):
        return pltpu.make_async_copy(shard(a, c, owners[q], k), acc[a].at[k, q], local_sem.at[a, k, q])

    def over(a, k, q, core):
        return remote(
            shard(a, core, owners[q], k),
            mate[a].at[k, q],
            send_sem.at[q, a, k],
            recv_sem.at[q, a, k],
            partner,
        )

    def hop(kind, a, k, q, target, to):
        return remote(acc[a].at[k, q], target, send_sem.at[kind, a, k], recv_sem.at[kind, a, k], to)

    t_half, t_x, t_y, t_z, t_last = range(4, 9)

    def half_to(a):
        return ny if kinds[a] == 1 else nx

    def begin():
        @pl.loop(0, 4)
        def _(step):
            k = farthest_first(z, step)
            for q in (3, 1, 2, 0):
                for a in range(n):
                    over(a, k, q, 1 - c).start()
                    load(a, k, q).start()

    def arrived(a, k, q):
        load(a, k, q).wait()
        over(a, k, q, c).wait_recv()

    def first(step):
        k = farthest_first(z, step)
        for a in range(n):
            arrived(a, k, 3)
            here = acc[a].at[k, 3]
            here[...] = (wide(here) + wide(mate[a].at[k, 3])).astype(low)
            hop(t_half, a, k, 3, corner[a].at[k], half_to(a)).start()

    def second(step):
        k = farthest_first(z, step)
        for q, half, kind, target, to in ((1, 1, t_x, from_x, nx), (2, 2, t_y, from_y, ny)):
            for a in range(n):
                arrived(a, k, q)
                here = acc[a].at[k, q]
                if kinds[a] == half:
                    hop(t_half, a, k, 3, corner[a].at[k], to).wait_recv()
                    here[...] = (
                        wide(here) + wide(mate[a].at[k, q]) + wide(corner[a].at[k])
                    ).astype(low)
                else:
                    here[...] = (wide(here) + wide(mate[a].at[k, q])).astype(low)
                hop(kind, a, k, q, target[a].at[k], to).start()

    def gathered(a, k):
        arrived(a, k, 0)
        hop(t_x, a, k, 1, from_x[a].at[k], nx).wait_recv()
        hop(t_y, a, k, 2, from_y[a].at[k], ny).wait_recv()
        return (
            wide(acc[a].at[k, 0])
            + wide(mate[a].at[k, 0])
            + (wide(from_x[a].at[k]) + wide(from_y[a].at[k]))
        )

    def third(step):
        k = farthest_first(z, step)
        inner = jnp.logical_or(jnp.logical_and(k < z, z < 3), jnp.logical_and(k > z, z > 0))
        for a in range(n):
            here = acc[a].at[k, 0]
            here[...] = gathered(a, k).astype(low)

            @pl.when(inner)
            def _(a=a, here=here):
                hop(t_z, a, k, 0, chain[a].at[k], up).wait_recv()
                here[...] = (wide(here) + wide(chain[a].at[k])).astype(low)

            pl.when(k > z + 1)(hop(t_z, a, k, 0, chain[a].at[k], up).start)
            pl.when(k < z - 1)(hop(t_z, a, k, 0, chain[a].at[k], down).start)
            pl.when(k == z + 1)(hop(t_z, a, k, 0, last[a].at[0], up).start)
            pl.when(k == z - 1)(hop(t_last, a, k, 0, last[a].at[1], down).start)

    def body(step):
        pl.when(step < 4)(lambda: first(step))
        pl.when(jnp.logical_and(step >= 1, step < 5))(lambda: second(step - 1))
        pl.when(step >= 2)(lambda: third(step - 2))

    def end():
        for a in range(n):
            outs[a][...] = gathered(a, z)

            @pl.when(z > 0)
            def _(a=a):
                hop(t_z, a, z, 0, last[a].at[0], up).wait_recv()
                outs[a][...] += wide(last[a].at[0])

            @pl.when(z < 3)
            def _(a=a):
                hop(t_last, a, z, 0, last[a].at[1], down).wait_recv()
                outs[a][...] += wide(last[a].at[1])

    def leave():
        @pl.loop(0, 4)
        def _(step):
            k = farthest_first(z, step)
            for a in range(n):
                for q in range(4):
                    over(a, k, q, 1 - c).wait_send()
                hop(t_half, a, k, 3, corner[a].at[k], half_to(a)).wait_send()
                hop(t_x, a, k, 1, from_x[a].at[k], nx).wait_send()
                hop(t_y, a, k, 2, from_y[a].at[k], ny).wait_send()
                pl.when(jnp.logical_or(k > z, k < z - 1))(
                    hop(t_z, a, k, 0, chain[a].at[k], up).wait_send
                )
                pl.when(k == z - 1)(hop(t_last, a, k, 0, last[a].at[1], down).wait_send)

    return (begin, body, end, leave)


def scatter_buffers(shards):
    out = []
    for lead in ((4, 4), (4, 4), (4,), (4,), (4,), (4,), (2,)):
        out += [pltpu.VMEM(lead + shape, jnp.bfloat16) for shape in shards]
    return out


def scatter_semaphores(n):
    dma = pltpu.SemaphoreType.DMA
    return [dma((9, n, 4)), dma((9, n, 4)), dma((n, 4, 4))]


BIG_SHARDS = ((24, D), (24, FF), (96, D))


def backward_kernel(
    grad_attn,
    grad_h1,
    result,
    g_small,
    g_out,
    g_up,
    g_down,
    qkv,
    sides,
    vec_small,
    table,
    keys,
    probs,
    attn_heads,
    x_seq,
    w_att,
    out_rows,
    out_grad,
    f_att,
    f_small,
    f_out,
    f_up,
    f_down,
    grad_heads,
    grad_qkv,
    wide_key,
    weights,
    grad_key,
    grad_value,
    grad_table,
    grad_vec,
    g_wide,
    g_att,
    att_x,
    att_z,
    att_last,
    att_q,
    dx_part,
    dx_in,
    dx_y,
    dx_out,
    dx_back,
    small_full,
    trade_send,
    trade_recv,
    trade_local,
    swap_sem,
    att_send,
    att_recv,
    quad_sem,
    dx_sem,
    *rest,
):
    small_buffers, rest = (rest[:7], rest[7:])
    small_sems, rest = (rest[:3], rest[3:])
    big_buffers, big_sems = (rest[:21], rest[21:])
    low = jnp.bfloat16
    x, c, z, y = place()
    group = y * 2 + c
    nx, ny, partner = (device(1 - x, c, z, y), device(x, c, z, 1 - y), device(x, 1 - c, z, y))
    cross = device(x, 1 - c, z, 1 - y)
    up, down = (
        device(x, c, jnp.minimum(z + 1, 3), y),
        device(x, c, jnp.maximum(z - 1, 0), y),
    )
    peers = [(None, nx), (None, ny), (None, partner), (None, cross), (z > 0, down), (z < 3, up)]
    greet(peers + swap_peers())
    quad = ((y, 1 - c), (1 - y, c), (1 - y, 1 - c))

    def trade_copy(i, k):
        yy, core = quad[i]
        b = (2 * c + k) * 2 + y
        return remote(
            grad_attn.at[yy * 2 + core, k],
            grad_heads.at[b],
            trade_send.at[i, k],
            trade_recv.at[b],
            device(x, core, z, yy),
        )

    def trade_here(k):
        b = (2 * c + k) * 2 + y
        return pltpu.make_async_copy(grad_attn.at[group, k], grad_heads.at[b], trade_local.at[k])

    for k in range(2):
        for i in (2, 1, 0):
            trade_copy(i, k).start()
        trade_here(k).start()
    big_begin, big_body, big_end, big_leave = scatter_plan(
        (2, 1, 2), [g_out, g_up, g_down], [f_out, f_up, f_down], big_buffers, *big_sems
    )
    small_begin, small_body, small_end, small_leave = scatter_plan(
        (1,), [small_full], [f_small], small_buffers, *small_sems
    )
    big_begin()
    result_start, result_wait = swap_copies(
        result, out_rows, swap_sem.at[0], swap_sem.at[1], swap_sem.at[2]
    )
    result_start()
    vec = vec_small[...]
    for h in range(3):
        key = qkv[:, 192 + h * 64 : 256 + h * 64]
        wide_key[h] = jnp.concatenate([key, sides[:, 64:128]], axis=1)
    weights[...] = wide(w_att).reshape(D, D).astype(low)
    grad_key[...] = jnp.zeros_like(grad_key)
    grad_value[...] = jnp.zeros_like(grad_value)
    grad_table[...] = jnp.zeros_like(grad_table)
    grad_vec[...] = jnp.zeros_like(grad_vec)
    for k in range(2):
        trade_here(k).wait()
        for yy, core in quad:
            b = (2 * core + k) * 2 + yy
            remote(
                grad_heads.at[b], grad_heads.at[b], trade_send.at[0, 0], trade_recv.at[b], partner
            ).wait_recv()

    width = 1024 + ROWS
    scale = DH ** (-0.5)

    @pl.loop(0, 4)
    def _(step):
        big_body(step)
        start = pl.multiple_of(step * ROWS, ROWS)
        block = qkv[pl.ds(start, ROWS), 0:192]
        side = sides[pl.ds(start, ROWS), 0:64].astype(jnp.float32)
        kind = side[:, 0:1]
        from_n = pl.multiple_of(1024 - ROWS - start, 128)
        grads = grad_heads[pl.ds(step * 2, 2)].reshape(ROWS, 192)
        outs = attn_heads[pl.ds(start, ROWS), :].astype(jnp.float32)
        grad_queries = []
        row = lax.broadcasted_iota(jnp.int32, (ROWS, ROWS), 0)
        column = lax.broadcasted_iota(jnp.int32, (ROWS, ROWS), 1)
        reverse = jnp.where(row + column == ROWS - 1, 1.0, 0.0).astype(low)
        for h in range(3):
            lanes = slice(h * 64, h * 64 + 64)
            content, position, typed, _, _ = query_parts(block[:, lanes], vec, h, kind)
            prob = probs[h, pl.ds(start, ROWS), :]
            grad = grads[:, lanes]
            delta = jnp.sum(outs[:, lanes] * grad.astype(jnp.float32), axis=1, keepdims=True)
            grad_probs = mm(grad, qkv[:, 384 + h * 64 : 448 + h * 64], NT)
            grad_value[h] += mm(prob, grad, TN)
            grad_scores = (prob.astype(jnp.float32) * (grad_probs - delta)).astype(low)
            grad_key[h] += mm(grad_scores, content.astype(low), TN)
            grad_wide = mm(grad_scores, wide_key[h])
            turned = mm(reverse, grad_scores)
            padded = jnp.concatenate([turned, jnp.zeros((ROWS, ROWS), jnp.float32)], axis=1)
            skew = pltpu.roll(padded, 0, 1, stride=1, stride_axis=0).astype(low)
            slab = keys[lanes, pl.ds(from_n, width)]
            turned = mm(skew, slab, NT) * scale
            high = turned.astype(low)
            low_part = (turned - high.astype(jnp.float32)).astype(low)
            grad_position = mm(reverse, high) + mm(reverse, low_part)
            position = mm(reverse, position).astype(low)
            grad_table[lanes, pl.ds(from_n, width)] += mm(position, skew, TN)
            grad_content = grad_wide[:, :64] * scale
            to_zero = grad_wide[:, 64:65] * scale
            to_one = grad_wide[:, 65:66] * scale
            same = jnp.where(kind > 0.5, to_one, to_zero)
            other = jnp.where(kind > 0.5, to_zero, to_one)
            grad_typed = other * vec[3:4, lanes] + same * vec[4:5, lanes]
            total = lambda value: jnp.sum(value, axis=0, keepdims=True)
            grad_vec[:, lanes] += jnp.concatenate(
                [
                    total(grad_content),
                    total(grad_position),
                    total(grad_typed),
                    total(other * typed),
                    total(same * typed),
                    jnp.zeros((3, 64), jnp.float32),
                ],
                axis=0,
            )
            grad_queries.append(grad_content + grad_position + grad_typed)
        grad_qkv[pl.ds(start, ROWS), 0:192] = jnp.concatenate(grad_queries, axis=1).astype(low)

    grad_qkv[:, 192:384] = jnp.concatenate([grad_key[h] for h in range(3)], axis=1).astype(low)
    grad_qkv[:, 384:576] = jnp.concatenate([grad_value[h] for h in range(3)], axis=1).astype(low)

    small_full[...] = g_small[...]
    line = lax.broadcasted_iota(jnp.int32, (16, 128), 0)
    for i in range(8):
        part = jnp.concatenate(
            [grad_vec[:, i * 24 : i * 24 + 24], jnp.zeros((8, 104), jnp.float32)], axis=1
        )
        part = jnp.concatenate([part, jnp.zeros((8, 128), jnp.float32)], axis=0)
        here = small_full.at[group * 8 + i]
        here[...] = jnp.where(line < 5, part, wide(here)).astype(low)
    small_begin()

    def dx_rows(core, k):
        start = pl.multiple_of((2 * core + k) * 256, 256)
        value = mm(grad_qkv[pl.ds(start, 256), :], weights[:, :576], NT)
        dx_part[pl.ds((2 * core + k) * 2, 2)] = value.astype(low).reshape(2, 128, D)

    def dx_over(core, k):
        part = dx_part.at[pl.ds((2 * core + k) * 2, 2)]
        return remote(part, dx_in.at[k], dx_sem.at[0, k], dx_sem.at[1, k], partner)

    for k in range(2):
        dx_rows(1 - c, k)
        dx_over(1 - c, k).start()

    g_wide[:, 0:576] = mm(x_seq[...].reshape(1024, D), grad_qkv[...], TN)
    g_wide[:, 576:768] = mm(table[...], grad_table[...].astype(low), NT)
    g_att[...] = g_wide[...].reshape(2, 2, 4, 2, 24, D).astype(low)

    def att_over(k):
        return remote(g_att.at[1 - x, :, k], att_x.at[k], att_send.at[0, k], att_recv.at[0, k], nx)

    for step in range(4):
        att_over(farthest_first(z, step)).start()
    small_body(0)
    for k in range(2):
        dx_rows(c, k)

    def dx_out_copy(k):
        return remote(dx_out.at[k], dx_y.at[k], dx_sem.at[2, k], dx_sem.at[3, k], ny)

    for k in range(2):
        dx_over(c, k).wait_recv()
        b = (2 * c + k) * 2 + 1 - y
        dx_out[k] = (wide(dx_part.at[b]) + wide(dx_in.at[k, 1 - y])).astype(low)
        dx_out_copy(k).start()
    big_body(4)
    small_body(1)

    def att_hop(kind, k, target, to):
        part = g_att.at[x, :, k]
        return remote(part, target, att_send.at[kind, k], att_recv.at[kind, k], to)

    for step in range(3):
        k = farthest_first(z, step)
        att_over(k).wait_recv()
        inner = jnp.logical_or(jnp.logical_and(k < z, z < 3), jnp.logical_and(k > z, z > 0))
        here = g_att.at[x, :, k]
        here[...] = (wide(here) + wide(att_x.at[k])).astype(low)

        @pl.when(inner)
        def _(here=here, k=k):
            att_hop(1, k, att_z.at[k], up).wait_recv()
            here[...] = (wide(here) + wide(att_z.at[k])).astype(low)

        pl.when(k > z + 1)(att_hop(1, k, att_z.at[k], up).start)
        pl.when(k < z - 1)(att_hop(1, k, att_z.at[k], down).start)
        pl.when(k == z + 1)(att_hop(1, k, att_last.at[0], up).start)
        pl.when(k == z - 1)(att_hop(2, k, att_last.at[1], down).start)
        small_body(step + 2)

    back_start, back_wait = swap_copies(
        dx_back.at[0], dx_back.at[1], swap_sem.at[3], swap_sem.at[4], swap_sem.at[5]
    )
    for k in range(2):
        dx_out_copy(k).wait_recv()
        b = (2 * c + k) * 2 + y
        value = wide(dx_part.at[b]) + wide(dx_in.at[k, y]) + wide(dx_y.at[k]) + grad_h1[k]
        dx_back[0, k] = value.astype(low)
    back_start()

    att_over(z).wait_recv()
    g_att[x, :, z] = (wide(g_att.at[x, :, z]) + wide(att_x.at[z])).astype(low)

    @pl.when(z > 0)
    def _():
        att_hop(1, z, att_last.at[0], up).wait_recv()
        g_att[x, :, z] = (wide(g_att.at[x, :, z]) + wide(att_last.at[0])).astype(low)

    @pl.when(z < 3)
    def _():
        att_hop(2, z, att_last.at[1], down).wait_recv()
        g_att[x, :, z] = (wide(g_att.at[x, :, z]) + wide(att_last.at[1])).astype(low)

    def quad_copy(i):
        yy, core = quad[i]
        return remote(
            g_att.at[x, core, z, yy],
            att_q.at[group],
            quad_sem.at[0, i],
            quad_sem.at[1, i],
            device(x, core, z, yy),
        )

    for i in range(3):
        quad_copy(i).start()
    small_end()
    big_end()
    f_att[group] = wide(g_att.at[x, c, z, y])
    for i, (yy, core) in enumerate(quad):
        other = yy * 2 + core
        remote(
            att_q.at[other], att_q.at[other], quad_sem.at[0, i], quad_sem.at[1, i], partner
        ).wait_recv()
        f_att[other] = wide(att_q.at[other])
    back_wait()
    out_grad[...] = wide(dx_back.at[1])
    result_wait()
    for k in range(2):
        for i in range(3):
            trade_copy(i, k).wait_send()
        dx_over(1 - c, k).wait_send()
        dx_out_copy(k).wait_send()
    for i in range(3):
        quad_copy(i).wait_send()
    for step in range(4):
        k = farthest_first(z, step)
        att_over(k).wait_send()
        pl.when(jnp.logical_or(k > z, k < z - 1))(att_hop(1, k, att_z.at[k], up).wait_send)
        pl.when(k == z - 1)(att_hop(2, k, att_last.at[1], down).wait_send)
    big_leave()
    small_leave()


def backward_attention(arrays, collective_id):
    low = jnp.bfloat16
    dma = pltpu.SemaphoreType.DMA
    shape = jax.ShapeDtypeStruct
    vmem = pltpu.VMEM
    in_specs = [VMEM_SPEC] * 4 + [ANY_SPEC] * 3 + [VMEM_SPEC] * 9
    outs = [
        (shape((2, 128, D), low), ANY_SPEC),
        (shape((2, 128, D), jnp.float32), VMEM_SPEC),
        (shape((4, 24, D), jnp.float32), VMEM_SPEC),
        (shape((16, 128), jnp.float32), VMEM_SPEC),
        (shape((24, D), jnp.float32), VMEM_SPEC),
        (shape((24, FF), jnp.float32), VMEM_SPEC),
        (shape((96, D), jnp.float32), VMEM_SPEC),
    ]
    return pl.pallas_call(
        backward_kernel,
        out_shape=[o[0] for o in outs],
        in_specs=in_specs,
        out_specs=[o[1] for o in outs],
        scratch_shapes=[
            vmem((8, 128, 192), low),
            vmem((1024, 576), low),
            vmem((3, 1024, 128), low),
            vmem((D, D), low),
            vmem((3, 1024, 64), jnp.float32),
            vmem((3, 1024, 64), jnp.float32),
            vmem((192, 2048), jnp.float32),
            vmem((8, 192), jnp.float32),
            vmem((D, D), jnp.float32),
            vmem((2, 2, 4, 2, 24, D), low),
            vmem((4, 2, 2, 24, D), low),
            vmem((4, 2, 2, 24, D), low),
            vmem((2, 2, 2, 24, D), low),
            vmem((4, 24, D), low),
            vmem((8, 128, D), low),
            vmem((2, 2, 128, D), low),
            vmem((2, 128, D), low),
            vmem((2, 128, D), low),
            vmem((2, 2, 128, D), low),
            vmem((32, 16, 128), low),
            dma((3, 2)),
            dma((8,)),
            dma((2,)),
            dma((6, 2)),
            dma((3, 4)),
            dma((3, 4)),
            dma((2, 3)),
            dma((4, 2)),
        ]
        + scatter_buffers(((16, 128),))
        + scatter_semaphores(1)
        + scatter_buffers(BIG_SHARDS)
        + scatter_semaphores(3),
        compiler_params=pltpu.CompilerParams(
            collective_id=collective_id, has_side_effects=True, vmem_limit_bytes=63 * 1024 * 1024
        ),
        name="backward_attention",
    )(*arrays)


HALF_PI_ROOT = 0.7978845608028654


def gelu_parts(v):
    inner = HALF_PI_ROOT * (v + 0.044715 * v * v * v)
    t = jnp.tanh(inner)
    value = 0.5 * v * (1.0 + t)
    slope = 0.5 * (1.0 + t) + 0.5 * v * (1.0 - t * t) * (
        HALF_PI_ROOT * (1.0 + 3.0 * 0.044715 * v * v)
    )
    return (value, slope)


BLOCK = 64


def dense_kernel(
    attn_rows,
    rows,
    cot,
    params,
    up_bias,
    w_out,
    w_up,
    w_down,
    result,
    grad_h1,
    grad_attn,
    g_small,
    g_out,
    g_up,
    g_down,
    v_out,
    v_up,
    v_down,
    s_out,
    s_up,
    s_down,
    slope,
    hidden,
    grad_pre,
    first_b,
    normed_one,
    inv_one,
    total,
    grad_first,
    grad_second,
    grad_branch,
    column_sums,
    up_sums,
    in_sem,
    out_sem,
):
    low = jnp.bfloat16
    loads = [
        pltpu.make_async_copy(src, dst, in_sem.at[i])
        for i, (src, dst) in enumerate(((w_out, v_out), (w_up, v_up), (w_down, v_down)))
    ]
    for copy in loads:
        copy.start()
    column_sums[...] = jnp.zeros_like(column_sums)
    attn = attn_rows[...].reshape(256, D)
    loads[0].wait()
    total[...] = mm(attn, v_out[...])

    def block_rows(step):
        start = pl.multiple_of(step * BLOCK, BLOCK)
        return (step // 2, pl.multiple_of((step % 2) * BLOCK, BLOCK), pl.ds(start, BLOCK))


    @pl.loop(0, 4)
    def _(step):
        half, inner, here = block_rows(step)
        h1 = rows[half, pl.ds(inner, BLOCK), :].astype(jnp.float32) + total[here, :]
        h1 = h1 + params[9:10, :]
        first, normed, inverse = layer_norm(h1, params[5:6, :], params[7:8, :])
        normed_one[here, :] = normed
        inv_one[here, :] = inverse
        first_b[here, :] = first.astype(low)
        total[here, :] = first + params[10:11, :]

    loads[1].wait()
    loads[2].wait()

    @pl.loop(0, 4)
    def _(j):
        lanes = pl.ds(pl.multiple_of(j * D, D), D)
        pre = mm(first_b[...], v_up[:, lanes]) + up_bias[:, lanes]
        value, derivative = gelu_parts(pre)
        hidden[j] = value.astype(low)
        slope[j] = derivative
        total[...] += mm(hidden[j], v_down[lanes, :])

    @pl.loop(0, 4)
    def _(step):
        half, inner, here = block_rows(step)
        out, normed, inverse = layer_norm(total[here, :], params[6:7, :], params[8:9, :])
        result[half, pl.ds(inner, BLOCK), :] = out.astype(low)
        grad = cot[half, pl.ds(inner, BLOCK), :].astype(jnp.float32)
        back = norm_back(grad, normed, inverse, params[6:7, :])
        grad_first[here, :] = back
        back = back.astype(low)
        grad_second[here, :] = back
        column_sums[1:2, :] += jnp.sum(grad * normed, axis=0, keepdims=True)
        column_sums[3:4, :] += jnp.sum(grad, axis=0, keepdims=True)
        column_sums[5:6, :] += jnp.sum(back.astype(jnp.float32), axis=0, keepdims=True)

    @pl.loop(0, 4)
    def _(j):
        lanes = pl.ds(pl.multiple_of(j * D, D), D)
        grad = (mm(grad_second[...], v_down[lanes, :], NT) * slope[j]).astype(low)
        grad_pre[j] = grad
        up_sums[:, lanes] = jnp.sum(grad.astype(jnp.float32), axis=0, keepdims=True)
        grad_first[...] += mm(grad, v_up[:, lanes], NT)

    @pl.loop(0, 4)
    def _(step):
        half, inner, here = block_rows(step)
        grad = grad_first[here, :]
        normed = normed_one[here, :]
        back = norm_back(grad, normed, inv_one[here, :], params[5:6, :])
        grad_h1[half, pl.ds(inner, BLOCK), :] = back
        back = back.astype(low)
        grad_branch[here, :] = back
        column_sums[0:1, :] += jnp.sum(grad * normed, axis=0, keepdims=True)
        column_sums[2:3, :] += jnp.sum(grad, axis=0, keepdims=True)
        column_sums[4:5, :] += jnp.sum(back.astype(jnp.float32), axis=0, keepdims=True)

    back = mm(grad_branch[...], v_out[...], NT).astype(low)
    for g in range(4):
        grad_attn[g] = back[:, g * 192 : g * 192 + 192].reshape(2, 128, 192)

    def store(i, src, dst):
        return pltpu.make_async_copy(src, dst, out_sem.at[i])

    @pl.loop(0, 4)
    def _(j):
        lanes = pl.ds(pl.multiple_of(j * D, D), D)
        s_down[lanes, :] = mm(hidden[j], grad_second[...], TN).astype(low)
        store(j, s_down.at[lanes], g_down.at[lanes]).start()

    @pl.loop(0, 4)
    def _(j):
        lanes = pl.ds(pl.multiple_of(j * D, D), D)
        s_up[:, lanes] = mm(first_b[...], grad_pre[j], TN).astype(low)
        store(4 + j, s_up.at[:, lanes], g_up.at[:, lanes]).start()

    s_out[...] = mm(attn, grad_branch[...], TN).astype(low)
    store(8, s_out, g_out).start()

    line = lax.broadcasted_iota(jnp.int32, (16, 128), 0)
    sums = jnp.concatenate(
        [jnp.zeros((5, D), jnp.float32), column_sums[...], jnp.zeros((3, D), jnp.float32)], axis=0
    )
    tall = up_sums[...]
    for i in range(32):
        part = jnp.concatenate(
            [sums[:, i * 24 : i * 24 + 24], jnp.zeros((16, 104), jnp.float32)], axis=1
        )
        long = jnp.concatenate(
            [tall[:, i * 96 : i * 96 + 96], jnp.zeros((1, 32), jnp.float32)], axis=1
        )
        g_small[i] = jnp.where(line == 11, jnp.broadcast_to(long, (16, 128)), part).astype(low)

    for j in range(4):
        lanes = pl.ds(j * D, D)
        store(j, s_down.at[lanes], g_down.at[lanes]).wait()
        store(4 + j, s_up.at[:, lanes], g_up.at[:, lanes]).wait()
    store(8, s_out, g_out).wait()


def dense_layers(arrays):
    low = jnp.bfloat16
    shape = jax.ShapeDtypeStruct
    vmem = pltpu.VMEM
    outs = [
        (shape((2, 128, D), low), VMEM_SPEC),
        (shape((2, 128, D), jnp.float32), VMEM_SPEC),
        (shape((4, 2, 128, 192), low), VMEM_SPEC),
        (shape((32, 16, 128), low), VMEM_SPEC),
        (shape((HD, D), low), ANY_SPEC),
        (shape((D, FF), low), ANY_SPEC),
        (shape((FF, D), low), ANY_SPEC),
    ]
    return pl.pallas_call(
        dense_kernel,
        out_shape=[o[0] for o in outs],
        in_specs=[VMEM_SPEC] * 5 + [ANY_SPEC] * 3,
        out_specs=[o[1] for o in outs],
        scratch_shapes=[
            vmem((HD, D), low),
            vmem((D, FF), low),
            vmem((FF, D), low),
            vmem((HD, D), low),
            vmem((D, FF), low),
            vmem((FF, D), low),
            vmem((4, 256, D), jnp.float32),
            vmem((4, 256, D), low),
            vmem((4, 256, D), low),
            vmem((256, D), low),
            vmem((256, D), jnp.float32),
            vmem((256, 1), jnp.float32),
            vmem((256, D), jnp.float32),
            vmem((256, D), jnp.float32),
            vmem((256, D), low),
            vmem((256, D), low),
            vmem((8, D), jnp.float32),
            vmem((1, FF), jnp.float32),
            pltpu.SemaphoreType.DMA((3,)),
            pltpu.SemaphoreType.DMA((9,)),
        ],
        compiler_params=pltpu.CompilerParams(vmem_limit_bytes=56 * 1024 * 1024),
        name="dense_layers",
    )(*arrays)


def final_kernel(
    out_rows, out_grad, f_att, f_small, f_out, f_up, f_down, *results
):
    rows, grad, g_in, g_out, g_pos, g_up, g_down, head, gains, shifts, biases, ffn_bias = results
    rows[...] = out_rows[...]
    grad[...] = out_grad[...]
    g_up[...] = f_up[...]
    g_down[...] = f_down[...]
    g_out[...] = f_out[...]
    g_in[...] = jnp.concatenate(
        [f_att[g][:, s * 192 : s * 192 + 192] for s in range(3) for g in range(4)], axis=1
    )
    g_pos[...] = jnp.concatenate([f_att[g][:, 576:768] for g in range(4)], axis=1)
    head[...] = f_small[0:5, 0:24]
    gains[...] = f_small[5:7, 0:24]
    shifts[...] = f_small[7:9, 0:24]
    biases[...] = f_small[9:11, 0:24]
    ffn_bias[...] = f_small[11:12, 0:96]


def final_shapes(arrays):
    high = jnp.float32
    shapes = [
        ((2, 128, D), jnp.bfloat16),
        ((2, 128, D), high),
        ((24, 3 * HD), high),
        ((24, D), high),
        ((24, HD), high),
        ((24, FF), high),
        ((96, D), high),
        ((5, 24), high),
        ((2, 24), high),
        ((2, 24), high),
        ((2, 24), high),
        ((1, 96), high),
    ]
    return pl.pallas_call(
        final_kernel,
        out_shape=[jax.ShapeDtypeStruct(*shape) for shape in shapes],
        in_specs=[VMEM_SPEC] * 7,
        out_specs=[VMEM_SPEC] * 12,
        name="final_shapes",
    )(*arrays)


def sequence_device(
    tokens,
    seg_ids,
    token_types,
    attn_in,
    attn_out,
    pos_kernel,
    ffn_in,
    ffn_out,
    head_vectors,
    norm_gains,
    norm_shifts,
    out_bias,
    ffn_bias,
    cotangent,
):
    (
        x_seq,
        cot,
        w_att,
        w_out,
        w_up,
        w_down,
        sides,
        table,
        keys,
        qkv,
        probs,
        attn_heads,
        rows,
        attn_rows,
        params,
        up_bias,
        vec,
    ) = forward_attention(
        [
            tokens,
            cotangent,
            seg_ids,
            token_types,
            attn_in,
            pos_kernel,
            head_vectors,
            norm_gains,
            norm_shifts,
            out_bias,
            ffn_bias.reshape(1, 96),
            attn_out,
            ffn_in,
            ffn_out,
        ],
        0,
    )
    result, grad_h1, grad_attn, g_small, g_out, g_up, g_down = dense_layers(
        [
            attn_rows,
            rows,
            cot,
            params,
            up_bias,
            w_out.reshape(HD, D),
            w_up.reshape(D, FF),
            w_down.reshape(FF, D),
        ]
    )
    sums = backward_attention(
        [
            grad_attn,
            grad_h1,
            result,
            g_small,
            g_out.reshape(32, 24, D),
            g_up.reshape(32, 24, FF),
            g_down.reshape(32, 96, D),
            qkv,
            sides,
            vec,
            table,
            keys,
            probs,
            attn_heads,
            x_seq,
            w_att,
        ],
        1,
    )
    outs = final_shapes(sums)
    return tuple(outs[:11]) + (outs[11].reshape(96),)


def solution(mesh):
    placed = (
        P("dp", "fsdp", None),
        P("dp", None),
        P("dp", None),
        P(("dp", "fsdp"), None),
        P(("dp", "fsdp"), None),
        P(("dp", "fsdp"), None),
        P(("dp", "fsdp"), None),
        P(("dp", "fsdp"), None),
        P(None, ("dp", "fsdp")),
        P(None, ("dp", "fsdp")),
        P(None, ("dp", "fsdp")),
        P(None, ("dp", "fsdp")),
        P(("dp", "fsdp")),
        P("dp", "fsdp", None),
    )
    two_by_four = tuple(mesh.shape[name] for name in ("dp", "fsdp")) == (4, 8)
    return jax.shard_map(
        sequence_device if two_by_four else per_device,
        mesh=mesh,
        in_specs=placed,
        out_specs=(
            P("dp", "fsdp", None),
            P("dp", "fsdp", None),
            P(("dp", "fsdp"), None),
            P(("dp", "fsdp"), None),
            P(("dp", "fsdp"), None),
            P(("dp", "fsdp"), None),
            P(("dp", "fsdp"), None),
            P(None, ("dp", "fsdp")),
            P(None, ("dp", "fsdp")),
            P(None, ("dp", "fsdp")),
            P(None, ("dp", "fsdp")),
            P(("dp", "fsdp")),
        ),
        check_vma=False,
    )
```
